256 devices in a mesh: tm: 256 (over x, z, y, core).
Axes of the slice: x: 4, y: 4, z: 8, core: 2. Of those that a mesh axis runs over, the one named last changes fastest.
Arguments:
- measurements: float32 [256, 128], P('tm'), may hold values from -6 to 6
- noise_levels: float32 [256, 128], P('tm'), may hold values from 0.05 to 2
- transition: float32 [256, 256], replicated, may hold values from -0.5 to 1.5
- sensing: float32 [128, 256], replicated, may hold values from -0.75 to 0.75
- process_noise: float32 [256, 256], replicated, may hold values from -0.2 to 0.6, as said below
- prior_mean: float32 [256], replicated, may hold values from -5 to 5
- prior_covariance: float32 [256, 256], replicated, may hold values from -0.6 to 2.5, as said below
Outputs:
- smoothed_means: float32 [256, 256], P('tm')
- smoothed_covariances: float32 [256, 256, 256], P('tm')
The draws below stay inside these ranges and needn't reach their ends.
Inputs may be any that keep to these rules, and one draw needn't show every extreme that they name: `process_noise`: symmetric positive definite. `prior_covariance`: symmetric positive definite.
All inputs are finite; a program needn't handle non-finite values.
Results may differ from the reference program's by a relative error of at most 0.0003.
Values sent between devices are 32-bit elements; how exact they have to be, the bound alone decides.
A program may use at most 128 MiB of HBM per device.

```python
import math
import jax
import jax.numpy as jnp
from jax import lax

NS = 256
NO = 128
TIME = 256


def slow_modes(key):
    picks = jax.random.randint(jax.random.fold_in(key, 5), (NS,), 0, 2)
    return picks.astype(jnp.float32)


def definite_matrix(key, scale, floor_low, floor_high):
    first_key, second_key = jax.random.split(key)
    basis = jax.random.truncated_normal(first_key, -4.0, 4.0, (NS, NS), jnp.float32)
    diagonal = jax.random.uniform(second_key, (NS,), jnp.float32, floor_low, floor_high)
    product = jnp.dot(basis, basis.T, precision=lax.Precision.HIGHEST)
    return scale * product / NS + jnp.diag(diagonal)


def draw_transition(key, part):
    slow = slow_modes(key)
    first_key, second_key, third_key = jax.random.split(jax.random.fold_in(key, 7), 3)
    slow_rate = jax.random.uniform(first_key, (NS,), jnp.float32, 0.995, 0.9995)
    fast_rate = jax.random.uniform(second_key, (NS,), jnp.float32, 0.3, 0.6)
    coupling = jax.random.truncated_normal(third_key, -4.0, 4.0, (NS, NS), jnp.float32)
    rates = slow * slow_rate + (1.0 - slow) * fast_rate
    fast_rows = (1.0 - slow)[:, None]
    return jnp.diag(rates) + fast_rows * (0.2 * coupling / jnp.sqrt(jnp.float32(NS)))


def draw_sensing(key, part):
    slow = slow_modes(key)
    values = jax.random.truncated_normal(jax.random.fold_in(key, 13), -4.0, 4.0, (NO, NS), jnp.float32)
    column_scale = slow * 0.05 + (1.0 - slow)
    return values * column_scale[None, :] / jnp.sqrt(jnp.float32(NS))


def draw_process_noise(key, part):
    slow = slow_modes(key)
    mode_scale = slow * 0.1 + (1.0 - slow)
    base = definite_matrix(jax.random.fold_in(key, 11), 0.1, 0.02, 0.2)
    return mode_scale[:, None] * base * mode_scale[None, :]


def draw_prior_covariance(key, part):
    return definite_matrix(jax.random.fold_in(key, 23), 0.5, 0.2, 1.0)


def block_levels(rng, shape, cuts, least, top_value):
    def one(position, shards_of):
        steps = jax.random.uniform(jax.random.fold_in(jax.random.fold_in(rng, 6), position), (shards_of,), jnp.float32, least / len(cuts), top_value / len(cuts))
        return jnp.repeat(jnp.exp(steps), shape[position] // shards_of).reshape((-1,) + (1,) * (len(shape) - position - 1))

    gain = one(*cuts[0])
    for cut in cuts[1:]:
        gain = gain * one(*cut)
    return gain


def bell_draw(stream_key, dims, scale, reach, cuts=(), kind=jnp.bfloat16):
    array = scale * jax.random.normal(stream_key, dims, jnp.float32)
    if cuts:
        array = array * block_levels(stream_key, dims, cuts, -0.22, 0.18)
    return jnp.clip(array, -reach, reach).astype(kind)


def setup_inputs(seed: int = 0) -> dict:
    seeds = jax.random.split(jax.random.key(seed), 8)
    measurements = bell_draw(seeds[0], (TIME, NO), 1.0, 6.0, ((0, 256),), jnp.float32)
    noise_levels = jnp.clip(jnp.exp(math.log(2.0) - 3.6888794 * jax.random.uniform(seeds[1], (TIME, NO), jnp.float32) ** block_levels(seeds[1], (TIME, NO), ((0, 256),), -0.2, 0.2)), 0.05, 2.0)
    transition = draw_transition(jax.random.fold_in(seeds[7], 71), 0)
    sensing = draw_sensing(jax.random.fold_in(seeds[7], 71), 0)
    process_noise = draw_process_noise(jax.random.fold_in(seeds[7], 71), 0)
    prior_mean = bell_draw(seeds[5], (NS,), 1.0, 5.0, (), jnp.float32)
    prior_covariance = draw_prior_covariance(jax.random.fold_in(seeds[7], 71), 0)
    return dict(measurements=measurements, noise_levels=noise_levels, transition=transition, sensing=sensing, process_noise=process_noise, prior_mean=prior_mean, prior_covariance=prior_covariance)


def dense(left, right):
    return jnp.dot(left, right, precision=lax.Precision.HIGHEST)

def lower_solve(factor, values):
    return jax.scipy.linalg.solve_triangular(factor, values, lower=True)

def build_element(measure, levels, sensed, transition, sensing, start_noise, start_center, active):
    state_width = transition.shape[0]
    gain_rows = dense(sensing, start_noise)
    innovation = dense(gain_rows, sensing.T) + jnp.diag(levels)
    factor = jnp.linalg.cholesky(innovation)
    scaled = lower_solve(factor, jnp.concatenate([gain_rows, sensed], axis=1))
    white_gain = scaled[:, :state_width]
    white_sensed = scaled[:, state_width:]
    white_error = lower_solve(factor, measure - dense(sensing, start_center))
    white_measure = lower_solve(factor, measure)
    evolve = active * (transition - dense(white_gain.T, white_sensed))
    offset = start_center + dense(white_gain.T, white_error)
    spread = start_noise - dense(white_gain.T, white_gain)
    info_vector = active * dense(white_sensed.T, white_measure)
    info_matrix = active * dense(white_sensed.T, white_sensed)
    return (evolve, offset, spread, info_vector, info_matrix)

def factors(early_spread, vacancy, late_evolve, late_matrix):
    identity = jnp.eye(early_spread.shape[0], dtype=jnp.float32)
    root_factor = jnp.linalg.cholesky(early_spread + vacancy * identity) * (1.0 - vacancy)
    root_info = dense(root_factor.T, late_matrix)
    inner_factor = jnp.linalg.cholesky(identity + dense(root_info, root_factor))
    carried = lower_solve(inner_factor, dense(root_factor.T, late_evolve.T))
    mixing = lower_solve(inner_factor, root_info)
    return (root_factor, inner_factor, carried, mixing)

def absorb(center, spread, vacancy, element):
    late_evolve, late_offset, late_spread, late_vector, late_matrix = element[:5]
    root_factor, inner_factor, carried, mixing = factors(spread, vacancy, late_evolve, late_matrix)
    through = late_evolve - dense(carried.T, mixing)
    new_center = dense(through, center + dense(spread, late_vector)) + late_offset
    new_spread = dense(carried.T, carried) + late_spread
    return (new_center, new_spread)

def smooth_element(center, spread, transition, process_noise, active):
    forward_map = dense(transition, spread)
    predicted = dense(forward_map, transition.T) + process_noise
    factor = jnp.linalg.cholesky(predicted)
    solved = lower_solve(factor, forward_map)
    back_gain = active * jax.scipy.linalg.solve_triangular(factor, solved, lower=True, trans=1).T
    lift = center - dense(back_gain, dense(transition, center))
    leftover = spread - active * dense(solved.T, solved)
    return (back_gain, lift, leftover)

def reference(measurements, noise_levels, transition, sensing, process_noise, prior_mean, prior_covariance):
    sensed = dense(sensing, transition)
    start_noise = dense(dense(transition, prior_covariance), transition.T) + process_noise
    start_center = dense(transition, prior_mean)
    first_element = build_element(measurements[0], noise_levels[0], sensed, transition, sensing, start_noise, start_center, 0.0)
    zero_center = jnp.zeros_like(prior_mean)
    no_vacancy = jnp.zeros((), jnp.float32)

    def forward(carry, inputs):
        center, spread = carry
        element = build_element(inputs[0], inputs[1], sensed, transition, sensing, process_noise, zero_center, 1.0)
        center, spread = absorb(center, spread, no_vacancy, element)
        return ((center, spread), (center, spread))
    start_state = (first_element[1], first_element[2])
    final_state, filtered_rest = lax.scan(forward, start_state, (measurements[1:], noise_levels[1:]))
    centers = jnp.concatenate([first_element[1][None], filtered_rest[0]], axis=0)
    spreads = jnp.concatenate([first_element[2][None], filtered_rest[1]], axis=0)

    def backward(carry, inputs):
        smooth_center, smooth_spread = carry
        back_gain, lift, leftover = smooth_element(inputs[0], inputs[1], transition, process_noise, 1.0)
        smooth_center = dense(back_gain, smooth_center) + lift
        smooth_spread = dense(dense(back_gain, smooth_spread), back_gain.T) + leftover
        return ((smooth_center, smooth_spread), (smooth_center, smooth_spread))
    last_state = (centers[-1], spreads[-1])
    first_state, smoothed_rest = lax.scan(backward, last_state, (centers[:-1], spreads[:-1]), reverse=True)
    smoothed_means = jnp.concatenate([smoothed_rest[0], centers[-1][None]], axis=0)
    smoothed_covariances = jnp.concatenate([smoothed_rest[1], spreads[-1][None]], axis=0)
    return (smoothed_means, smoothed_covariances)
```

```python
import jax
import jax.numpy as jnp
from jax import lax
from jax.experimental import pallas as pl
from jax.experimental.pallas import tpu as pltpu
from jax.sharding import PartitionSpec as P

F32 = jnp.float32
BF16 = jnp.bfloat16
NN = (((1,), (0,)), ((), ()))
NT = (((1,), (1,)), ((), ()))


def exact(left, right, dims=NN):
    return lax.dot_general(
        left, right, dims, precision=lax.Precision.HIGHEST, preferred_element_type=F32
    )


def rough(left, right, dims=NN):
    return lax.dot_general(
        left.astype(BF16), right.astype(BF16), dims, preferred_element_type=F32
    )


def unit(size):
    rows = lax.broadcasted_iota(jnp.int32, (size, size), 0)
    columns = lax.broadcasted_iota(jnp.int32, (size, size), 1)
    return (rows == columns).astype(F32)


def inverse(product, bound, pair):
    size = product.shape[0]
    eye = unit(size)
    whole = eye + product

    def descend(times, limit):
        low = 1.0 / bound
        scaled = whole * low
        gain = 4.0 / ((1.0 + low) * (1.0 + low))
        step = gain * ((1.0 + low) * eye - scaled)
        pair[:size, :] = step * low
        pair[size:, :] = times(scaled, step)

        def more(low):
            return low < limit

        def turn(low):
            gain = 4.0 / ((1.0 + low) * (1.0 + low))
            step = gain * ((1.0 + low) * eye - pair[size:, :])
            pair[...] = times(pair[...], step)
            return low * gain

        lax.while_loop(more, turn, low * gain)
        return times(pair[:size, :], 2.0 * eye - pair[size:, :])

    small = bound < 128.0

    @pl.when(small)
    def _():
        pair[:size, :] = descend(rough, 0.95)

    @pl.when(jnp.logical_not(small))
    def _():
        pair[:size, :] = descend(exact, 0.999)

    guess = pair[:size, :]
    for times in (rough, exact):
        guess = guess + rough(guess, eye - exact(whole, guess))
    return guess


def spectral_bound(product, mirrored):
    return 1.0 + 1.001 * jnp.sqrt(jnp.maximum(jnp.sum(product * mirrored), 0.0))


def leaf_kernel(first_ref, y_ref, r_ref, f_ref, h_ref, q_ref, m_ref, p_ref, out_ref, noise, center, pair):
    first = first_ref[0] == 0
    no = h_ref.shape[0]
    ns = h_ref.shape[1]
    move = f_ref[...]
    noise[...] = q_ref[...]
    center[...] = jnp.zeros_like(center)

    @pl.when(first)
    def _():
        noise[...] += exact(exact(move, p_ref[...]), move, NT)
        center[...] = exact(jnp.broadcast_to(m_ref[...], center.shape), move, NT)

    active = jnp.where(first, 0.0, 1.0)
    eye = unit(no)
    weight = lax.rsqrt(r_ref[...])
    weights = jnp.sum(eye * weight, axis=1, keepdims=True)
    sense = h_ref[...] * weights
    y = jnp.broadcast_to(y_ref[...] * weight, (8, no))
    base = noise[...]
    gain = exact(sense, base)
    sensed = exact(sense, move)
    inner = exact(gain, sense, NT)
    mixed = inverse(inner, spectral_bound(inner, inner), pair)
    gained = exact(mixed, gain)
    joined = exact(mixed, sensed)
    gain_t = gain.T
    out_ref[:ns, :] = active * (move - exact(gain_t, joined))
    out_ref[ns : 2 * ns, :] = base - exact(gain_t, gained)
    out_ref[2 * ns : 3 * ns, :] = active * exact(sensed.T, joined)
    error = y - exact(center[...], sense, NT)
    out_ref[3 * ns : 3 * ns + 8, :] = center[...] + exact(error, gained)
    out_ref[3 * ns + 8 : 3 * ns + 16, :] = active * exact(y, joined)


def parts(ref):
    ns = ref.shape[1]
    return (
        ref[:ns, :],
        ref[ns : 2 * ns, :],
        ref[2 * ns : 3 * ns, :],
        ref[3 * ns : 3 * ns + 8, :],
        ref[3 * ns + 8 : 3 * ns + 16, :],
    )


def ahead_kernel(e_ref, l_ref, out_ref, pair):
    ns = e_ref.shape[1]
    move, spread, bind, offset, pull = parts(e_ref)
    late = l_ref[:ns, :]
    product = exact(spread, late)
    mixed = inverse(product, spectral_bound(product, exact(late, spread)), pair)
    out_ref[:ns, :] = exact(move.T, exact(exact(late, mixed), move)) + bind
    residue = l_ref[ns:, :] - exact(offset, late)
    out_ref[ns:, :] = exact(exact(residue, mixed), move) + pull


def join_kernel(i_ref, j_ref, out_ref, pair):
    ns = i_ref.shape[1]
    move_i, spread_i, bind_i, offset_i, pull_i = parts(i_ref)
    move_j, spread_j, bind_j, offset_j, pull_j = parts(j_ref)
    product = exact(spread_i, bind_j)
    mixed = inverse(product, spectral_bound(product, exact(bind_j, spread_i)), pair)
    through = exact(move_j, mixed)
    out_ref[:ns, :] = exact(through, move_i)
    out_ref[ns : 2 * ns, :] = exact(exact(through, spread_i), move_j, NT) + spread_j
    out_ref[2 * ns : 3 * ns, :] = exact(move_i.T, exact(exact(bind_j, mixed), move_i)) + bind_i
    out_ref[3 * ns : 3 * ns + 8, :] = (
        exact(offset_i + exact(pull_j, spread_i), through, NT) + offset_j
    )
    residue = pull_j - exact(offset_i, bind_j)
    out_ref[3 * ns + 8 : 3 * ns + 16, :] = exact(exact(residue, mixed), move_i) + pull_i


def last_kernel(i_ref, j_ref, l_ref, mean_ref, cov_ref, spread, pair):
    ns = j_ref.shape[1]
    spread_i = i_ref[:ns, :]
    offset_i = i_ref[ns : ns + 8, :]
    move_j, spread_j, bind_j, offset_j, pull_j = parts(j_ref)
    product = exact(spread_i, bind_j)
    mixed = inverse(product, spectral_bound(product, exact(bind_j, spread_i)), pair)
    through = exact(move_j, mixed)
    spread[...] = exact(exact(through, spread_i), move_j, NT) + spread_j
    offset = exact(offset_i + exact(pull_j, spread_i), through, NT) + offset_j
    late = l_ref[:ns, :]
    whole = spread[...]
    product = exact(whole, late)
    mixed = inverse(product, spectral_bound(product, exact(late, whole)), pair)
    cov_ref[...] = exact(mixed, whole)
    mean_ref[...] = exact(offset + exact(l_ref[ns:, :], whole), mixed, NT)


VMEM = pl.BlockSpec(memory_space=pltpu.VMEM)
SMEM = pl.BlockSpec(memory_space=pltpu.SMEM)


def call(kernel, args, outs, scratch, flops, name):
    read = sum(a.size for a in args) * 4
    return pl.pallas_call(
        kernel,
        out_shape=outs,
        in_specs=[SMEM if a.ndim == 1 else VMEM for a in args],
        out_specs=jax.tree.map(lambda _: VMEM, outs),
        scratch_shapes=scratch,
        cost_estimate=pl.CostEstimate(flops=flops, bytes_accessed=read, transcendentals=0),
        name=name,
    )(*args)


def shards(measurements, noise_levels, transition, sensing, process_noise, prior_mean, prior_covariance):
    ns = transition.shape[0]
    no = sensing.shape[0]
    count = lax.axis_size("tm")
    device = lax.axis_index("tm")
    pair = pltpu.VMEM((2 * ns, ns), F32)
    whole = jax.ShapeDtypeStruct((3 * ns + 16, ns), F32)
    half = jax.ShapeDtypeStruct((ns + 8, ns), F32)
    work = 2 * ns**3 * 60
    element = call(
        leaf_kernel,
        (
            device.astype(jnp.int32).reshape(1),
            measurements,
            noise_levels,
            transition,
            sensing,
            process_noise,
            prior_mean.reshape(1, ns),
            prior_covariance,
        ),
        whole,
        [pltpu.VMEM((ns, ns), F32), pltpu.VMEM((8, ns), F32), pltpu.VMEM((2 * no, no), F32)],
        work,
        "leaf",
    )
    later = jnp.zeros((ns + 8, ns), F32)
    distance = 1
    while distance < count:
        up = [(i, i + distance) for i in range(count - distance)]
        down = [(i + distance, i) for i in range(count - distance)]
        last = distance * 2 >= count
        if last:
            sent = jnp.concatenate([element[ns : 2 * ns], element[3 * ns : 3 * ns + 8]], axis=0)
        else:
            sent = element
        arrived = lax.ppermute(sent, "tm", up)
        if distance == 1:
            ahead = jnp.concatenate([element[2 * ns : 3 * ns], element[3 * ns + 8 :]], axis=0)
        else:
            ahead = call(ahead_kernel, (element, later), half, [pair], work, "ahead")
        behind = lax.ppermute(ahead, "tm", down)
        if not last:
            element = call(join_kernel, (arrived, element), whole, [pair], work, "join")
        later = jnp.where(device + distance < count, behind, later)
        distance *= 2
    mean, cov = call(
        last_kernel,
        (arrived, element, later),
        (jax.ShapeDtypeStruct((8, ns), F32), jax.ShapeDtypeStruct((ns, ns), F32)),
        [pltpu.VMEM((ns, ns), F32), pair],
        work,
        "last",
    )
    return (mean[:1], cov[None])


def solution(mesh):
    return jax.shard_map(
        shards,
        mesh=mesh,
        in_specs=(P("tm", None), P("tm", None), P(), P(), P(), P(), P()),
        out_specs=(P("tm", None), P("tm", None, None)),
        check_vma=False,
    )
```

```python
import jax
import jax.numpy as jnp
from jax import lax
from jax.experimental import pallas as pl
from jax.experimental.pallas import tpu as pltpu
from jax.sharding import PartitionSpec as P

F32 = jnp.float32
BF16 = jnp.bfloat16
NN = (((1,), (0,)), ((), ()))
NT = (((1,), (1,)), ((), ()))


def exact(left, right, dims=NN):
    return lax.dot_general(
        left, right, dims, precision=lax.Precision.HIGHEST, preferred_element_type=F32
    )


def rough(left, right, dims=NN):
    return lax.dot_general(
        left.astype(BF16), right.astype(BF16), dims, preferred_element_type=F32
    )


def unit(size):
    rows = lax.broadcasted_iota(jnp.int32, (size, size), 0)
    columns = lax.broadcasted_iota(jnp.int32, (size, size), 1)
    return (rows == columns).astype(F32)


def inverse(product, bound, pair):
    size = product.shape[0]
    eye = unit(size)
    whole = eye + product

    def descend(times, limit):
        low = 1.0 / bound
        scaled = whole * low
        gain = 4.0 / ((1.0 + low) * (1.0 + low))
        step = gain * ((1.0 + low) * eye - scaled)
        pair[:size, :] = step * low
        pair[size:, :] = times(scaled, step)

        def more(low):
            return low < limit

        def turn(low):
            gain = 4.0 / ((1.0 + low) * (1.0 + low))
            step = gain * ((1.0 + low) * eye - pair[size:, :])
            pair[...] = times(pair[...], step)
            return low * gain

        lax.while_loop(more, turn, low * gain)
        return times(pair[:size, :], 2.0 * eye - pair[size:, :])

    small = bound < 128.0

    @pl.when(small)
    def _():
        pair[:size, :] = descend(rough, 0.95)

    @pl.when(jnp.logical_not(small))
    def _():
        pair[:size, :] = descend(exact, 0.999)

    guess = pair[:size, :]
    for times in (rough, exact):
        guess = guess + rough(guess, eye - exact(whole, guess))
    return guess


def spectral_bound(product, mirrored):
    return 1.0 + 1.001 * jnp.sqrt(jnp.maximum(jnp.sum(product * mirrored), 0.0))


def pack(out, value, vector):
    ns = value.shape[0]
    n = ns // 2
    rows = lax.broadcasted_iota(jnp.int32, (n, n), 0)
    columns = lax.broadcasted_iota(jnp.int32, (n, n), 1)
    low, high = value[:n, :n], value[n:, n:]
    out[:n, :n] = value[n:, :n]
    out[:n, n:] = jnp.where(rows >= columns, low, high)
    out[n : n + 8, :] = jnp.zeros((8, ns), F32)
    out[n : n + 1, :] = vector[:1, :]
    out[n + 1 : n + 2, :n] = jnp.sum(
        jnp.where(rows == columns, high, 0.0), axis=0, keepdims=True
    )


def unpack(ref):
    ns = ref.shape[1]
    n = ns // 2
    rows = lax.broadcasted_iota(jnp.int32, (n, n), 0)
    columns = lax.broadcasted_iota(jnp.int32, (n, n), 1)
    corner = ref[:n, :n]
    mixed = ref[:n, n:]
    turned = mixed.T
    diagonal = jnp.broadcast_to(ref[n + 1 : n + 2, :n], (n, n))
    low = jnp.where(rows >= columns, mixed, turned)
    high = jnp.where(rows < columns, mixed, jnp.where(rows == columns, diagonal, turned))
    value = jnp.concatenate(
        [
            jnp.concatenate([low, corner.T], axis=1),
            jnp.concatenate([corner, high], axis=1),
        ],
        axis=0,
    )
    return value, spread_rows(ref, n)


def spread_rows(ref, at):
    return jnp.broadcast_to(ref[at : at + 1, :], (8, ref.shape[1]))


def leaf_kernel(
    first_ref, y_ref, r_ref, f_ref, h_ref, q_ref, m_ref, p_ref,
    spread_msg, move_msg, bind_msg, spread_ref, bind_ref, noise, center, pair,
):
    first = first_ref[0] == 0
    no = h_ref.shape[0]
    ns = h_ref.shape[1]
    move = f_ref[...]
    noise[...] = q_ref[...]
    center[...] = jnp.zeros_like(center)

    @pl.when(first)
    def _():
        noise[...] += exact(exact(move, p_ref[...]), move, NT)
        center[...] = exact(jnp.broadcast_to(m_ref[...], center.shape), move, NT)

    active = jnp.where(first, 0.0, 1.0)
    eye = unit(no)
    weight = lax.rsqrt(r_ref[...])
    weights = jnp.sum(eye * weight, axis=1, keepdims=True)
    sense = h_ref[...] * weights
    y = jnp.broadcast_to(y_ref[...] * weight, (8, no))
    base = noise[...]
    gain = exact(sense, base)
    sensed = exact(sense, move)
    inner = exact(gain, sense, NT)
    mixed = inverse(inner, spectral_bound(inner, inner), pair)
    gained = exact(mixed, gain)
    joined = exact(mixed, sensed)
    gain_t = gain.T
    spread_ref[...] = base - exact(gain_t, gained)
    bind_ref[...] = active * exact(sensed.T, joined)
    error = y - exact(center[...], sense, NT)
    pack(spread_msg, spread_ref[...], center[...] + exact(error, gained))
    pull = active * exact(y, joined)
    move_msg[:ns, :] = active * (move - exact(gain_t, joined))
    pack(move_msg.at[ns:, :], bind_ref[...], pull)
    pack(bind_msg, bind_ref[...], pull)


def resolve(spread_i, bind_j, pair):
    product = exact(spread_i, bind_j)
    return inverse(product, spectral_bound(product, exact(bind_j, spread_i)), pair)


def ahead_kernel(
    keep_ref, spread_msg, move_msg, spread_ref, bind_ref, old_ref, behind_msg,
    out_msg, later_ref, pair,
):
    ns = spread_ref.shape[0]
    take_later(keep_ref, old_ref, behind_msg, later_ref)
    move = move_msg[:ns, :]
    late = later_ref[:ns, :]
    mixed = resolve(spread_ref[...], late, pair)
    offset = spread_rows(spread_msg, ns // 2)
    pull = spread_rows(move_msg, ns + ns // 2)
    residue = later_ref[ns:, :] - exact(offset, late)
    bind = exact(move.T, exact(exact(late, mixed), move)) + bind_ref[...]
    pack(out_msg, bind, exact(exact(residue, mixed), move) + pull)


def take_later(keep_ref, old_ref, behind_msg, later_ref):
    ns = later_ref.shape[1]
    keep = keep_ref[0] > 0

    @pl.when(keep)
    def _():
        later_ref[...] = old_ref[...]

    @pl.when(jnp.logical_not(keep))
    def _():
        value, vector = unpack(behind_msg)
        later_ref[:ns, :] = value
        later_ref[ns:, :] = vector


def spread_kernel(arrived_msg, spread_msg, move_msg, spread_ref, bind_ref, out_msg, out_ref, middle, pair):
    ns = spread_ref.shape[0]
    spread_i, offset_i = unpack(arrived_msg)
    move, bind = move_msg[:ns, :], bind_ref[...]
    mixed = resolve(spread_i, bind, pair)
    through = exact(move, mixed)
    pull = spread_rows(move_msg, ns + ns // 2)
    offset = spread_rows(spread_msg, ns // 2)
    out_ref[...] = exact(exact(through, spread_i), move, NT) + spread_ref[...]
    pack(out_msg, out_ref[...], exact(offset_i + exact(pull, spread_i), through, NT) + offset)
    middle[:ns, :] = through
    middle[ns : 2 * ns, :] = exact(bind, mixed)
    middle[2 * ns :, :] = exact(pull - exact(offset_i, bind), mixed)


def move_kernel(arrived_msg, middle, out_msg, bind_out):
    ns = bind_out.shape[0]
    move_i = arrived_msg[:ns, :]
    bind_i, pull_i = unpack(arrived_msg.at[ns:, :])
    out_msg[:ns, :] = exact(middle[:ns, :], move_i)
    bind_out[...] = exact(move_i.T, exact(middle[ns : 2 * ns, :], move_i)) + bind_i
    pack(out_msg.at[ns:, :], bind_out[...], exact(middle[2 * ns :, :], move_i) + pull_i)


def last_kernel(keep_ref, spread_msg, spread_ref, old_ref, behind_msg, mean_ref, cov_ref, later_ref, pair):
    ns = spread_ref.shape[0]
    take_later(keep_ref, old_ref, behind_msg, later_ref)
    late = later_ref[:ns, :]
    whole = spread_ref[...]
    mixed = resolve(whole, late, pair)
    cov_ref[...] = exact(mixed, whole)
    offset = spread_rows(spread_msg, ns // 2)
    mean_ref[...] = exact(offset + exact(later_ref[ns:, :], whole), mixed, NT)


VMEM = pl.BlockSpec(memory_space=pltpu.VMEM)
SMEM = pl.BlockSpec(memory_space=pltpu.SMEM)


def call(kernel, args, rows, scratch, work, name):
    width = args[-1].shape[-1]
    read = sum(a.size for a in args) * 4
    return pl.pallas_call(
        kernel,
        out_shape=tuple(jax.ShapeDtypeStruct((r, width), F32) for r in rows),
        in_specs=[SMEM if a.ndim == 1 else VMEM for a in args],
        out_specs=tuple(VMEM for _ in rows),
        scratch_shapes=scratch,
        cost_estimate=pl.CostEstimate(flops=work, bytes_accessed=read, transcendentals=0),
        name=name,
    )(*args)


def shards(measurements, noise_levels, transition, sensing, process_noise, prior_mean, prior_covariance):
    ns = transition.shape[0]
    no = sensing.shape[0]
    count = lax.axis_size("tm")
    device = lax.axis_index("tm")
    pair = pltpu.VMEM((2 * ns, ns), F32)
    half = ns // 2 + 8
    full = ns + half
    work = 2 * ns**3 * 60
    sent, moved, ahead, spread, bind = call(
        leaf_kernel,
        (
            device.astype(jnp.int32).reshape(1),
            measurements,
            noise_levels,
            transition,
            sensing,
            process_noise,
            prior_mean.reshape(1, ns),
            prior_covariance,
        ),
        (half, full, half, ns, ns),
        [pltpu.VMEM((ns, ns), F32), pltpu.VMEM((8, ns), F32), pltpu.VMEM((2 * no, no), F32)],
        work,
        "leaf",
    )
    later = jnp.zeros((ns + 8, ns), F32)
    distance = 1
    behind = None
    keep = None
    while distance < count:
        up = [(i, i + distance) for i in range(count - distance)]
        down = [(i + distance, i) for i in range(count - distance)]
        last = distance * 2 >= count
        spread_in = lax.ppermute(sent, "tm", up)
        if not last:
            move_in = lax.ppermute(moved, "tm", up)
        new_sent, new_spread, middle = call(
            spread_kernel,
            (spread_in, sent, moved, spread, bind),
            (half, ns, 2 * ns + 8),
            [pair],
            work,
            "spread",
        )
        if behind is not None:
            ahead, later = call(
                ahead_kernel,
                (keep, sent, moved, spread, bind, later, behind),
                (half, ns + 8),
                [pair],
                work,
                "ahead",
            )
        behind = lax.ppermute(ahead, "tm", down)
        keep = (device + distance >= count).astype(jnp.int32).reshape(1)
        sent, spread = new_sent, new_spread
        if not last:
            moved, bind = call(move_kernel, (move_in, middle), (full, ns), [], work // 3, "move")
        distance *= 2
    mean, cov = call(
        last_kernel,
        (keep, sent, spread, later, behind),
        (8, ns),
        [pltpu.VMEM((ns + 8, ns), F32), pair],
        work,
        "last",
    )
    return (mean[:1], cov[None])


def solution(mesh):
    return jax.shard_map(
        shards,
        mesh=mesh,
        in_specs=(P("tm", None), P("tm", None), P(), P(), P(), P(), P()),
        out_specs=(P("tm", None), P("tm", None, None)),
        check_vma=False,
    )
```

```python
import functools

import jax
import jax.numpy as jnp
from jax import lax
from jax.experimental import pallas as pl
from jax.experimental.pallas import tpu as pltpu
from jax.sharding import PartitionSpec as P

F32 = jnp.float32
BF16 = jnp.bfloat16
NN = (((1,), (0,)), ((), ()))
NT = (((1,), (1,)), ((), ()))


def exact(left, right, dims=NN):
    return lax.dot_general(
        left, right, dims, precision=lax.Precision.HIGHEST, preferred_element_type=F32
    )


def rough(left, right, dims=NN):
    return lax.dot_general(
        left.astype(BF16), right.astype(BF16), dims, preferred_element_type=F32
    )


def unit(size):
    rows = lax.broadcasted_iota(jnp.int32, (size, size), 0)
    columns = lax.broadcasted_iota(jnp.int32, (size, size), 1)
    return (rows == columns).astype(F32)


def inverse(product, bound, pair):
    size = product.shape[0]
    eye = unit(size)
    whole = eye + product

    def descend(times, limit):
        low = 1.0 / bound
        scaled = whole * low
        gain = 4.0 / ((1.0 + low) * (1.0 + low))
        step = gain * ((1.0 + low) * eye - scaled)
        pair[:size, :] = step * low
        pair[size:, :] = times(scaled, step)

        def more(low):
            return low < limit

        def turn(low):
            gain = 4.0 / ((1.0 + low) * (1.0 + low))
            step = gain * ((1.0 + low) * eye - pair[size:, :])
            pair[...] = times(pair[...], step)
            return low * gain

        lax.while_loop(more, turn, low * gain)
        return times(pair[:size, :], 2.0 * eye - pair[size:, :])

    small = bound < 128.0

    @pl.when(small)
    def _():
        pair[:size, :] = descend(rough, 0.95)

    @pl.when(jnp.logical_not(small))
    def _():
        pair[:size, :] = descend(exact, 0.999)

    guess = pair[:size, :]
    for times in (rough, exact):
        guess = guess + rough(guess, eye - exact(whole, guess))
    return guess


def spectral_bound(product, mirrored):
    return 1.0 + 1.001 * jnp.sqrt(jnp.maximum(jnp.sum(product * mirrored), 0.0))


def pack(out, value, vector):
    ns = value.shape[0]
    n = ns // 2
    rows = lax.broadcasted_iota(jnp.int32, (n, n), 0)
    columns = lax.broadcasted_iota(jnp.int32, (n, n), 1)
    low, high = value[:n, :n], value[n:, n:]
    out[:n, :n] = value[n:, :n]
    out[:n, n:] = jnp.where(rows >= columns, low, high)
    out[n : n + 8, :] = jnp.zeros((8, ns), F32)
    out[n : n + 1, :] = vector[:1, :]
    out[n + 1 : n + 2, :n] = jnp.sum(
        jnp.where(rows == columns, high, 0.0), axis=0, keepdims=True
    )


def unpack(ref):
    ns = ref.shape[1]
    n = ns // 2
    rows = lax.broadcasted_iota(jnp.int32, (n, n), 0)
    columns = lax.broadcasted_iota(jnp.int32, (n, n), 1)
    corner = ref[:n, :n]
    mixed = ref[:n, n:]
    turned = mixed.T
    diagonal = jnp.broadcast_to(ref[n + 1 : n + 2, :n], (n, n))
    low = jnp.where(rows >= columns, mixed, turned)
    high = jnp.where(rows < columns, mixed, jnp.where(rows == columns, diagonal, turned))
    value = jnp.concatenate(
        [
            jnp.concatenate([low, corner.T], axis=1),
            jnp.concatenate([corner, high], axis=1),
        ],
        axis=0,
    )
    return value, spread_rows(ref, n)


def spread_rows(ref, at):
    return jnp.broadcast_to(ref[at : at + 1, :], (8, ref.shape[1]))


def leaf_kernel(
    first_ref, y_ref, r_ref, f_ref, h_ref, q_ref, m_ref, p_ref,
    spread_msg, move_msg, own_ref, bind_ref, noise, center, pair,
):
    first = first_ref[0] == 0
    no = h_ref.shape[0]
    ns = h_ref.shape[1]
    move = f_ref[...]
    noise[...] = q_ref[...]
    center[...] = jnp.zeros_like(center)

    @pl.when(first)
    def _():
        noise[...] += exact(exact(move, p_ref[...]), move, NT)
        center[...] = exact(jnp.broadcast_to(m_ref[...], center.shape), move, NT)

    active = jnp.where(first, 0.0, 1.0)
    eye = unit(no)
    weight = lax.rsqrt(r_ref[...])
    weights = jnp.sum(eye * weight, axis=1, keepdims=True)
    sense = h_ref[...] * weights
    y = jnp.broadcast_to(y_ref[...] * weight, (8, no))
    base = noise[...]
    gain = exact(sense, base)
    sensed = exact(sense, move)
    inner = exact(gain, sense, NT)
    mixed = inverse(inner, spectral_bound(inner, inner), pair)
    gained = exact(mixed, gain)
    joined = exact(mixed, sensed)
    gain_t = gain.T
    own_ref[:ns, :] = base - exact(gain_t, gained)
    bind_ref[...] = active * exact(sensed.T, joined)
    error = y - exact(center[...], sense, NT)
    own_ref[ns:, :] = center[...] + exact(error, gained)
    pack(spread_msg, own_ref[:ns, :], own_ref[ns:, :])
    move_msg[:ns, :] = active * (move - exact(gain_t, joined))
    pack(move_msg.at[ns:, :], bind_ref[...], active * exact(y, joined))


def resolve_kernel(with_later, arrived, own_ref, move_msg, bind_ref, later_ref, inner_ref, ahead_ref, pair):
    ns = own_ref.shape[1]
    pull = spread_rows(move_msg, ns + ns // 2)
    bind = bind_ref[...]
    both = exact(arrived[...], bind)
    product = both[:ns, :]
    limit = spectral_bound(product, rough(bind, arrived[:ns, :]))
    inner_ref[:ns, :] = inverse(product, limit, pair)
    inner_ref[ns:, :] = pull - both[ns:, :]
    if with_later:
        late = later_ref[:ns, :]
        both = exact(own_ref[...], late)
        product = both[:ns, :]
        limit = spectral_bound(product, rough(late, own_ref[:ns, :]))
        ahead_ref[:ns, :] = inverse(product, limit, pair)
        ahead_ref[ns:, :] = later_ref[ns:, :] - both[ns:, :]


def exchange_kernel(
    distance, count, begin, last,
    inner_ref, ahead_ref, arrived, own_ref, move_msg, bind_ref, later_ref,
    own_out, later_out, move_out, bind_out, arrived_out,
    stack, middle, spread_msg, bind_msg, move_land, spread_land, bind_land,
    send_sems, recv_sems,
):
    ns = own_ref.shape[1]
    mine = lax.axis_index("tm")
    hops = (distance, -distance) if last else (distance, -distance, 2 * distance, -2 * distance)
    barrier = pltpu.get_barrier_semaphore()
    expected = jnp.int32(0)
    for hop in hops:
        inside = jnp.logical_and(mine + hop >= 0, mine + hop < count)
        expected = expected + inside.astype(jnp.int32)

        @pl.when(inside)
        def _(hop=hop):
            pl.semaphore_signal(
                barrier, inc=1, device_id=(mine + hop,), device_id_type=pl.DeviceIdType.MESH
            )

    def carry(source, land, slot, hop):
        target = lax.rem(mine + hop + count, count)
        copy = pltpu.make_async_remote_copy(
            src_ref=source,
            dst_ref=land,
            send_sem=send_sems.at[slot],
            recv_sem=recv_sems.at[slot],
            device_id=(target,),
            device_id_type=pl.DeviceIdType.MESH,
        )
        sends = jnp.logical_and(mine + hop >= 0, mine + hop < count)
        takes = jnp.logical_and(mine - hop >= 0, mine - hop < count)
        return copy, sends, takes

    move_copy, move_sends, move_takes = carry(move_msg, move_land, 0, distance)
    spread_copy, spread_sends, spread_takes = carry(spread_msg, spread_land, 1, 2 * distance)
    bind_source = move_msg.at[ns:, :] if begin else bind_msg
    bind_copy, bind_sends, bind_takes = carry(bind_source, bind_land, 2, -distance)

    move = move_msg[:ns, :]
    stack[:ns, :] = move
    stack[ns : 2 * ns, :] = bind_ref[...]
    stack[2 * ns :, :] = inner_ref[ns:, :]
    middle[...] = exact(stack[...], inner_ref[:ns, :])
    pull = spread_rows(move_msg, ns + ns // 2)

    pl.semaphore_wait(barrier, expected)
    if not last:
        pl.when(move_sends)(move_copy.start)
    if begin:
        pl.when(bind_sends)(bind_copy.start)
    stack[:ns, :] = middle[:ns, :]
    stack[ns : ns + 8, :] = pull
    both = exact(stack[: ns + 8, :], arrived[:ns, :])
    offset = exact(arrived[ns:, :] + both[ns:, :], middle[:ns, :], NT)
    own_out[:ns, :] = exact(both[:ns, :], move, NT) + own_ref[:ns, :]
    own_out[ns:, :] = offset + own_ref[ns:, :]
    if not last:
        pack(spread_msg, own_out[:ns, :], own_out[ns:, :])
        pl.when(spread_sends)(spread_copy.start)
    if not begin:
        stack[:ns, :] = later_ref[:ns, :]
        stack[ns : ns + 8, :] = ahead_ref[ns:, :]
        both = exact(exact(stack[: ns + 8, :], ahead_ref[:ns, :]), move)
        pack(bind_msg, exact(move.T, both[:ns, :]) + bind_ref[...], both[ns:, :] + pull)
        pl.when(bind_sends)(bind_copy.start)

    if not last:

        @pl.when(move_takes)
        def _():
            move_copy.wait_recv()

        @pl.when(jnp.logical_not(move_takes))
        def _():
            move_land[...] = jnp.zeros_like(move_land)

        move_i = move_land[:ns, :]
        bind_i, pull_i = unpack(move_land.at[ns:, :])
        both = exact(middle[...], move_i)
        move_out[:ns, :] = both[:ns, :]
        bind_out[...] = exact(move_i.T, both[ns : 2 * ns, :]) + bind_i
        pack(move_out.at[ns:, :], bind_out[...], both[2 * ns :, :] + pull_i)

        @pl.when(spread_takes)
        def _():
            spread_copy.wait_recv()
            value, vector = unpack(spread_land)
            arrived_out[:ns, :] = value
            arrived_out[ns:, :] = vector

        @pl.when(jnp.logical_not(spread_takes))
        def _():
            arrived_out[...] = jnp.zeros_like(arrived_out)

        pl.when(move_sends)(move_copy.wait_send)
        pl.when(spread_sends)(spread_copy.wait_send)

    @pl.when(bind_takes)
    def _():
        bind_copy.wait_recv()
        value, vector = unpack(bind_land)
        later_out[:ns, :] = value
        later_out[ns:, :] = vector

    @pl.when(jnp.logical_not(bind_takes))
    def _():
        later_out[...] = later_ref[...]

    pl.when(bind_sends)(bind_copy.wait_send)


def last_kernel(own_ref, later_ref, mean_ref, cov_ref, pair):
    ns = own_ref.shape[1]
    late = later_ref[:ns, :]
    whole = own_ref[:ns, :]
    product = exact(whole, late)
    mixed = inverse(product, spectral_bound(product, rough(late, whole)), pair)
    cov_ref[...] = exact(mixed, whole)
    mean_ref[...] = exact(own_ref[ns:, :] + exact(later_ref[ns:, :], whole), mixed, NT)


def unpack_kernel(message, out):
    ns = out.shape[1]
    value, vector = unpack(message)
    out[:ns, :] = value
    out[ns:, :] = vector


VMEM = pl.BlockSpec(memory_space=pltpu.VMEM)
SMEM = pl.BlockSpec(memory_space=pltpu.SMEM)


def call(kernel, args, rows, scratch, work, name, **params):
    width = args[-1].shape[-1]
    read = sum(a.size for a in args) * 4
    return pl.pallas_call(
        kernel,
        out_shape=tuple(jax.ShapeDtypeStruct((r, width), F32) for r in rows),
        in_specs=[SMEM if a.ndim == 1 else VMEM for a in args],
        out_specs=tuple(VMEM for _ in rows),
        scratch_shapes=scratch,
        cost_estimate=pl.CostEstimate(flops=work, bytes_accessed=read, transcendentals=0),
        compiler_params=pltpu.CompilerParams(**params),
        name=name,
    )(*args)


def shards(measurements, noise_levels, transition, sensing, process_noise, prior_mean, prior_covariance):
    ns = transition.shape[0]
    no = sensing.shape[0]
    count = lax.axis_size("tm")
    device = lax.axis_index("tm")
    pair = pltpu.VMEM((2 * ns, ns), F32)
    half = ns // 2 + 8
    full = ns + half
    tall = ns + 8
    work = 2 * ns**3 * 60
    spread_msg, moved, own, bind = call(
        leaf_kernel,
        (
            device.astype(jnp.int32).reshape(1),
            measurements,
            noise_levels,
            transition,
            sensing,
            process_noise,
            prior_mean.reshape(1, ns),
            prior_covariance,
        ),
        (half, full, tall, ns),
        [pltpu.VMEM((ns, ns), F32), pltpu.VMEM((8, ns), F32), pltpu.VMEM((2 * no, no), F32)],
        work,
        "leaf",
    )
    spread_msg = lax.ppermute(spread_msg, "tm", [(i, i + 1) for i in range(count - 1)])
    (arrived,) = call(unpack_kernel, (spread_msg,), (tall,), [], work // 60, "unpack")
    later = jnp.zeros((tall, ns), F32)
    distance = 1
    while distance < count:
        begin = distance == 1
        last = distance * 2 >= count
        inner, ahead = call(
            functools.partial(resolve_kernel, not begin),
            (arrived, own, moved, bind, later),
            (tall, tall),
            [pair],
            work,
            "resolve",
        )
        small = (8, 8, 8) if last else (full, ns, tall)
        own, later, moved_new, bind_new, arrived = call(
            functools.partial(exchange_kernel, distance, count, begin, last),
            (inner, ahead, arrived, own, moved, bind, later),
            (tall, tall) + small,
            [
                pltpu.VMEM((2 * ns + 8, ns), F32),
                pltpu.VMEM((2 * ns + 8, ns), F32),
                pltpu.VMEM((half, ns), F32),
                pltpu.VMEM((half, ns), F32),
                pltpu.VMEM((full, ns), F32),
                pltpu.VMEM((half, ns), F32),
                pltpu.VMEM((half, ns), F32),
                pltpu.SemaphoreType.DMA((3,)),
                pltpu.SemaphoreType.DMA((3,)),
            ],
            work,
            f"exchange_{distance}",
            collective_id=distance.bit_length() - 1,
            has_side_effects=True,
        )
        moved, bind = moved_new, bind_new
        distance *= 2
    mean, cov = call(last_kernel, (own, later), (8, ns), [pair], work, "last")
    return (mean[:1], cov[None])


def solution(mesh):
    return jax.shard_map(
        shards,
        mesh=mesh,
        in_specs=(P("tm", None), P("tm", None), P(), P(), P(), P(), P()),
        out_specs=(P("tm", None), P("tm", None, None)),
        check_vma=False,
    )
```

```python
import functools

import jax
import jax.numpy as jnp
from jax import lax
from jax.experimental import pallas as pl
from jax.experimental.pallas import tpu as pltpu
from jax.sharding import PartitionSpec as P

F32 = jnp.float32
BF16 = jnp.bfloat16
NN = (((1,), (0,)), ((), ()))
NT = (((1,), (1,)), ((), ()))


def exact(left, right, dims=NN):
    return lax.dot_general(
        left, right, dims, precision=lax.Precision.HIGHEST, preferred_element_type=F32
    )


def rough(left, right, dims=NN):
    return lax.dot_general(
        left.astype(BF16), right.astype(BF16), dims, preferred_element_type=F32
    )


def unit(size):
    rows = lax.broadcasted_iota(jnp.int32, (size, size), 0)
    columns = lax.broadcasted_iota(jnp.int32, (size, size), 1)
    return (rows == columns).astype(F32)


def inverse(product, bound, pair):
    size = product.shape[0]
    eye = unit(size)
    whole = eye + product

    def descend(times, limit):
        low = 1.0 / bound
        scaled = whole * low
        gain = 4.0 / ((1.0 + low) * (1.0 + low))
        step = gain * ((1.0 + low) * eye - scaled)
        pair[:size, :] = step * low
        pair[size:, :] = times(scaled, step)

        def more(low):
            return low < limit

        def turn(low):
            gain = 4.0 / ((1.0 + low) * (1.0 + low))
            step = gain * ((1.0 + low) * eye - pair[size:, :])
            pair[...] = times(pair[...], step)
            return low * gain

        lax.while_loop(more, turn, low * gain)
        return times(pair[:size, :], 2.0 * eye - pair[size:, :])

    small = bound < 128.0

    @pl.when(small)
    def _():
        pair[:size, :] = descend(rough, 0.95)

    @pl.when(jnp.logical_not(small))
    def _():
        pair[:size, :] = descend(exact, 0.999)

    guess = pair[:size, :]
    for times in (rough, exact):
        guess = guess + rough(guess, eye - exact(whole, guess))
    return guess


def spectral_bound(product, mirrored):
    return 1.0 + 1.001 * jnp.sqrt(jnp.maximum(jnp.sum(product * mirrored), 0.0))


def pack(out, value, vector):
    ns = value.shape[0]
    n = ns // 2
    rows = lax.broadcasted_iota(jnp.int32, (n, n), 0)
    columns = lax.broadcasted_iota(jnp.int32, (n, n), 1)
    low, high = value[:n, :n], value[n:, n:]
    out[:n, :n] = value[n:, :n]
    out[:n, n:] = jnp.where(rows >= columns, low, high)
    out[n : n + 8, :] = jnp.zeros((8, ns), F32)
    out[n : n + 1, :] = vector[:1, :]
    out[n + 1 : n + 2, :n] = jnp.sum(
        jnp.where(rows == columns, high, 0.0), axis=0, keepdims=True
    )


def unpack(ref):
    ns = ref.shape[1]
    n = ns // 2
    rows = lax.broadcasted_iota(jnp.int32, (n, n), 0)
    columns = lax.broadcasted_iota(jnp.int32, (n, n), 1)
    corner = ref[:n, :n]
    mixed = ref[:n, n:]
    turned = mixed.T
    diagonal = jnp.broadcast_to(ref[n + 1 : n + 2, :n], (n, n))
    low = jnp.where(rows >= columns, mixed, turned)
    high = jnp.where(rows < columns, mixed, jnp.where(rows == columns, diagonal, turned))
    value = jnp.concatenate(
        [
            jnp.concatenate([low, corner.T], axis=1),
            jnp.concatenate([corner, high], axis=1),
        ],
        axis=0,
    )
    return value, spread_rows(ref, n)


def spread_rows(ref, at):
    return jnp.broadcast_to(ref[at : at + 1, :], (8, ref.shape[1]))


def fill(ref, value, vector):
    ns = value.shape[1]
    ref[:ns, :] = value
    ref[ns:, :] = vector


def leaf(first, y_ref, r_ref, f_ref, h_ref, noise, center, out, pair):
    no = h_ref.shape[0]
    ns = h_ref.shape[1]
    tall = ns + 8
    move = f_ref[...]
    active = jnp.where(first, 0.0, 1.0)
    eye = unit(no)
    weight = lax.rsqrt(r_ref[...])
    weights = jnp.sum(eye * weight, axis=1, keepdims=True)
    sense = h_ref[...] * weights
    y = jnp.broadcast_to(y_ref[...] * weight, (8, no))
    base = noise[...]
    gain = exact(sense, base)
    sensed = exact(sense, move)
    inner = exact(gain, sense, NT)
    mixed = inverse(inner, spectral_bound(inner, inner), pair)
    gained = exact(mixed, gain)
    joined = exact(mixed, sensed)
    gain_t = gain.T
    out[:ns, :] = active * (move - exact(gain_t, joined))
    error = y - exact(center[...], sense, NT)
    fill(
        out.at[ns : ns + tall, :],
        base - exact(gain_t, gained),
        center[...] + exact(error, gained),
    )
    fill(
        out.at[ns + tall :, :], active * exact(sensed.T, joined), active * exact(y, joined)
    )


def resolve(x_ref, y_ref, out, pair):
    ns = x_ref.shape[1]
    value = y_ref[:ns, :]
    both = exact(x_ref[...], value)
    product = both[:ns, :]
    bound = spectral_bound(product, rough(value, x_ref[:ns, :]))
    out[:ns, :] = inverse(product, bound, pair)
    out[ns:, :] = y_ref[ns:, :] - both[ns:, :]


def later_spread(through, x_ref, move, pull, s_ref, out):
    ns = x_ref.shape[1]
    carried = exact(through, x_ref[:ns, :])
    offset = exact(x_ref[ns:, :] + exact(pull, x_ref[:ns, :]), through, NT)
    fill(out, exact(carried, move, NT) + s_ref[:ns, :], offset + s_ref[ns:, :])


def start_kernel(
    place_ref, ye_ref, re_ref, yo_ref, ro_ref, f_ref, h_ref, q_ref, m_ref, p_ref,
    even, odd, s_out, move_out, y_out, spread_msg, noise, center, half_pair, solved, pair,
):
    chip, core = place_ref[0], place_ref[1]
    ns = h_ref.shape[1]
    tall = ns + 8
    move = f_ref[...]
    noise[...] = q_ref[...]
    center[...] = jnp.zeros_like(center)
    leaf(False, yo_ref, ro_ref, f_ref, h_ref, noise, center, odd, half_pair)

    @pl.when(chip == 0)
    def _():
        noise[...] += exact(exact(move, p_ref[...]), move, NT)
        center[...] = exact(jnp.broadcast_to(m_ref[...], center.shape), move, NT)

    leaf(chip == 0, ye_ref, re_ref, f_ref, h_ref, noise, center, even, half_pair)
    x_ref = even.at[ns : ns + tall, :]
    y_ref = odd.at[ns + tall :, :]
    resolve(x_ref, y_ref, solved, pair)
    later = odd[:ns, :]
    early = even[:ns, :]
    through = exact(later, solved[:ns, :])
    later_spread(through, x_ref, later, y_ref[ns:, :], odd.at[ns : ns + tall, :], s_out)
    pack(spread_msg, s_out[:ns, :], s_out[ns:, :])
    move_out[:ns, :] = exact(through, early)
    bound = exact(exact(y_ref[:ns, :], solved[:ns, :]), early)
    bind = exact(early.T, bound) + even[ns + tall : ns + tall + ns, :]
    pull = exact(exact(solved[ns:, :], solved[:ns, :]), early) + even[2 * ns + tall :, :]
    pack(move_out.at[ns:, :], bind, pull)
    scale = jnp.where(core == 0, 1.0, 0.0)
    fill(y_out, scale * bind, scale * pull)


def first_kernel(place_ref, message, s_ref, y_ref, x_out, out, pair):
    ns = x_out.shape[1]
    core = place_ref[1]

    @pl.when(core == 0)
    def _():
        fill(x_out, *unpack(message))

    @pl.when(core != 0)
    def _():
        x_out[...] = s_ref[...]

    resolve(x_out, y_ref, out, pair)


def resolve_kernel(x_ref, y_ref, out, pair):
    resolve(x_ref, y_ref, out, pair)


def greet(mine, count, cases):
    barrier = pltpu.get_barrier_semaphore()
    expected = jnp.int32(0)
    for wanted, hop in cases:
        inside = jnp.logical_and(mine + hop >= 0, mine + hop < count)
        inside = jnp.logical_and(inside, wanted)
        expected = expected + inside.astype(jnp.int32)

        @pl.when(inside)
        def _(hop=hop):
            pl.semaphore_signal(
                barrier, inc=1, device_id=(mine + hop,), device_id_type=pl.DeviceIdType.MESH
            )

    return lambda: pl.semaphore_wait(barrier, expected)


def exchange_kernel(
    hop, spread_hop, count, last,
    solved, x_ref, y_ref, s_ref, move_ref,
    x_out, y_out, s_out, move_out,
    middle, through, spread_msg, bind_msg, move_land, spread_land, bind_land,
    send_sems, recv_sems,
):
    ns = x_ref.shape[1]
    mine = lax.axis_index("tm")
    lead = lax.rem(mine, 2) == 0
    side = jnp.logical_not(lead)
    cases = [(lead, 1), (side, -1), (lead, spread_hop), (lead, -spread_hop)]
    if last:
        cases += [(side, hop), (side, -hop)]
    else:
        cases += [(True, hop), (True, -hop)]
    arrive = greet(mine, count, cases)

    def carry(source, land, send, recv, by):
        return pltpu.make_async_remote_copy(
            src_ref=source,
            dst_ref=land,
            send_sem=send_sems.at[send],
            recv_sem=recv_sems.at[recv],
            device_id=(lax.rem(mine + by + count, count),),
            device_id_type=pl.DeviceIdType.MESH,
        )

    def reaches(by):
        return jnp.logical_and(mine + by >= 0, mine + by < count)

    move_side = carry(move_ref, move_land, 0, 0, 1)
    spread_up = carry(spread_msg, spread_land, 1, 1, spread_hop)
    spread_side = carry(spread_msg, spread_land, 2, 1, 1)
    bind_down = carry(bind_msg, bind_land, 3, 2, -hop)
    move_sends = jnp.logical_and(lead, reaches(hop))
    spread_sends = jnp.logical_and(lead, reaches(spread_hop))
    bind_sends = jnp.logical_and(side, reaches(-hop))
    spread_takes = jnp.logical_or(side, reaches(-spread_hop))
    if last:
        joins = side
        move_takes = side
    else:
        move_up = carry(move_ref, move_land, 4, 0, hop)
        joins = True
        move_takes = jnp.logical_or(side, reaches(-hop))

    arrive()
    if not last:
        pl.when(move_sends)(move_up.start)
    pl.when(lead)(move_side.start)

    @pl.when(lead)
    def _():
        through[...] = exact(move_ref[:ns, :], solved[:ns, :])
        later_spread(through[...], x_ref, move_ref[:ns, :], y_ref[ns:, :], s_ref, s_out)
        pack(spread_msg, s_out[:ns, :], s_out[ns:, :])

    pl.when(spread_sends)(spread_up.start)
    pl.when(lead)(spread_side.start)

    fill(middle, y_ref[:ns, :], solved[ns:, :])
    middle[...] = exact(middle[...], solved[:ns, :])

    @pl.when(move_takes)
    def _():
        move_side.wait_recv()

    @pl.when(jnp.logical_not(move_takes))
    def _():
        move_land[...] = jnp.zeros_like(move_land)

    def rest():
        early = move_land[:ns, :]
        bind_i, pull_i = unpack(move_land.at[ns:, :])
        both = exact(middle[...], early)
        bind = exact(early.T, both[:ns, :]) + bind_i
        fill(y_out, bind, both[ns:, :] + pull_i)
        pack(bind_msg, y_out[:ns, :], y_out[ns:, :])

    if last:
        pl.when(side)(rest)
    else:
        rest()
    pl.when(bind_sends)(bind_down.start)
    if not last:

        @pl.when(lead)
        def _():
            move_out[:ns, :] = exact(through[...], move_land[:ns, :])
            move_out[ns:, :] = bind_msg[...]

    @pl.when(spread_takes)
    def _():
        spread_side.wait_recv()
        fill(x_out, *unpack(spread_land))

    @pl.when(jnp.logical_not(spread_takes))
    def _():
        x_out[...] = jnp.zeros_like(x_out)

    @pl.when(jnp.logical_and(side, reaches(hop)))
    def _():
        bind_down.wait_recv()
        fill(y_out, *unpack(bind_land))

    @pl.when(jnp.logical_and(side, jnp.logical_not(reaches(hop))))
    def _():
        y_out[...] = y_ref[...]

    if not last:
        pl.when(move_sends)(move_up.wait_send)
    pl.when(lead)(move_side.wait_send)
    pl.when(spread_sends)(spread_up.wait_send)
    pl.when(lead)(spread_side.wait_send)
    pl.when(bind_sends)(bind_down.wait_send)


def choose_kernel(place_ref, x_ref, y_ref, even, odd, out, left, right, pair):
    ns = x_ref.shape[1]
    tall = ns + 8
    core = place_ref[1]

    @pl.when(core == 0)
    def _():
        left[...] = x_ref[...]
        right[...] = even[ns + tall :, :]

    @pl.when(core != 0)
    def _():
        left[...] = odd[ns : ns + tall, :]
        right[...] = y_ref[...]

    resolve(left, right, out, pair)


def finish_kernel(count, solved, x_ref, y_ref, even, odd, s_out, y_out, middle, message, land, send_sem, recv_sem):
    ns = x_ref.shape[1]
    tall = ns + 8
    mine = lax.axis_index("tm")
    lead = lax.rem(mine, 2) == 0
    side = jnp.logical_not(lead)
    arrive = greet(mine, count, [(lead, 1), (side, -1)])
    copy = pltpu.make_async_remote_copy(
        src_ref=message,
        dst_ref=land,
        send_sem=send_sem,
        recv_sem=recv_sem,
        device_id=(lax.rem(mine - 1 + count, count),),
        device_id_type=pl.DeviceIdType.MESH,
    )

    @pl.when(lead)
    def _():
        move = even[:ns, :]
        through = exact(move, solved[:ns, :])
        later_spread(
            through, x_ref, move, even[2 * ns + tall :, :], even.at[ns : ns + tall, :], s_out
        )

    @pl.when(side)
    def _():
        move = odd[:ns, :]
        fill(middle, y_ref[:ns, :], solved[ns:, :])
        both = exact(exact(middle[...], solved[:ns, :]), move)
        bind = exact(move.T, both[:ns, :]) + odd[ns + tall : 2 * ns + tall, :]
        pack(message, bind, both[ns:, :] + odd[2 * ns + tall :, :])
        s_out[...] = x_ref[...]
        y_out[...] = y_ref[...]

    arrive()

    @pl.when(side)
    def _():
        copy.start()
        copy.wait_send()

    @pl.when(lead)
    def _():
        copy.wait_recv()
        fill(y_out, *unpack(land))


def last_kernel(own_ref, later_ref, mean_ref, cov_ref, pair):
    ns = own_ref.shape[1]
    late = later_ref[:ns, :]
    whole = own_ref[:ns, :]
    product = exact(whole, late)
    mixed = inverse(product, spectral_bound(product, rough(late, whole)), pair)
    cov_ref[...] = exact(mixed, whole)
    mean_ref[...] = exact(own_ref[ns:, :] + exact(later_ref[ns:, :], whole), mixed, NT)


VMEM = pl.BlockSpec(memory_space=pltpu.VMEM)
SMEM = pl.BlockSpec(memory_space=pltpu.SMEM)


def call(kernel, args, rows, scratch, work, name, **params):
    width = args[-1].shape[-1]
    read = sum(a.size for a in args) * 4
    return pl.pallas_call(
        kernel,
        out_shape=tuple(jax.ShapeDtypeStruct((r, width), F32) for r in rows),
        in_specs=[SMEM if a.ndim == 1 else VMEM for a in args],
        out_specs=tuple(VMEM for _ in rows),
        scratch_shapes=scratch,
        cost_estimate=pl.CostEstimate(flops=work, bytes_accessed=read, transcendentals=0),
        compiler_params=pltpu.CompilerParams(**params),
        name=name,
    )(*args)


def shards(measurements, noise_levels, transition, sensing, process_noise, prior_mean, prior_covariance):
    ns = transition.shape[0]
    no = sensing.shape[0]
    count = lax.axis_size("tm")
    device = lax.axis_index("tm").astype(jnp.int32)
    chip, core = device // 2, device % 2
    place = jnp.stack([chip, core])
    half = ns // 2 + 8
    full = ns + half
    tall = ns + 8
    work = 2 * ns**3 * 60

    def rows(r, columns=ns):
        return pltpu.VMEM((r, columns), F32)

    pair = rows(2 * ns)
    mine = jnp.concatenate([measurements, noise_levels], axis=0)
    other = lax.ppermute(mine, "tm", [(i, i ^ 1) for i in range(count)])
    lead = core == 0
    early = jnp.where(lead, mine, other)
    late = jnp.where(lead, other, mine)
    even, odd, s, moved, y, message = call(
        start_kernel,
        (
            place,
            early[:1],
            early[1:],
            late[:1],
            late[1:],
            transition,
            sensing,
            process_noise,
            prior_mean.reshape(1, ns),
            prior_covariance,
        ),
        (2 * tall + ns, 2 * tall + ns, tall, full, tall, half),
        [rows(ns), rows(8), rows(2 * no, no), rows(tall), pair],
        work,
        "start",
    )
    message = lax.ppermute(message, "tm", [(i, i + 2) for i in range(0, count - 2, 2)])
    x, solved = call(first_kernel, (place, message, s, y), (tall, tall), [pair], work, "first")
    hop = 2
    while hop < count:
        last = hop * 2 >= count
        small = (tall, 8) if last else (tall, full)
        spread_hop = 2 if last else 2 * hop
        x, y, s, moved = call(
            functools.partial(exchange_kernel, hop, spread_hop, count, last),
            (solved, x, y, s, moved),
            (tall, tall) + small,
            [
                rows(tall),
                rows(ns),
                rows(half),
                rows(half),
                rows(full),
                rows(half),
                rows(half),
                pltpu.SemaphoreType.DMA((5,)),
                pltpu.SemaphoreType.DMA((3,)),
            ],
            work,
            f"exchange_{hop}",
            collective_id=hop.bit_length(),
            has_side_effects=True,
        )
        if not last:
            (solved,) = call(resolve_kernel, (x, y), (tall,), [pair], work, "resolve")
        hop *= 2
    (solved,) = call(
        choose_kernel, (place, x, y, even, odd), (tall,), [rows(tall), rows(tall), pair], work, "choose"
    )
    own, later = call(
        functools.partial(finish_kernel, count),
        (solved, x, y, even, odd),
        (tall, tall),
        [rows(tall), rows(half), rows(half), pltpu.SemaphoreType.DMA, pltpu.SemaphoreType.DMA],
        work,
        "finish",
        collective_id=0,
        has_side_effects=True,
    )
    mean, cov = call(last_kernel, (own, later), (8, ns), [pair], work, "last")
    return (mean[:1], cov[None])


def solution(mesh):
    return jax.shard_map(
        shards,
        mesh=mesh,
        in_specs=(P("tm", None), P("tm", None), P(), P(), P(), P(), P()),
        out_specs=(P("tm", None), P("tm", None, None)),
        check_vma=False,
    )
```

```python
import functools

import jax
import jax.numpy as jnp
from jax import lax
from jax.experimental import pallas as pl
from jax.experimental.pallas import tpu as pltpu
from jax.sharding import PartitionSpec as P

F32 = jnp.float32
BF16 = jnp.bfloat16
NN = (((1,), (0,)), ((), ()))
NT = (((1,), (1,)), ((), ()))


def exact(left, right, dims=NN):
    return lax.dot_general(
        left, right, dims, precision=lax.Precision.HIGHEST, preferred_element_type=F32
    )


def rough(left, right, dims=NN):
    return lax.dot_general(
        left.astype(BF16), right.astype(BF16), dims, preferred_element_type=F32
    )


def unit(size):
    rows = lax.broadcasted_iota(jnp.int32, (size, size), 0)
    columns = lax.broadcasted_iota(jnp.int32, (size, size), 1)
    return (rows == columns).astype(F32)


def medium(left, right, dims=NN):
    left_high, right_high = left.astype(BF16), right.astype(BF16)
    left_low = (left - left_high.astype(F32)).astype(BF16)
    right_low = (right - right_high.astype(F32)).astype(BF16)

    def times(a, b):
        return lax.dot_general(a, b, dims, preferred_element_type=F32)

    return times(left_high, right_high) + (
        times(left_high, right_low) + times(left_low, right_high)
    )


def inverse(product, bound, pair):
    size = product.shape[0]
    eye = unit(size)
    whole = eye + product
    small = bound < 128.0

    def gain_of(low):
        return 4.0 / ((1.0 + low) * (1.0 + low))

    @pl.when(small)
    def _():
        low = 1.0 / bound
        scaled = whole * low
        step = gain_of(low) * ((1.0 + low) * eye - scaled)
        pair[:size, :] = step * low
        pair[size : 2 * size, :] = rough(scaled, step)

        def turn(low):
            step = gain_of(low) * ((1.0 + low) * eye - pair[size : 2 * size, :])
            pair[: 2 * size, :] = rough(pair[: 2 * size, :], step)
            return low * gain_of(low)

        lax.while_loop(lambda low: low < 0.95, turn, low * gain_of(low))
        pair[:size, :] = rough(pair[:size, :], 2.0 * eye - pair[size : 2 * size, :])

    @pl.when(jnp.logical_not(small))
    def _():
        low = 1.0 / bound
        pair[:size, :] = eye * low
        pair[size : 2 * size, :] = whole * low

        def apply(rows):
            def block(i, carry):
                at = pl.ds(pl.multiple_of(i * 64, 64), 64)
                pair[at, :] = exact(pair[at, :], pair[2 * size :, :])
                return carry

            lax.fori_loop(0, rows // 64, block, 0)

        def turn(low):
            pair[2 * size :, :] = gain_of(low) * (
                (1.0 + low) * eye - pair[size : 2 * size, :]
            )
            apply(2 * size)
            return low * gain_of(low)

        lax.while_loop(lambda low: low < 0.999, turn, low)
        pair[2 * size :, :] = 2.0 * eye - pair[size : 2 * size, :]
        apply(size)

    guess = pair[:size, :]
    guess = guess + rough(guess, eye - medium(whole, guess))
    return guess + rough(guess, eye - exact(whole, guess))


def spectral_bound(product, mirrored):
    return 1.0 + 1.02 * jnp.sqrt(jnp.maximum(jnp.sum(product * mirrored), 0.0))


def pack(out, value, vector):
    ns = value.shape[0]
    n = ns // 2
    rows = lax.broadcasted_iota(jnp.int32, (n, n), 0)
    columns = lax.broadcasted_iota(jnp.int32, (n, n), 1)
    low, high = value[:n, :n], value[n:, n:]
    out[:n, :n] = value[n:, :n]
    out[:n, n:] = jnp.where(rows >= columns, low, high)
    out[n : n + 8, :] = jnp.zeros((8, ns), F32)
    out[n : n + 1, :] = vector[:1, :]
    out[n + 1 : n + 2, :n] = jnp.sum(
        jnp.where(rows == columns, high, 0.0), axis=0, keepdims=True
    )


def unpack(ref):
    ns = ref.shape[1]
    n = ns // 2
    rows = lax.broadcasted_iota(jnp.int32, (n, n), 0)
    columns = lax.broadcasted_iota(jnp.int32, (n, n), 1)
    corner = ref[:n, :n]
    mixed = ref[:n, n:]
    turned = mixed.T
    diagonal = jnp.broadcast_to(ref[n + 1 : n + 2, :n], (n, n))
    low = jnp.where(rows >= columns, mixed, turned)
    high = jnp.where(rows < columns, mixed, jnp.where(rows == columns, diagonal, turned))
    value = jnp.concatenate(
        [
            jnp.concatenate([low, corner.T], axis=1),
            jnp.concatenate([corner, high], axis=1),
        ],
        axis=0,
    )
    return value, spread_rows(ref, n)


def spread_rows(ref, at):
    return jnp.broadcast_to(ref[at : at + 1, :], (8, ref.shape[1]))


def fill(ref, value, vector):
    ns = value.shape[1]
    ref[:ns, :] = value
    ref[ns:, :] = vector


def leaf(first, y_ref, r_ref, f_ref, h_ref, noise, center, out, pair):
    no = h_ref.shape[0]
    ns = h_ref.shape[1]
    tall = ns + 8
    move = f_ref[...]
    active = jnp.where(first, 0.0, 1.0)
    eye = unit(no)
    weight = lax.rsqrt(r_ref)
    weights = jnp.sum(eye * weight, axis=1, keepdims=True)
    sense = h_ref[...] * weights
    y = jnp.broadcast_to(y_ref * weight, (8, no))
    base = noise[...]
    gain = exact(sense, base)
    sensed = exact(sense, move)
    inner = exact(gain, sense, NT)
    mixed = inverse(inner, spectral_bound(inner, inner), pair)
    gained = exact(mixed, gain)
    joined = exact(mixed, sensed)
    gain_t = gain.T
    out[:ns, :] = active * (move - exact(gain_t, joined))
    error = y - exact(center[...], sense, NT)
    fill(
        out.at[ns : ns + tall, :],
        base - exact(gain_t, gained),
        center[...] + exact(error, gained),
    )
    fill(
        out.at[ns + tall :, :], active * exact(sensed.T, joined), active * exact(y, joined)
    )


def resolve(x_ref, y_ref, out, pair):
    ns = x_ref.shape[1]
    value = y_ref[:ns, :]
    both = exact(x_ref[...], value)
    product = both[:ns, :]
    bound = spectral_bound(product, rough(value, x_ref[:ns, :]))
    out[:ns, :] = inverse(product, bound, pair)
    out[ns:, :] = y_ref[ns:, :] - both[ns:, :]


def later_spread(through, x_ref, move, pull, s_ref, out):
    ns = x_ref.shape[1]
    carried = exact(through, x_ref[:ns, :])
    offset = exact(x_ref[ns:, :] + exact(pull, x_ref[:ns, :]), through, NT)
    fill(out, exact(carried, move, NT) + s_ref[:ns, :], offset + s_ref[ns:, :])


def start_kernel(
    place_ref, mine_ref, other_ref, f_ref, h_ref, q_ref, m_ref, p_ref,
    even, odd, s_out, move_out, bind_out, y_out, spread_msg, noise, center, half_pair, solved, pair,
):
    chip, core = lax.div(place_ref[0], 2), lax.rem(place_ref[0], 2)
    lead = core == 0
    ye_ref = jnp.where(lead, mine_ref[:1, :], other_ref[:1, :])
    re_ref = jnp.where(lead, mine_ref[1:2, :], other_ref[1:2, :])
    yo_ref = jnp.where(lead, other_ref[:1, :], mine_ref[:1, :])
    ro_ref = jnp.where(lead, other_ref[1:2, :], mine_ref[1:2, :])
    ns = h_ref.shape[1]
    tall = ns + 8
    move = f_ref[...]
    noise[...] = q_ref[...]
    center[...] = jnp.zeros_like(center)
    leaf(False, yo_ref, ro_ref, f_ref, h_ref, noise, center, odd, half_pair)

    @pl.when(chip == 0)
    def _():
        noise[...] += exact(exact(move, p_ref[...]), move, NT)
        center[...] = exact(jnp.broadcast_to(m_ref[...], center.shape), move, NT)

    leaf(chip == 0, ye_ref, re_ref, f_ref, h_ref, noise, center, even, half_pair)
    x_ref = even.at[ns : ns + tall, :]
    y_ref = odd.at[ns + tall :, :]
    resolve(x_ref, y_ref, solved, pair)
    later = odd[:ns, :]
    early = even[:ns, :]
    through = exact(later, solved[:ns, :])
    later_spread(through, x_ref, later, y_ref[ns:, :], odd.at[ns : ns + tall, :], s_out)
    pack(spread_msg, s_out[:ns, :], s_out[ns:, :])
    move_out[...] = exact(through, early)
    bound = exact(exact(y_ref[:ns, :], solved[:ns, :]), early)
    bind = exact(early.T, bound) + even[ns + tall : ns + tall + ns, :]
    pull = exact(exact(solved[ns:, :], solved[:ns, :]), early) + even[2 * ns + tall :, :]
    pack(bind_out, bind, pull)
    scale = jnp.where(core == 0, 1.0, 0.0)
    fill(y_out, scale * bind, scale * pull)


def resolve_kernel(x_ref, y_ref, out, pair):
    resolve(x_ref, y_ref, out, pair)


def greet(mine, count, cases):
    barrier = pltpu.get_barrier_semaphore()
    expected = jnp.int32(0)
    for wanted, hop in cases:
        inside = jnp.logical_and(mine + hop >= 0, mine + hop < count)
        inside = jnp.logical_and(inside, wanted)
        expected = expected + inside.astype(jnp.int32)

        @pl.when(inside)
        def _(hop=hop):
            pl.semaphore_signal(
                barrier, inc=1, device_id=(mine + hop,), device_id_type=pl.DeviceIdType.MESH
            )


    def arrive():
        @pl.when(expected > 0)
        def _():
            pl.semaphore_wait(barrier, expected)

    return arrive


def shift_kernel(hop, count, message, s_ref, x_out, land, send_sem, recv_sem):
    mine = lax.axis_index("tm")
    lead = lax.rem(mine, 2) == 0
    side = jnp.logical_not(lead)
    arrive = greet(mine, count, [(lead, hop), (lead, -hop)])
    copy = pltpu.make_async_remote_copy(
        src_ref=message,
        dst_ref=land,
        send_sem=send_sem,
        recv_sem=recv_sem,
        device_id=(lax.rem(mine + hop, count),),
        device_id_type=pl.DeviceIdType.MESH,
    )
    sends = jnp.logical_and(lead, mine + hop < count)
    takes = jnp.logical_and(lead, mine - hop >= 0)
    arrive()
    pl.when(sends)(copy.start)

    @pl.when(side)
    def _():
        x_out[...] = s_ref[...]

    @pl.when(jnp.logical_and(lead, mine - hop < 0))
    def _():
        x_out[...] = jnp.zeros_like(x_out)

    @pl.when(takes)
    def _():
        copy.wait_recv()
        fill(x_out, *unpack(land))

    pl.when(sends)(copy.wait_send)


def exchange_kernel(
    hop, spread_hop, count, last,
    solved, x_ref, y_ref, s_ref, move_ref, bind_ref,
    x_out, y_out, s_out, move_out, bind_out,
    middle, through, spread_msg, bind_msg, move_land, pull_land, spread_land, bind_land,
    send_sems, recv_sems,
):
    ns = x_ref.shape[1]
    mine = lax.axis_index("tm")
    lead = lax.rem(mine, 2) == 0
    side = jnp.logical_not(lead)
    cases = [(lead, 1), (side, -1), (lead, spread_hop), (lead, -spread_hop)]
    if last:
        cases += [(side, hop), (side, -hop)]
    else:
        cases += [(True, hop), (True, -hop)]
    arrive = greet(mine, count, cases)

    def carry(source, land, send, recv, by):
        return pltpu.make_async_remote_copy(
            src_ref=source,
            dst_ref=land,
            send_sem=send_sems.at[send],
            recv_sem=recv_sems.at[recv],
            device_id=(lax.rem(mine + by + count, count),),
            device_id_type=pl.DeviceIdType.MESH,
        )

    def reaches(by):
        return jnp.logical_and(mine + by >= 0, mine + by < count)

    move_side = carry(move_ref, move_land, 0, 0, 1)
    pull_side = carry(bind_ref, pull_land, 1, 1, 1)
    spread_up = carry(spread_msg, spread_land, 2, 2, spread_hop)
    spread_side = carry(spread_msg, spread_land, 3, 2, 1)
    bind_down = carry(bind_msg, bind_land, 4, 3, -hop)
    move_sends = jnp.logical_and(lead, reaches(hop))
    spread_sends = jnp.logical_and(lead, reaches(spread_hop))
    bind_sends = jnp.logical_and(side, reaches(-hop))
    spread_takes = jnp.logical_or(side, reaches(-spread_hop))
    if last:
        move_takes = side
    else:
        move_up = carry(move_ref, move_land, 5, 0, hop)
        pull_up = carry(bind_ref, pull_land, 6, 1, hop)
        move_takes = jnp.logical_or(side, reaches(-hop))

    @pl.when(lead)
    def _():
        through[...] = exact(move_ref[...], solved[:ns, :])

    @pl.when(side)
    def _():
        fill(middle, y_ref[:ns, :], solved[ns:, :])
        middle[...] = medium(middle[...], solved[:ns, :])

    arrive()
    if not last:

        @pl.when(move_sends)
        def _():
            move_up.start()
            pull_up.start()

    @pl.when(lead)
    def _():
        move_side.start()
        pull_side.start()
        later_spread(through[...], x_ref, move_ref[...], y_ref[ns:, :], s_ref, s_out)
        pack(spread_msg, s_out[:ns, :], s_out[ns:, :])

    pl.when(spread_sends)(spread_up.start)

    @pl.when(lead)
    def _():
        spread_side.start()
        if not last:
            fill(middle, y_ref[:ns, :], solved[ns:, :])
            middle[...] = medium(middle[...], solved[:ns, :])

    @pl.when(move_takes)
    def _():
        move_side.wait_recv()

    @pl.when(jnp.logical_not(move_takes))
    def _():
        move_land[...] = jnp.zeros_like(move_land)
        pull_land[...] = jnp.zeros_like(pull_land)

    def rest():
        early = move_land[...]
        both = medium(middle[...], early)
        bind = medium(early.T, both[:ns, :])

        @pl.when(move_takes)
        def _():
            pull_side.wait_recv()

        bind_i, pull_i = unpack(pull_land)
        fill(y_out, bind + bind_i, both[ns:, :] + pull_i)
        pack(bind_msg, y_out[:ns, :], y_out[ns:, :])

    if last:
        pl.when(side)(rest)
    else:
        rest()
    pl.when(bind_sends)(bind_down.start)
    if not last:

        @pl.when(lead)
        def _():
            move_out[...] = exact(through[...], move_land[...])
            bind_out[...] = bind_msg[...]

    @pl.when(spread_takes)
    def _():
        spread_side.wait_recv()
        fill(x_out, *unpack(spread_land))

    @pl.when(jnp.logical_not(spread_takes))
    def _():
        x_out[...] = jnp.zeros_like(x_out)

    @pl.when(jnp.logical_and(side, reaches(hop)))
    def _():
        bind_down.wait_recv()
        fill(y_out, *unpack(bind_land))

    @pl.when(jnp.logical_and(side, jnp.logical_not(reaches(hop))))
    def _():
        y_out[...] = y_ref[...]

    if not last:

        @pl.when(move_sends)
        def _():
            move_up.wait_send()
            pull_up.wait_send()

    @pl.when(lead)
    def _():
        move_side.wait_send()
        pull_side.wait_send()

    pl.when(spread_sends)(spread_up.wait_send)
    pl.when(lead)(spread_side.wait_send)
    pl.when(bind_sends)(bind_down.wait_send)


def choose_kernel(place_ref, x_ref, y_ref, even, odd, out, left, right, pair):
    ns = x_ref.shape[1]
    tall = ns + 8
    core = lax.rem(place_ref[0], 2)

    @pl.when(core == 0)
    def _():
        left[...] = x_ref[...]
        right[...] = even[ns + tall :, :]

    @pl.when(core != 0)
    def _():
        left[...] = odd[ns : ns + tall, :]
        right[...] = y_ref[...]

    resolve(left, right, out, pair)


def finish_kernel(count, solved, x_ref, y_ref, even, odd, s_out, y_out, middle, message, land, send_sem, recv_sem):
    ns = x_ref.shape[1]
    tall = ns + 8
    mine = lax.axis_index("tm")
    lead = lax.rem(mine, 2) == 0
    side = jnp.logical_not(lead)
    arrive = greet(mine, count, [(lead, 1), (side, -1)])
    copy = pltpu.make_async_remote_copy(
        src_ref=message,
        dst_ref=land,
        send_sem=send_sem,
        recv_sem=recv_sem,
        device_id=(lax.rem(mine - 1 + count, count),),
        device_id_type=pl.DeviceIdType.MESH,
    )

    @pl.when(lead)
    def _():
        move = even[:ns, :]
        through = exact(move, solved[:ns, :])
        later_spread(
            through, x_ref, move, even[2 * ns + tall :, :], even.at[ns : ns + tall, :], s_out
        )

    @pl.when(side)
    def _():
        move = odd[:ns, :]
        fill(middle, y_ref[:ns, :], solved[ns:, :])
        both = medium(medium(middle[...], solved[:ns, :]), move)
        bind = medium(move.T, both[:ns, :]) + odd[ns + tall : 2 * ns + tall, :]
        pack(message, bind, both[ns:, :] + odd[2 * ns + tall :, :])
        s_out[...] = x_ref[...]
        y_out[...] = y_ref[...]

    arrive()

    @pl.when(side)
    def _():
        copy.start()
        copy.wait_send()

    @pl.when(lead)
    def _():
        copy.wait_recv()
        fill(y_out, *unpack(land))


def last_kernel(own_ref, later_ref, mean_ref, cov_ref, pair):
    ns = own_ref.shape[1]
    late = later_ref[:ns, :]
    whole = own_ref[:ns, :]
    product = exact(whole, late)
    mixed = inverse(product, spectral_bound(product, rough(late, whole)), pair)
    cov_ref[...] = exact(mixed, whole)
    mean_ref[...] = exact(own_ref[ns:, :] + exact(later_ref[ns:, :], whole), mixed, NT)[:1, :]


KERNEL_VMEM = 16 * 2**20
VMEM = pl.BlockSpec(memory_space=pltpu.VMEM)
SMEM = pl.BlockSpec(memory_space=pltpu.SMEM)


def call(kernel, args, rows, scratch, work, name, **params):
    width = args[-1].shape[-1]
    read = sum(a.size for a in args) * 4
    return pl.pallas_call(
        kernel,
        out_shape=tuple(jax.ShapeDtypeStruct((r, width), F32) for r in rows),
        in_specs=[SMEM if a.ndim == 1 else VMEM for a in args],
        out_specs=tuple(VMEM for _ in rows),
        scratch_shapes=scratch,
        cost_estimate=pl.CostEstimate(flops=work, bytes_accessed=read, transcendentals=0),
        compiler_params=pltpu.CompilerParams(vmem_limit_bytes=KERNEL_VMEM, **params),
        name=name,
    )(*args)


def shards(measurements, noise_levels, transition, sensing, process_noise, prior_mean, prior_covariance):
    ns = transition.shape[0]
    no = sensing.shape[0]
    count = lax.axis_size("tm")
    device = lax.axis_index("tm").astype(jnp.int32)
    place = device.reshape(1)
    half = ns // 2 + 8
    tall = ns + 8
    work = 2 * ns**3 * 60

    def rows(r, columns=ns):
        return pltpu.VMEM((r, columns), F32)

    pair = rows(3 * ns)
    mine = jnp.concatenate([measurements, noise_levels], axis=0)
    other = lax.ppermute(mine, "tm", [(i, i ^ 1) for i in range(count)])
    even, odd, s, moved, bound, y, message = call(
        start_kernel,
        (
            place,
            mine,
            other,
            transition,
            sensing,
            process_noise,
            prior_mean.reshape(1, ns),
            prior_covariance,
        ),
        (2 * tall + ns, 2 * tall + ns, tall, ns, half, tall, half),
        [rows(ns), rows(8), rows(3 * no, no), rows(tall), pair],
        work,
        "start",
    )
    (x,) = call(
        functools.partial(shift_kernel, 2, count),
        (message, s),
        (tall,),
        [rows(half), pltpu.SemaphoreType.DMA, pltpu.SemaphoreType.DMA],
        work // 60,
        "shift",
        collective_id=1,
        has_side_effects=True,
    )
    hop = 2
    while hop < count:
        last = hop * 2 >= count
        small = (8, 8) if last else (ns, half)
        spread_hop = 2 if last else 2 * hop
        (solved,) = call(resolve_kernel, (x, y), (tall,), [pair], work, "resolve")
        x, y, s, moved, bound = call(
            functools.partial(exchange_kernel, hop, spread_hop, count, last),
            (solved, x, y, s, moved, bound),
            (tall, tall, tall) + small,
            [
                rows(tall),
                rows(ns),
                rows(half),
                rows(half),
                rows(ns),
                rows(half),
                rows(half),
                rows(half),
                pltpu.SemaphoreType.DMA((7,)),
                pltpu.SemaphoreType.DMA((4,)),
            ],
            work,
            f"exchange_{hop}",
            collective_id=hop.bit_length(),
            has_side_effects=True,
        )
        hop *= 2
    (solved,) = call(
        choose_kernel, (place, x, y, even, odd), (tall,), [rows(tall), rows(tall), pair], work, "choose"
    )
    own, later = call(
        functools.partial(finish_kernel, count),
        (solved, x, y, even, odd),
        (tall, tall),
        [rows(tall), rows(half), rows(half), pltpu.SemaphoreType.DMA, pltpu.SemaphoreType.DMA],
        work,
        "finish",
        collective_id=0,
        has_side_effects=True,
    )
    mean, cov = call(last_kernel, (own, later), (1, ns), [pair], work, "last")
    return (mean, cov[None])


def solution(mesh):
    return jax.shard_map(
        shards,
        mesh=mesh,
        in_specs=(P("tm", None), P("tm", None), P(), P(), P(), P(), P()),
        out_specs=(P("tm", None), P("tm", None, None)),
        check_vma=False,
    )
```

```python
import functools

import jax
import jax.numpy as jnp
from jax import lax
from jax.experimental import pallas as pl
from jax.experimental.pallas import tpu as pltpu
from jax.sharding import PartitionSpec as P

F32 = jnp.float32
BF16 = jnp.bfloat16
NN = (((1,), (0,)), ((), ()))
NT = (((1,), (1,)), ((), ()))


def exact(left, right, dims=NN):
    return lax.dot_general(
        left, right, dims, precision=lax.Precision.HIGHEST, preferred_element_type=F32
    )


def rough(left, right, dims=NN):
    return lax.dot_general(
        left.astype(BF16), right.astype(BF16), dims, preferred_element_type=F32
    )


def unit(size):
    rows = lax.broadcasted_iota(jnp.int32, (size, size), 0)
    columns = lax.broadcasted_iota(jnp.int32, (size, size), 1)
    return (rows == columns).astype(F32)


def medium(left, right, dims=NN):
    left_high, right_high = left.astype(BF16), right.astype(BF16)
    left_low = (left - left_high.astype(F32)).astype(BF16)
    right_low = (right - right_high.astype(F32)).astype(BF16)

    def times(a, b):
        return lax.dot_general(a, b, dims, preferred_element_type=F32)

    return times(left_high, right_high) + (
        times(left_high, right_low) + times(left_low, right_high)
    )


def inverse(product, bound, pair):
    size = product.shape[0]
    eye = unit(size)
    whole = eye + product
    small = bound < 128.0

    def gain_of(low):
        return 4.0 / ((1.0 + low) * (1.0 + low))

    def more(state):
        return jnp.logical_not(state[1])

    @pl.when(small)
    def _():
        low = 1.0 / bound
        scaled = whole * low
        step = gain_of(low) * ((1.0 + low) * eye - scaled)
        pair[:size, :] = step * low
        pair[size : 2 * size, :] = rough(scaled, step)

        def turn(state):
            low, _ = state
            ends = low >= 0.95
            low = jnp.where(ends, 1.0, low)
            step = gain_of(low) * ((1.0 + low) * eye - pair[size : 2 * size, :])
            pair[: 2 * size, :] = rough(pair[: 2 * size, :], step)
            return low * gain_of(low), ends

        lax.while_loop(more, turn, (low * gain_of(low), jnp.bool_(False)))

    @pl.when(jnp.logical_not(small))
    def _():
        low = 1.0 / bound
        pair[:size, :] = eye * low
        pair[size : 2 * size, :] = whole * low

        def turn(state):
            low, _ = state
            ends = low >= 0.999
            low = jnp.where(ends, 1.0, low)
            pair[2 * size :, :] = gain_of(low) * (
                (1.0 + low) * eye - pair[size : 2 * size, :]
            )

            def block(i, carry):
                at = pl.ds(pl.multiple_of(i * 32, 32), 32)
                pair[at, :] = exact(pair[at, :], pair[2 * size :, :])
                return carry

            lax.fori_loop(0, 2 * size // 32, block, 0)
            return low * gain_of(low), ends

        lax.while_loop(more, turn, (low, jnp.bool_(False)))

    def correct(i, carry):
        guess = pair[:size, :]
        pair[:size, :] = guess + rough(guess, eye - medium(whole, guess))
        return carry

    lax.fori_loop(0, 2, correct, 0)
    return pair[:size, :]


def spectral_bound(product, mirrored):
    return 1.0 + 1.02 * jnp.sqrt(jnp.maximum(jnp.sum(product * mirrored), 0.0))


def pack(out, value, vector):
    ns = value.shape[0]
    n = ns // 2
    rows = lax.broadcasted_iota(jnp.int32, (n, n), 0)
    columns = lax.broadcasted_iota(jnp.int32, (n, n), 1)
    low, high = value[:n, :n], value[n:, n:]
    out[:n, :n] = value[n:, :n]
    out[:n, n:] = jnp.where(rows >= columns, low, high)
    out[n : n + 8, :] = jnp.zeros((8, ns), F32)
    out[n : n + 1, :] = vector[:1, :]
    out[n + 1 : n + 2, :n] = jnp.sum(
        jnp.where(rows == columns, high, 0.0), axis=0, keepdims=True
    )


def unpack(ref):
    ns = ref.shape[1]
    n = ns // 2
    rows = lax.broadcasted_iota(jnp.int32, (n, n), 0)
    columns = lax.broadcasted_iota(jnp.int32, (n, n), 1)
    corner = ref[:n, :n]
    mixed = ref[:n, n:]
    turned = mixed.T
    diagonal = jnp.broadcast_to(ref[n + 1 : n + 2, :n], (n, n))
    low = jnp.where(rows >= columns, mixed, turned)
    high = jnp.where(rows < columns, mixed, jnp.where(rows == columns, diagonal, turned))
    value = jnp.concatenate(
        [
            jnp.concatenate([low, corner.T], axis=1),
            jnp.concatenate([corner, high], axis=1),
        ],
        axis=0,
    )
    return value, spread_rows(ref, n)


def spread_rows(ref, at):
    return jnp.broadcast_to(ref[at : at + 1, :], (8, ref.shape[1]))


def fill(ref, value, vector):
    ns = value.shape[1]
    ref[:ns, :] = value
    ref[ns:, :] = vector


def resolve(x_ref, y_ref, out, pair):
    ns = x_ref.shape[1]
    value = y_ref[:ns, :]
    both = medium(x_ref[...], value)
    product = both[:ns, :]
    bound = spectral_bound(product, rough(value, x_ref[:ns, :]))
    out[:ns, :] = inverse(product, bound, pair)
    out[ns:, :] = y_ref[ns:, :] - both[ns:, :]


def later_spread(through, x_ref, move, s_ref, out):
    ns = x_ref.shape[1]
    carried = medium(through[...], x_ref[:ns, :])
    offset = exact(x_ref[ns:, :] + carried[ns:, :], through[:ns, :], NT)
    fill(out, medium(carried[:ns, :], move, NT) + s_ref[:ns, :], offset + s_ref[ns:, :])


def start_kernel(
    place_ref, mine_ref, other_ref, f_hbm, h_hbm, q_hbm, m_ref, p_hbm,
    leaves, x_out, y_out,
    f_ref, h_ref, noise, p_ref, center, plain, sensed_plain, inner_plain, half_pair, sems,
):
    chip, core = lax.div(place_ref[0], 2), lax.rem(place_ref[0], 2)
    lead = core == 0
    no, ns = h_ref.shape
    tall = ns + 8
    size = 2 * tall + ns
    copies = [
        pltpu.make_async_copy(source, target, sems.at[i])
        for i, (source, target) in enumerate(((h_hbm, h_ref), (f_hbm, f_ref), (q_hbm, noise)))
    ]
    for copy in copies:
        copy.start()
    center[...] = jnp.zeros_like(center)
    eye = unit(no)
    copies[0].wait()
    copies[1].wait()
    sensed_plain[...] = exact(h_ref[...], f_ref[...])
    copies[2].wait()

    def leaf(i, carry):
        first = jnp.logical_and(i == 1, chip == 0)
        own = (i == 1) == lead
        at = pl.multiple_of(i * size, 8)

        @pl.when(first)
        def _():
            copy = pltpu.make_async_copy(p_hbm, p_ref, sems.at[3])
            copy.start()
            copy.wait()
            noise[...] += exact(exact(f_ref[...], p_ref[...]), f_ref[...], NT)
            center[...] = exact(jnp.broadcast_to(m_ref[...], center.shape), f_ref[...], NT)

        @pl.when(jnp.logical_or(i == 0, first))
        def _():
            plain[...] = exact(h_ref[...], noise[...])
            inner_plain[...] = exact(plain[...], h_ref[...], NT)

        weight = lax.rsqrt(jnp.where(own, mine_ref[1:2, :], other_ref[1:2, :]))
        y = jnp.where(own, mine_ref[:1, :], other_ref[:1, :]) * weight
        y = jnp.broadcast_to(y, (8, no))
        weights = jnp.sum(eye * weight, axis=1, keepdims=True)
        gain = plain[...] * weights
        sensed = sensed_plain[...] * weights
        inner = inner_plain[...] * weights * weight
        active = jnp.where(first, 0.0, 1.0)
        mixed = inverse(inner, spectral_bound(inner, inner), half_pair)
        gained = exact(mixed, gain)
        joined = exact(mixed, sensed)
        gain_t = gain.T
        error = y - exact(center[...], h_ref[...], NT) * weight
        leaves[pl.ds(at, ns), :] = active * (f_ref[...] - exact(gain_t, joined))
        leaves[pl.ds(at + ns, ns), :] = noise[...] - exact(gain_t, gained)
        leaves[pl.ds(at + 2 * ns, 8), :] = center[...] + exact(error, gained)
        leaves[pl.ds(at + ns + tall, ns), :] = active * medium(sensed.T, joined)
        leaves[pl.ds(at + 2 * ns + tall, 8), :] = active * exact(y, joined)
        return carry

    lax.fori_loop(0, 2, leaf, 0)
    x_out[...] = leaves[size + ns : size + ns + tall, :]
    y_out[...] = leaves[ns + tall : size, :]


def pair_kernel(
    place_ref, solved, leaves, s_out, move_out, bind_out, y_out, spread_msg, through
):
    ns = solved.shape[1]
    tall = ns + 8
    size = 2 * tall + ns
    odd, even = leaves.at[:size, :], leaves.at[size:, :]
    lead = lax.rem(place_ref[0], 2) == 0
    x_ref = even.at[ns : ns + tall, :]
    y_ref = odd.at[ns + tall :, :]
    later = odd[:ns, :]
    early = even[:ns, :]
    fill(through, exact(later, solved[:ns, :]), y_ref[ns:, :])
    later_spread(through, x_ref, later, odd.at[ns : ns + tall, :], s_out)
    pack(spread_msg, s_out[:ns, :], s_out[ns:, :])
    move_out[...] = exact(through[:ns, :], early)
    fill(through, y_ref[:ns, :], solved[ns:, :])
    both = medium(medium(through[...], solved[:ns, :]), early)
    bind = medium(early.T, both[:ns, :]) + even[ns + tall : ns + tall + ns, :]
    pull = both[ns:, :] + even[2 * ns + tall :, :]
    pack(bind_out, bind, pull)
    scale = jnp.where(lead, 1.0, 0.0)
    fill(y_out, scale * bind, scale * pull)


def resolve_kernel(x_ref, y_ref, out, pair):
    resolve(x_ref, y_ref, out, pair)


def greet(mine, count, cases):
    barrier = pltpu.get_barrier_semaphore()
    expected = jnp.int32(0)
    for wanted, hop in cases:
        inside = jnp.logical_and(mine + hop >= 0, mine + hop < count)
        inside = jnp.logical_and(inside, wanted)
        expected = expected + inside.astype(jnp.int32)

        @pl.when(inside)
        def _(hop=hop):
            pl.semaphore_signal(
                barrier, inc=1, device_id=(mine + hop,), device_id_type=pl.DeviceIdType.MESH
            )


    def arrive():
        @pl.when(expected > 0)
        def _():
            pl.semaphore_wait(barrier, expected)

    return arrive


def shift_kernel(hop, count, message, s_ref, x_out, land, send_sem, recv_sem):
    mine = lax.axis_index("tm")
    lead = lax.rem(mine, 2) == 0
    side = jnp.logical_not(lead)
    arrive = greet(mine, count, [(lead, hop), (lead, -hop)])
    copy = pltpu.make_async_remote_copy(
        src_ref=message,
        dst_ref=land,
        send_sem=send_sem,
        recv_sem=recv_sem,
        device_id=(lax.rem(mine + hop, count),),
        device_id_type=pl.DeviceIdType.MESH,
    )
    sends = jnp.logical_and(lead, mine + hop < count)
    takes = jnp.logical_and(lead, mine - hop >= 0)
    arrive()
    pl.when(sends)(copy.start)

    @pl.when(side)
    def _():
        x_out[...] = s_ref[...]

    @pl.when(jnp.logical_and(lead, mine - hop < 0))
    def _():
        x_out[...] = jnp.zeros_like(x_out)

    @pl.when(takes)
    def _():
        copy.wait_recv()
        fill(x_out, *unpack(land))

    pl.when(sends)(copy.wait_send)


def exchange_kernel(
    hop, spread_hop, count, last,
    solved, x_ref, y_ref, s_ref, move_ref, bind_ref,
    x_out, y_out, s_out, move_out, bind_out,
    middle, through, spread_msg, bind_msg, move_land, pull_land, spread_land, bind_land,
    send_sems, recv_sems,
):
    ns = x_ref.shape[1]
    mine = lax.axis_index("tm")
    lead = lax.rem(mine, 2) == 0
    side = jnp.logical_not(lead)
    cases = [(lead, 1), (side, -1), (lead, spread_hop), (lead, -spread_hop)]
    if last:
        cases += [(side, hop), (side, -hop)]
    else:
        cases += [(True, hop), (True, -hop)]
    arrive = greet(mine, count, cases)

    def carry(source, land, send, recv, by):
        return pltpu.make_async_remote_copy(
            src_ref=source,
            dst_ref=land,
            send_sem=send_sems.at[send],
            recv_sem=recv_sems.at[recv],
            device_id=(lax.rem(mine + by + count, count),),
            device_id_type=pl.DeviceIdType.MESH,
        )

    def reaches(by):
        return jnp.logical_and(mine + by >= 0, mine + by < count)

    move_side = carry(move_ref, move_land, 0, 0, 1)
    pull_side = carry(bind_ref, pull_land, 1, 1, 1)
    spread_up = carry(spread_msg, spread_land, 2, 2, spread_hop)
    spread_side = carry(spread_msg, spread_land, 3, 2, 1)
    bind_down = carry(bind_msg, bind_land, 4, 3, -hop)
    move_sends = jnp.logical_and(lead, reaches(hop))
    spread_sends = jnp.logical_and(lead, reaches(spread_hop))
    bind_sends = jnp.logical_and(side, reaches(-hop))
    spread_takes = jnp.logical_or(side, reaches(-spread_hop))
    if last:
        move_takes = side
    else:
        move_up = carry(move_ref, move_land, 5, 0, hop)
        pull_up = carry(bind_ref, pull_land, 6, 1, hop)
        move_takes = jnp.logical_or(side, reaches(-hop))

    @pl.when(lead)
    def _():
        fill(through, exact(move_ref[...], solved[:ns, :]), y_ref[ns:, :])

    arrive()
    if not last:

        @pl.when(move_sends)
        def _():
            move_up.start()
            pull_up.start()

    @pl.when(lead)
    def _():
        move_side.start()
        pull_side.start()

    def mix():
        fill(middle, y_ref[:ns, :], solved[ns:, :])
        middle[...] = medium(middle[...], solved[:ns, :])

    if last:
        pl.when(side)(mix)
    else:
        mix()

    @pl.when(lead)
    def _():
        later_spread(through, x_ref, move_ref[...], s_ref, s_out)
        pack(spread_msg, s_out[:ns, :], s_out[ns:, :])

    pl.when(spread_sends)(spread_up.start)
    pl.when(lead)(spread_side.start)

    @pl.when(move_takes)
    def _():
        move_side.wait_recv()

    @pl.when(jnp.logical_not(move_takes))
    def _():
        move_land[...] = jnp.zeros_like(move_land)
        pull_land[...] = jnp.zeros_like(pull_land)

    def rest():
        early = move_land[...]
        both = medium(middle[...], early)
        bind = medium(early.T, both[:ns, :])

        @pl.when(move_takes)
        def _():
            pull_side.wait_recv()

        bind_i, pull_i = unpack(pull_land)
        fill(y_out, bind + bind_i, both[ns:, :] + pull_i)
        pack(bind_msg, y_out[:ns, :], y_out[ns:, :])

    if last:
        pl.when(side)(rest)
    else:
        rest()
    pl.when(bind_sends)(bind_down.start)
    if not last:

        @pl.when(lead)
        def _():
            move_out[...] = exact(through[:ns, :], move_land[...])
            bind_out[...] = bind_msg[...]

    @pl.when(spread_takes)
    def _():
        spread_side.wait_recv()
        fill(x_out, *unpack(spread_land))

    @pl.when(jnp.logical_not(spread_takes))
    def _():
        x_out[...] = jnp.zeros_like(x_out)

    @pl.when(jnp.logical_and(side, reaches(hop)))
    def _():
        bind_down.wait_recv()
        fill(y_out, *unpack(bind_land))

    @pl.when(jnp.logical_and(side, jnp.logical_not(reaches(hop))))
    def _():
        y_out[...] = y_ref[...]

    if not last:

        @pl.when(move_sends)
        def _():
            move_up.wait_send()
            pull_up.wait_send()

    @pl.when(lead)
    def _():
        move_side.wait_send()
        pull_side.wait_send()

    pl.when(spread_sends)(spread_up.wait_send)
    pl.when(lead)(spread_side.wait_send)
    pl.when(bind_sends)(bind_down.wait_send)


def choose_kernel(place_ref, x_ref, y_ref, leaves, left, right):
    ns = x_ref.shape[1]
    tall = ns + 8
    core = lax.rem(place_ref[0], 2)
    odd, even = leaves.at[: 2 * tall + ns, :], leaves.at[2 * tall + ns :, :]

    @pl.when(core == 0)
    def _():
        left[...] = x_ref[...]
        right[...] = even[ns + tall :, :]

    @pl.when(core != 0)
    def _():
        left[...] = odd[ns : ns + tall, :]
        right[...] = y_ref[...]


def finish_kernel(count, solved, x_ref, y_ref, leaves, s_out, y_out, middle, message, land, send_sem, recv_sem):
    ns = x_ref.shape[1]
    tall = ns + 8
    mine = lax.axis_index("tm")
    lead = lax.rem(mine, 2) == 0
    side = jnp.logical_not(lead)
    odd, even = leaves.at[: 2 * tall + ns, :], leaves.at[2 * tall + ns :, :]
    arrive = greet(mine, count, [(lead, 1), (side, -1)])
    copy = pltpu.make_async_remote_copy(
        src_ref=message,
        dst_ref=land,
        send_sem=send_sem,
        recv_sem=recv_sem,
        device_id=(lax.rem(mine - 1 + count, count),),
        device_id_type=pl.DeviceIdType.MESH,
    )

    @pl.when(lead)
    def _():
        move = even[:ns, :]
        fill(middle, exact(move, solved[:ns, :]), even[2 * ns + tall :, :])
        later_spread(middle, x_ref, move, even.at[ns : ns + tall, :], s_out)

    @pl.when(side)
    def _():
        move = odd[:ns, :]
        fill(middle, y_ref[:ns, :], solved[ns:, :])
        both = medium(medium(middle[...], solved[:ns, :]), move)
        bind = medium(move.T, both[:ns, :]) + odd[ns + tall : 2 * ns + tall, :]
        pack(message, bind, both[ns:, :] + odd[2 * ns + tall :, :])
        s_out[...] = x_ref[...]
        y_out[...] = y_ref[...]

    arrive()

    @pl.when(side)
    def _():
        copy.start()
        copy.wait_send()

    @pl.when(lead)
    def _():
        copy.wait_recv()
        fill(y_out, *unpack(land))


def last_kernel(solved, own_ref, later_ref, mean_ref, cov_ref):
    ns = own_ref.shape[1]
    mixed = solved[:ns, :]
    whole = own_ref[:ns, :]
    cov_ref[...] = exact(mixed, whole)
    mean_ref[...] = exact(own_ref[ns:, :] + exact(later_ref[ns:, :], whole), mixed, NT)[:1, :]


KERNEL_VMEM = 16 * 2**20
ALL_VMEM = 67 * 10**6
VMEM = pl.BlockSpec(memory_space=pltpu.VMEM)
HBM = pl.BlockSpec(memory_space=pltpu.MemorySpace.HBM)
SMEM = pl.BlockSpec(memory_space=pltpu.SMEM)


def call(kernel, args, rows, scratch, work, name, far=(), room=KERNEL_VMEM, **params):
    width = args[-1].shape[-1]
    read = sum(a.size for a in args) * 4
    return pl.pallas_call(
        kernel,
        out_shape=tuple(jax.ShapeDtypeStruct((r, width), F32) for r in rows),
        in_specs=[
            HBM if i in far else SMEM if a.ndim == 1 else VMEM for i, a in enumerate(args)
        ],
        out_specs=tuple(VMEM for _ in rows),
        scratch_shapes=scratch,
        cost_estimate=pl.CostEstimate(flops=work, bytes_accessed=read, transcendentals=0),
        compiler_params=pltpu.CompilerParams(vmem_limit_bytes=room, **params),
        name=name,
    )(*args)


def shards(measurements, noise_levels, transition, sensing, process_noise, prior_mean, prior_covariance):
    ns = transition.shape[0]
    no = sensing.shape[0]
    count = lax.axis_size("tm")
    device = lax.axis_index("tm").astype(jnp.int32)
    place = device.reshape(1)
    half = ns // 2 + 8
    tall = ns + 8
    work = 2 * ns**3 * 60

    def rows(r, columns=ns):
        return pltpu.VMEM((r, columns), F32)

    pair = rows(3 * ns)
    mine = jnp.concatenate([measurements, noise_levels], axis=0)
    other = lax.ppermute(mine, "tm", [(i, i ^ 1) for i in range(count)])
    def resolved(x, y):
        return call(resolve_kernel, (x, y), (tall,), [pair], work, "resolve")[0]

    leaves, x, y = call(
        start_kernel,
        (
            place,
            mine,
            other,
            transition,
            sensing,
            process_noise,
            prior_mean.reshape(1, ns),
            prior_covariance,
        ),
        (2 * (2 * tall + ns), tall, tall),
        [
            rows(ns),
            rows(no),
            rows(ns),
            rows(ns),
            rows(8),
            rows(no),
            rows(no),
            rows(no, no),
            rows(3 * no, no),
            pltpu.SemaphoreType.DMA((4,)),
        ],
        work,
        "start",
        far=(3, 4, 5, 7),
        room=ALL_VMEM,
    )
    s, moved, bound, y, message = call(
        pair_kernel,
        (place, resolved(x, y), leaves),
        (tall, ns, half, tall, half),
        [rows(tall)],
        work // 3,
        "pair",
    )
    (x,) = call(
        functools.partial(shift_kernel, 2, count),
        (message, s),
        (tall,),
        [rows(half), pltpu.SemaphoreType.DMA, pltpu.SemaphoreType.DMA],
        work // 60,
        "shift",
        collective_id=1,
        has_side_effects=True,
    )
    hop = 2
    while hop < count:
        last = hop * 2 >= count
        small = (8, 8) if last else (ns, half)
        spread_hop = 2 if last else 2 * hop
        solved = resolved(x, y)
        x, y, s, moved, bound = call(
            functools.partial(exchange_kernel, hop, spread_hop, count, last),
            (solved, x, y, s, moved, bound),
            (tall, tall, tall) + small,
            [
                rows(tall),
                rows(tall),
                rows(half),
                rows(half),
                rows(ns),
                rows(half),
                rows(half),
                rows(half),
                pltpu.SemaphoreType.DMA((7,)),
                pltpu.SemaphoreType.DMA((4,)),
            ],
            work,
            f"exchange_{hop}",
            collective_id=hop.bit_length(),
            has_side_effects=True,
        )
        hop *= 2
    left, right = call(choose_kernel, (place, x, y, leaves), (tall, tall), [], work // 60, "choose")
    solved = resolved(left, right)
    own, later = call(
        functools.partial(finish_kernel, count),
        (solved, x, y, leaves),
        (tall, tall),
        [rows(tall), rows(half), rows(half), pltpu.SemaphoreType.DMA, pltpu.SemaphoreType.DMA],
        work,
        "finish",
        collective_id=0,
        has_side_effects=True,
    )
    mean, cov = call(last_kernel, (resolved(own, later), own, later), (1, ns), [], work // 20, "last")
    return (mean, cov[None])


def solution(mesh):
    return jax.shard_map(
        shards,
        mesh=mesh,
        in_specs=(P("tm", None), P("tm", None), P(), P(), P(), P(), P()),
        out_specs=(P("tm", None), P("tm", None, None)),
        check_vma=False,
    )
```

```python
import functools

import jax
import jax.numpy as jnp
from jax import lax
from jax.experimental import pallas as pl
from jax.experimental.pallas import tpu as pltpu
from jax.sharding import PartitionSpec as P

F32 = jnp.float32
BF16 = jnp.bfloat16
NN = (((1,), (0,)), ((), ()))
NT = (((1,), (1,)), ((), ()))


def exact(left, right, dims=NN):
    return lax.dot_general(
        left, right, dims, precision=lax.Precision.HIGHEST, preferred_element_type=F32
    )


def rough(left, right, dims=NN):
    return lax.dot_general(
        left.astype(BF16), right.astype(BF16), dims, preferred_element_type=F32
    )


def unit(size):
    rows = lax.broadcasted_iota(jnp.int32, (size, size), 0)
    columns = lax.broadcasted_iota(jnp.int32, (size, size), 1)
    return (rows == columns).astype(F32)


def medium(left, right, dims=NN):
    left_high, right_high = left.astype(BF16), right.astype(BF16)
    left_low = (left - left_high.astype(F32)).astype(BF16)
    right_low = (right - right_high.astype(F32)).astype(BF16)

    def times(a, b):
        return lax.dot_general(a, b, dims, preferred_element_type=F32)

    return times(left_high, right_high) + (
        times(left_high, right_low) + times(left_low, right_high)
    )


def inverse(product, bound, pair):
    size = product.shape[0]
    eye = unit(size)
    whole = eye + product
    small = bound < 128.0

    def gain_of(low):
        return 4.0 / ((1.0 + low) * (1.0 + low))

    def more(state):
        return jnp.logical_not(state[1])

    @pl.when(small)
    def _():
        low = 1.0 / bound
        scaled = whole * low
        step = gain_of(low) * ((1.0 + low) * eye - scaled)
        pair[:size, :] = step * low
        pair[size : 2 * size, :] = rough(scaled, step)

        def turn(state):
            low, _ = state
            ends = low >= 0.95
            low = jnp.where(ends, 1.0, low)
            step = gain_of(low) * ((1.0 + low) * eye - pair[size : 2 * size, :])
            pair[: 2 * size, :] = rough(pair[: 2 * size, :], step)
            return low * gain_of(low), ends

        lax.while_loop(more, turn, (low * gain_of(low), jnp.bool_(False)))

    @pl.when(jnp.logical_not(small))
    def _():
        low = 1.0 / bound
        pair[:size, :] = eye * low
        pair[size : 2 * size, :] = whole * low

        def turn(state):
            low, _ = state
            ends = low >= 0.999
            low = jnp.where(ends, 1.0, low)
            pair[2 * size :, :] = gain_of(low) * (
                (1.0 + low) * eye - pair[size : 2 * size, :]
            )

            def block(i, carry):
                at = pl.ds(pl.multiple_of(i * 32, 32), 32)
                pair[at, :] = exact(pair[at, :], pair[2 * size :, :])
                return carry

            lax.fori_loop(0, 2 * size // 32, block, 0)
            return low * gain_of(low), ends

        lax.while_loop(more, turn, (low, jnp.bool_(False)))

    def correct(i, carry):
        guess = pair[:size, :]
        pair[:size, :] = guess + rough(guess, eye - medium(whole, guess))
        return carry

    lax.fori_loop(0, 2, correct, 0)
    return pair[:size, :]


def spectral_bound(product, mirrored):
    return 1.0 + 1.02 * jnp.sqrt(jnp.maximum(jnp.sum(product * mirrored), 0.0))


def pack(out, value, vector):
    ns = value.shape[0]
    n = ns // 2
    rows = lax.broadcasted_iota(jnp.int32, (n, n), 0)
    columns = lax.broadcasted_iota(jnp.int32, (n, n), 1)
    low, high = value[:n, :n], value[n:, n:]
    out[:n, :n] = value[n:, :n]
    out[:n, n:] = jnp.where(rows >= columns, low, high)
    out[n : n + 8, :] = jnp.zeros((8, ns), F32)
    out[n : n + 1, :] = vector[:1, :]
    out[n + 1 : n + 2, :n] = jnp.sum(
        jnp.where(rows == columns, high, 0.0), axis=0, keepdims=True
    )


def unpack(ref):
    ns = ref.shape[1]
    n = ns // 2
    rows = lax.broadcasted_iota(jnp.int32, (n, n), 0)
    columns = lax.broadcasted_iota(jnp.int32, (n, n), 1)
    corner = ref[:n, :n]
    mixed = ref[:n, n:]
    turned = mixed.T
    diagonal = jnp.broadcast_to(ref[n + 1 : n + 2, :n], (n, n))
    low = jnp.where(rows >= columns, mixed, turned)
    high = jnp.where(rows < columns, mixed, jnp.where(rows == columns, diagonal, turned))
    value = jnp.concatenate(
        [
            jnp.concatenate([low, corner.T], axis=1),
            jnp.concatenate([corner, high], axis=1),
        ],
        axis=0,
    )
    return value, spread_rows(ref, n)


def spread_rows(ref, at):
    return jnp.broadcast_to(ref[at : at + 1, :], (8, ref.shape[1]))


def fill(ref, value, vector):
    ns = value.shape[1]
    ref[:ns, :] = value
    ref[ns:, :] = vector


def resolve(x_ref, y_ref, out, pair):
    ns = x_ref.shape[1]
    value = y_ref[:ns, :]
    both = medium(x_ref[...], value)
    product = both[:ns, :]
    bound = spectral_bound(product, rough(value, x_ref[:ns, :]))
    out[:ns, :] = inverse(product, bound, pair)
    out[ns:, :] = y_ref[ns:, :] - both[ns:, :]


def later_spread(through, x_ref, move, s_ref, out):
    ns = x_ref.shape[1]
    carried = medium(through[...], x_ref[:ns, :])
    offset = exact(x_ref[ns:, :] + carried[ns:, :], through[:ns, :], NT)
    fill(out, medium(carried[:ns, :], move, NT) + s_ref[:ns, :], offset + s_ref[ns:, :])


def start_kernel(
    place_ref, mine_ref, other_ref, f_hbm, h_hbm, q_hbm, m_ref, p_hbm,
    leaves, solved,
    f_ref, h_ref, noise, p_ref, center, plain, sensed_plain, inner_plain, half_pair, pair, sems,
):
    chip, core = lax.div(place_ref[0], 2), lax.rem(place_ref[0], 2)
    lead = core == 0
    no, ns = h_ref.shape
    tall = ns + 8
    size = 2 * tall + ns
    copies = [
        pltpu.make_async_copy(source, target, sems.at[i])
        for i, (source, target) in enumerate(((h_hbm, h_ref), (f_hbm, f_ref), (q_hbm, noise)))
    ]
    for copy in copies:
        copy.start()
    center[...] = jnp.zeros_like(center)
    eye = unit(no)
    copies[0].wait()
    copies[1].wait()
    sensed_plain[...] = exact(h_ref[...], f_ref[...])
    copies[2].wait()

    def leaf(i, carry):
        first = jnp.logical_and(i == 1, chip == 0)
        own = (i == 1) == lead
        at = pl.multiple_of(i * size, 8)

        @pl.when(first)
        def _():
            copy = pltpu.make_async_copy(p_hbm, p_ref, sems.at[3])
            copy.start()
            copy.wait()
            noise[...] += exact(exact(f_ref[...], p_ref[...]), f_ref[...], NT)
            center[...] = exact(jnp.broadcast_to(m_ref[...], center.shape), f_ref[...], NT)

        @pl.when(jnp.logical_or(i == 0, first))
        def _():
            plain[...] = exact(h_ref[...], noise[...])
            inner_plain[...] = exact(plain[...], h_ref[...], NT)

        weight = lax.rsqrt(jnp.where(own, mine_ref[1:2, :], other_ref[1:2, :]))
        y = jnp.where(own, mine_ref[:1, :], other_ref[:1, :]) * weight
        y = jnp.broadcast_to(y, (8, no))
        weights = jnp.sum(eye * weight, axis=1, keepdims=True)
        gain = plain[...] * weights
        sensed = sensed_plain[...] * weights
        inner = inner_plain[...] * weights * weight
        active = jnp.where(first, 0.0, 1.0)
        mixed = inverse(inner, spectral_bound(inner, inner), half_pair)
        gained = exact(mixed, gain)
        joined = exact(mixed, sensed)
        gain_t = gain.T
        error = y - exact(center[...], h_ref[...], NT) * weight
        leaves[pl.ds(at, ns), :] = active * (f_ref[...] - exact(gain_t, joined))
        leaves[pl.ds(at + ns, ns), :] = noise[...] - exact(gain_t, gained)
        leaves[pl.ds(at + 2 * ns, 8), :] = center[...] + exact(error, gained)
        leaves[pl.ds(at + ns + tall, ns), :] = active * medium(sensed.T, joined)
        leaves[pl.ds(at + 2 * ns + tall, 8), :] = active * exact(y, joined)
        return carry

    lax.fori_loop(0, 2, leaf, 0)
    resolve(
        leaves.at[size + ns : size + ns + tall, :], leaves.at[ns + tall : size, :], solved, pair
    )


def resolve_kernel(x_ref, y_ref, out, pair):
    resolve(x_ref, y_ref, out, pair)


def greet(mine, count, cases):
    barrier = pltpu.get_barrier_semaphore()
    expected = jnp.int32(0)
    for wanted, hop in cases:
        inside = jnp.logical_and(mine + hop >= 0, mine + hop < count)
        inside = jnp.logical_and(inside, wanted)
        expected = expected + inside.astype(jnp.int32)

        @pl.when(inside)
        def _(hop=hop):
            pl.semaphore_signal(
                barrier, inc=1, device_id=(mine + hop,), device_id_type=pl.DeviceIdType.MESH
            )


    def arrive():
        @pl.when(expected > 0)
        def _():
            pl.semaphore_wait(barrier, expected)

    return arrive


def pair_kernel(
    hop, count,
    solved, leaves, x_out, y_out, s_out, move_out, bind_out,
    through, message, land, send_sem, recv_sem,
):
    ns = solved.shape[1]
    tall = ns + 8
    size = 2 * tall + ns
    mine = lax.axis_index("tm")
    lead = lax.rem(mine, 2) == 0
    side = jnp.logical_not(lead)
    arrive = greet(mine, count, [(lead, hop), (lead, -hop)])
    copy = pltpu.make_async_remote_copy(
        src_ref=message,
        dst_ref=land,
        send_sem=send_sem,
        recv_sem=recv_sem,
        device_id=(lax.rem(mine + hop, count),),
        device_id_type=pl.DeviceIdType.MESH,
    )
    sends = jnp.logical_and(lead, mine + hop < count)
    takes = jnp.logical_and(lead, mine - hop >= 0)
    odd, even = leaves.at[:size, :], leaves.at[size:, :]
    x_ref = even.at[ns : ns + tall, :]
    y_ref = odd.at[ns + tall :, :]
    later = odd[:ns, :]
    early = even[:ns, :]
    fill(through, exact(later, solved[:ns, :]), y_ref[ns:, :])
    later_spread(through, x_ref, later, odd.at[ns : ns + tall, :], s_out)
    pack(message, s_out[:ns, :], s_out[ns:, :])
    arrive()
    pl.when(sends)(copy.start)
    move_out[...] = exact(through[:ns, :], early)
    fill(through, y_ref[:ns, :], solved[ns:, :])
    both = medium(medium(through[...], solved[:ns, :]), early)
    bind = medium(early.T, both[:ns, :]) + even[ns + tall : ns + tall + ns, :]
    pull = both[ns:, :] + even[2 * ns + tall :, :]
    pack(bind_out, bind, pull)

    @pl.when(lead)
    def _():
        fill(y_out, bind, pull)

    @pl.when(side)
    def _():
        y_out[...] = jnp.zeros_like(y_out)
        x_out[...] = s_out[...]

    @pl.when(jnp.logical_and(lead, mine - hop < 0))
    def _():
        x_out[...] = jnp.zeros_like(x_out)

    @pl.when(takes)
    def _():
        copy.wait_recv()
        fill(x_out, *unpack(land))

    pl.when(sends)(copy.wait_send)


def exchange_kernel(
    hop, spread_hop, count, last,
    solved, x_ref, y_ref, s_ref, move_ref, bind_ref,
    x_out, y_out, s_out, move_out, bind_out,
    middle, through, spread_msg, bind_msg, move_land, pull_land, spread_land, bind_land,
    send_sems, recv_sems,
):
    ns = x_ref.shape[1]
    mine = lax.axis_index("tm")
    lead = lax.rem(mine, 2) == 0
    side = jnp.logical_not(lead)
    cases = [(lead, 1), (side, -1), (lead, spread_hop), (lead, -spread_hop)]
    if last:
        cases += [(side, hop), (side, -hop)]
    else:
        cases += [(True, hop), (True, -hop)]
    arrive = greet(mine, count, cases)

    def carry(source, land, send, recv, by):
        return pltpu.make_async_remote_copy(
            src_ref=source,
            dst_ref=land,
            send_sem=send_sems.at[send],
            recv_sem=recv_sems.at[recv],
            device_id=(lax.rem(mine + by + count, count),),
            device_id_type=pl.DeviceIdType.MESH,
        )

    def reaches(by):
        return jnp.logical_and(mine + by >= 0, mine + by < count)

    move_side = carry(move_ref, move_land, 0, 0, 1)
    pull_side = carry(bind_ref, pull_land, 1, 1, 1)
    spread_up = carry(spread_msg, spread_land, 2, 2, spread_hop)
    spread_side = carry(spread_msg, spread_land, 3, 2, 1)
    bind_down = carry(bind_msg, bind_land, 4, 3, -hop)
    move_sends = jnp.logical_and(lead, reaches(hop))
    spread_sends = jnp.logical_and(lead, reaches(spread_hop))
    bind_sends = jnp.logical_and(side, reaches(-hop))
    spread_takes = jnp.logical_or(side, reaches(-spread_hop))
    if last:
        move_takes = side
    else:
        move_up = carry(move_ref, move_land, 5, 0, hop)
        pull_up = carry(bind_ref, pull_land, 6, 1, hop)
        move_takes = jnp.logical_or(side, reaches(-hop))

    @pl.when(lead)
    def _():
        fill(through, exact(move_ref[...], solved[:ns, :]), y_ref[ns:, :])

    pl.when(lead)(arrive)
    if not last:

        @pl.when(move_sends)
        def _():
            move_up.start()
            pull_up.start()

    @pl.when(lead)
    def _():
        move_side.start()
        pull_side.start()

    def mix():
        fill(middle, y_ref[:ns, :], solved[ns:, :])
        middle[...] = medium(middle[...], solved[:ns, :])

    if last:
        pl.when(side)(mix)
    else:
        mix()

    @pl.when(lead)
    def _():
        later_spread(through, x_ref, move_ref[...], s_ref, s_out)
        pack(spread_msg, s_out[:ns, :], s_out[ns:, :])

    pl.when(spread_sends)(spread_up.start)
    pl.when(lead)(spread_side.start)

    @pl.when(move_takes)
    def _():
        move_side.wait_recv()

    @pl.when(jnp.logical_not(move_takes))
    def _():
        move_land[...] = jnp.zeros_like(move_land)
        pull_land[...] = jnp.zeros_like(pull_land)

    def rest():
        early = move_land[...]
        both = medium(middle[...], early)
        bind = medium(early.T, both[:ns, :])

        @pl.when(move_takes)
        def _():
            pull_side.wait_recv()

        bind_i, pull_i = unpack(pull_land)
        fill(y_out, bind + bind_i, both[ns:, :] + pull_i)
        pack(bind_msg, y_out[:ns, :], y_out[ns:, :])

    if last:
        pl.when(side)(rest)
    else:
        rest()
    pl.when(side)(arrive)
    pl.when(bind_sends)(bind_down.start)
    if not last:

        @pl.when(lead)
        def _():
            move_out[...] = exact(through[:ns, :], move_land[...])
            bind_out[...] = bind_msg[...]

    @pl.when(spread_takes)
    def _():
        spread_side.wait_recv()
        fill(x_out, *unpack(spread_land))

    @pl.when(jnp.logical_not(spread_takes))
    def _():
        x_out[...] = jnp.zeros_like(x_out)

    @pl.when(jnp.logical_and(side, reaches(hop)))
    def _():
        bind_down.wait_recv()
        fill(y_out, *unpack(bind_land))

    @pl.when(jnp.logical_and(side, jnp.logical_not(reaches(hop))))
    def _():
        y_out[...] = y_ref[...]

    if not last:

        @pl.when(move_sends)
        def _():
            move_up.wait_send()
            pull_up.wait_send()

    @pl.when(lead)
    def _():
        move_side.wait_send()
        pull_side.wait_send()

    pl.when(spread_sends)(spread_up.wait_send)
    pl.when(lead)(spread_side.wait_send)
    pl.when(bind_sends)(bind_down.wait_send)


def choose_kernel(place_ref, x_ref, y_ref, leaves, left, right):
    ns = x_ref.shape[1]
    tall = ns + 8
    core = lax.rem(place_ref[0], 2)
    odd, even = leaves.at[: 2 * tall + ns, :], leaves.at[2 * tall + ns :, :]

    @pl.when(core == 0)
    def _():
        left[...] = x_ref[...]
        right[...] = even[ns + tall :, :]

    @pl.when(core != 0)
    def _():
        left[...] = odd[ns : ns + tall, :]
        right[...] = y_ref[...]


def finish_kernel(count, solved, x_ref, y_ref, leaves, s_out, y_out, middle, message, land, send_sem, recv_sem):
    ns = x_ref.shape[1]
    tall = ns + 8
    mine = lax.axis_index("tm")
    lead = lax.rem(mine, 2) == 0
    side = jnp.logical_not(lead)
    odd, even = leaves.at[: 2 * tall + ns, :], leaves.at[2 * tall + ns :, :]
    arrive = greet(mine, count, [(lead, 1), (side, -1)])
    copy = pltpu.make_async_remote_copy(
        src_ref=message,
        dst_ref=land,
        send_sem=send_sem,
        recv_sem=recv_sem,
        device_id=(lax.rem(mine - 1 + count, count),),
        device_id_type=pl.DeviceIdType.MESH,
    )

    @pl.when(lead)
    def _():
        move = even[:ns, :]
        fill(middle, exact(move, solved[:ns, :]), even[2 * ns + tall :, :])
        later_spread(middle, x_ref, move, even.at[ns : ns + tall, :], s_out)

    @pl.when(side)
    def _():
        move = odd[:ns, :]
        fill(middle, y_ref[:ns, :], solved[ns:, :])
        both = medium(medium(middle[...], solved[:ns, :]), move)
        bind = medium(move.T, both[:ns, :]) + odd[ns + tall : 2 * ns + tall, :]
        pack(message, bind, both[ns:, :] + odd[2 * ns + tall :, :])
        s_out[...] = x_ref[...]
        y_out[...] = y_ref[...]

    arrive()

    @pl.when(side)
    def _():
        copy.start()
        copy.wait_send()

    @pl.when(lead)
    def _():
        copy.wait_recv()
        fill(y_out, *unpack(land))


def last_kernel(solved, own_ref, later_ref, mean_ref, cov_ref):
    ns = own_ref.shape[1]
    mixed = solved[:ns, :]
    whole = own_ref[:ns, :]
    cov_ref[...] = exact(mixed, whole)
    mean_ref[...] = exact(own_ref[ns:, :] + exact(later_ref[ns:, :], whole), mixed, NT)[:1, :]


KERNEL_VMEM = 16 * 2**20
ALL_VMEM = 67 * 10**6
VMEM = pl.BlockSpec(memory_space=pltpu.VMEM)
HBM = pl.BlockSpec(memory_space=pltpu.MemorySpace.HBM)
SMEM = pl.BlockSpec(memory_space=pltpu.SMEM)


def call(kernel, args, rows, scratch, work, name, far=(), room=KERNEL_VMEM, **params):
    width = args[-1].shape[-1]
    read = sum(a.size for a in args) * 4
    return pl.pallas_call(
        kernel,
        out_shape=tuple(jax.ShapeDtypeStruct((r, width), F32) for r in rows),
        in_specs=[
            HBM if i in far else SMEM if a.ndim == 1 else VMEM for i, a in enumerate(args)
        ],
        out_specs=tuple(VMEM for _ in rows),
        scratch_shapes=scratch,
        cost_estimate=pl.CostEstimate(flops=work, bytes_accessed=read, transcendentals=0),
        compiler_params=pltpu.CompilerParams(vmem_limit_bytes=room, **params),
        name=name,
    )(*args)


def shards(measurements, noise_levels, transition, sensing, process_noise, prior_mean, prior_covariance):
    ns = transition.shape[0]
    no = sensing.shape[0]
    count = lax.axis_size("tm")
    device = lax.axis_index("tm").astype(jnp.int32)
    place = device.reshape(1)
    half = ns // 2 + 8
    tall = ns + 8
    work = 2 * ns**3 * 60

    def rows(r, columns=ns):
        return pltpu.VMEM((r, columns), F32)

    pair = rows(3 * ns)
    mine = jnp.concatenate([measurements, noise_levels], axis=0)
    other = lax.ppermute(mine, "tm", [(i, i ^ 1) for i in range(count)])
    def resolved(x, y):
        return call(resolve_kernel, (x, y), (tall,), [pair], work, "resolve")[0]

    leaves, solved = call(
        start_kernel,
        (
            place,
            mine,
            other,
            transition,
            sensing,
            process_noise,
            prior_mean.reshape(1, ns),
            prior_covariance,
        ),
        (2 * (2 * tall + ns), tall),
        [
            rows(ns),
            rows(no),
            rows(ns),
            rows(ns),
            rows(8),
            rows(no),
            rows(no),
            rows(no, no),
            rows(3 * no, no),
            pair,
            pltpu.SemaphoreType.DMA((4,)),
        ],
        work,
        "start",
        far=(3, 4, 5, 7),
        room=ALL_VMEM,
    )
    x, y, s, moved, bound = call(
        functools.partial(pair_kernel, 2, count),
        (solved, leaves),
        (tall, tall, tall, ns, half),
        [rows(tall), rows(half), rows(half), pltpu.SemaphoreType.DMA, pltpu.SemaphoreType.DMA],
        work // 3,
        "pair",
        collective_id=1,
        has_side_effects=True,
    )
    hop = 2
    while hop < count:
        last = hop * 2 >= count
        small = (8, 8) if last else (ns, half)
        spread_hop = 2 if last else 2 * hop
        solved = resolved(x, y)
        x, y, s, moved, bound = call(
            functools.partial(exchange_kernel, hop, spread_hop, count, last),
            (solved, x, y, s, moved, bound),
            (tall, tall, tall) + small,
            [
                rows(tall),
                rows(tall),
                rows(half),
                rows(half),
                rows(ns),
                rows(half),
                rows(half),
                rows(half),
                pltpu.SemaphoreType.DMA((7,)),
                pltpu.SemaphoreType.DMA((4,)),
            ],
            work,
            f"exchange_{hop}",
            collective_id=hop.bit_length(),
            has_side_effects=True,
        )
        hop *= 2
    left, right = call(choose_kernel, (place, x, y, leaves), (tall, tall), [], work // 60, "choose")
    solved = resolved(left, right)
    own, later = call(
        functools.partial(finish_kernel, count),
        (solved, x, y, leaves),
        (tall, tall),
        [rows(tall), rows(half), rows(half), pltpu.SemaphoreType.DMA, pltpu.SemaphoreType.DMA],
        work,
        "finish",
        collective_id=0,
        has_side_effects=True,
    )
    mean, cov = call(last_kernel, (resolved(own, later), own, later), (1, ns), [], work // 20, "last")
    return (mean, cov[None])


def solution(mesh):
    return jax.shard_map(
        shards,
        mesh=mesh,
        in_specs=(P("tm", None), P("tm", None), P(), P(), P(), P(), P()),
        out_specs=(P("tm", None), P("tm", None, None)),
        check_vma=False,
    )
```

```python
import functools

import jax
import jax.numpy as jnp
from jax import lax
from jax.experimental import pallas as pl
from jax.experimental.pallas import tpu as pltpu
from jax.sharding import PartitionSpec as P

F32 = jnp.float32
BF16 = jnp.bfloat16
NN = (((1,), (0,)), ((), ()))
NT = (((1,), (1,)), ((), ()))


def exact(left, right, dims=NN):
    return lax.dot_general(
        left, right, dims, precision=lax.Precision.HIGHEST, preferred_element_type=F32
    )


def rough(left, right, dims=NN):
    return lax.dot_general(
        left.astype(BF16), right.astype(BF16), dims, preferred_element_type=F32
    )


def unit(size):
    rows = lax.broadcasted_iota(jnp.int32, (size, size), 0)
    columns = lax.broadcasted_iota(jnp.int32, (size, size), 1)
    return (rows == columns).astype(F32)


def medium(left, right, dims=NN):
    left_high, right_high = left.astype(BF16), right.astype(BF16)
    left_low = (left - left_high.astype(F32)).astype(BF16)
    right_low = (right - right_high.astype(F32)).astype(BF16)

    def times(a, b):
        return lax.dot_general(a, b, dims, preferred_element_type=F32)

    return times(left_high, right_high) + (
        times(left_high, right_low) + times(left_low, right_high)
    )


def inverse(product, bound, pair):
    size = product.shape[0]
    eye = unit(size)
    whole = eye + product
    small = bound < 128.0

    def gain_of(low):
        return 4.0 / ((1.0 + low) * (1.0 + low))

    def more(state):
        return jnp.logical_not(state[1])

    @pl.when(small)
    def _():
        low = 1.0 / bound
        scaled = whole * low
        step = gain_of(low) * ((1.0 + low) * eye - scaled)
        pair[:size, :] = step * low
        pair[size : 2 * size, :] = rough(scaled, step)

        def turn(state):
            low, _ = state
            ends = low >= 0.95
            low = jnp.where(ends, 1.0, low)
            step = gain_of(low) * ((1.0 + low) * eye - pair[size : 2 * size, :])
            pair[: 2 * size, :] = rough(pair[: 2 * size, :], step)
            return low * gain_of(low), ends

        lax.while_loop(more, turn, (low * gain_of(low), jnp.bool_(False)))

    @pl.when(jnp.logical_not(small))
    def _():
        low = 1.0 / bound
        pair[:size, :] = eye * low
        pair[size : 2 * size, :] = whole * low

        def turn(state):
            low, _ = state
            ends = low >= 0.999
            low = jnp.where(ends, 1.0, low)
            pair[2 * size :, :] = gain_of(low) * (
                (1.0 + low) * eye - pair[size : 2 * size, :]
            )

            def block(i, carry):
                at = pl.ds(pl.multiple_of(i * 32, 32), 32)
                pair[at, :] = exact(pair[at, :], pair[2 * size :, :])
                return carry

            lax.fori_loop(0, 2 * size // 32, block, 0)
            return low * gain_of(low), ends

        lax.while_loop(more, turn, (low, jnp.bool_(False)))

    def correct(i, carry):
        guess = pair[:size, :]
        pair[:size, :] = guess + rough(guess, eye - medium(whole, guess))
        return carry

    lax.fori_loop(0, 2, correct, 0)
    return pair[:size, :]


def spectral_bound(product, mirrored):
    return 1.0 + 1.02 * jnp.sqrt(jnp.maximum(jnp.sum(product * mirrored), 0.0))


def pack(out, value, vector):
    ns = value.shape[0]
    n = ns // 2
    rows = lax.broadcasted_iota(jnp.int32, (n, n), 0)
    columns = lax.broadcasted_iota(jnp.int32, (n, n), 1)
    low, high = value[:n, :n], value[n:, n:]
    out[:n, :n] = value[n:, :n]
    out[:n, n:] = jnp.where(rows >= columns, low, high)
    out[n : n + 8, :] = jnp.zeros((8, ns), F32)
    out[n : n + 1, :] = vector[:1, :]
    out[n + 1 : n + 2, :n] = jnp.sum(
        jnp.where(rows == columns, high, 0.0), axis=0, keepdims=True
    )


def unpack(ref):
    ns = ref.shape[1]
    n = ns // 2
    rows = lax.broadcasted_iota(jnp.int32, (n, n), 0)
    columns = lax.broadcasted_iota(jnp.int32, (n, n), 1)
    corner = ref[:n, :n]
    mixed = ref[:n, n:]
    turned = mixed.T
    diagonal = jnp.broadcast_to(ref[n + 1 : n + 2, :n], (n, n))
    low = jnp.where(rows >= columns, mixed, turned)
    high = jnp.where(rows < columns, mixed, jnp.where(rows == columns, diagonal, turned))
    value = jnp.concatenate(
        [
            jnp.concatenate([low, corner.T], axis=1),
            jnp.concatenate([corner, high], axis=1),
        ],
        axis=0,
    )
    return value, spread_rows(ref, n)


def spread_rows(ref, at):
    return jnp.broadcast_to(ref[at : at + 1, :], (8, ref.shape[1]))


def fill(ref, value, vector):
    ns = value.shape[1]
    ref[:ns, :] = value
    ref[ns:, :] = vector


def resolve(x_ref, y_ref, out, pair):
    ns = x_ref.shape[1]
    value = y_ref[:ns, :]
    both = medium(x_ref[...], value)
    product = both[:ns, :]
    bound = spectral_bound(product, rough(value, x_ref[:ns, :]))
    out[:ns, :] = inverse(product, bound, pair)
    out[ns:, :] = y_ref[ns:, :] - both[ns:, :]


def later_spread(through, x_ref, move, s_ref, out):
    ns = x_ref.shape[1]
    carried = medium(through[...], x_ref[:ns, :])
    offset = exact(x_ref[ns:, :] + carried[ns:, :], through[:ns, :], NT)
    fill(out, medium(carried[:ns, :], move, NT) + s_ref[:ns, :], offset + s_ref[ns:, :])


def start_kernel(
    place_ref, mine_ref, other_ref, f_hbm, h_hbm, q_hbm, m_ref, p_hbm,
    leaves,
    f_ref, h_ref, noise, p_ref, center, plain, sensed_plain, inner_plain, half_pair, pair, sems,
):
    chip, core = lax.div(place_ref[0], 2), lax.rem(place_ref[0], 2)
    lead = core == 0
    no, ns = h_ref.shape
    tall = ns + 8
    size = 2 * tall + ns
    copies = [
        pltpu.make_async_copy(source, target, sems.at[i])
        for i, (source, target) in enumerate(((h_hbm, h_ref), (f_hbm, f_ref), (q_hbm, noise)))
    ]
    for copy in copies:
        copy.start()
    center[...] = jnp.zeros_like(center)
    eye = unit(no)
    copies[0].wait()
    copies[1].wait()
    sensed_plain[...] = exact(h_ref[...], f_ref[...])
    copies[2].wait()

    def leaf(i, carry):
        first = jnp.logical_and(i == 1, chip == 0)
        own = (i == 1) == lead
        at = pl.multiple_of(i * size, 8)

        @pl.when(first)
        def _():
            copy = pltpu.make_async_copy(p_hbm, p_ref, sems.at[3])
            copy.start()
            copy.wait()
            noise[...] += exact(exact(f_ref[...], p_ref[...]), f_ref[...], NT)
            center[...] = exact(jnp.broadcast_to(m_ref[...], center.shape), f_ref[...], NT)

        @pl.when(jnp.logical_or(i == 0, first))
        def _():
            plain[...] = exact(h_ref[...], noise[...])
            inner_plain[...] = exact(plain[...], h_ref[...], NT)

        weight = lax.rsqrt(jnp.where(own, mine_ref[1:2, :], other_ref[1:2, :]))
        y = jnp.where(own, mine_ref[:1, :], other_ref[:1, :]) * weight
        y = jnp.broadcast_to(y, (8, no))
        weights = jnp.sum(eye * weight, axis=1, keepdims=True)
        gain = plain[...] * weights
        sensed = sensed_plain[...] * weights
        inner = inner_plain[...] * weights * weight
        active = jnp.where(first, 0.0, 1.0)
        mixed = inverse(inner, spectral_bound(inner, inner), half_pair)
        gained = exact(mixed, gain)
        joined = exact(mixed, sensed)
        gain_t = gain.T
        error = y - exact(center[...], h_ref[...], NT) * weight
        leaves[pl.ds(at, ns), :] = active * (f_ref[...] - exact(gain_t, joined))
        leaves[pl.ds(at + ns, ns), :] = noise[...] - exact(gain_t, gained)
        leaves[pl.ds(at + 2 * ns, 8), :] = center[...] + exact(error, gained)
        leaves[pl.ds(at + ns + tall, ns), :] = active * medium(sensed.T, joined)
        leaves[pl.ds(at + 2 * ns + tall, 8), :] = active * exact(y, joined)
        return carry

    lax.fori_loop(0, 2, leaf, 0)
    resolve(
        leaves.at[size + ns : size + ns + tall, :],
        leaves.at[ns + tall : size, :],
        leaves.at[2 * size :, :],
        pair,
    )


def resolve_kernel(x_ref, y_ref, out, pair):
    resolve(x_ref, y_ref, out, pair)


def greet(mine, count, cases):
    barrier = pltpu.get_barrier_semaphore()
    expected = jnp.int32(0)
    for wanted, hop in cases:
        inside = jnp.logical_and(mine + hop >= 0, mine + hop < count)
        inside = jnp.logical_and(inside, wanted)
        expected = expected + inside.astype(jnp.int32)

        @pl.when(inside)
        def _(hop=hop):
            pl.semaphore_signal(
                barrier, inc=1, device_id=(mine + hop,), device_id_type=pl.DeviceIdType.MESH
            )


    def arrive():
        @pl.when(expected > 0)
        def _():
            pl.semaphore_wait(barrier, expected)

    return arrive


def pair_kernel(
    hop, count,
    leaves, x_out, y_out, s_out, move_out, bind_out,
    through, message, land, send_sem, recv_sem,
):
    ns = leaves.shape[1]
    tall = ns + 8
    size = 2 * tall + ns
    mine = lax.axis_index("tm")
    lead = lax.rem(mine, 2) == 0
    side = jnp.logical_not(lead)
    arrive = greet(mine, count, [(lead, hop), (lead, -hop)])
    copy = pltpu.make_async_remote_copy(
        src_ref=message,
        dst_ref=land,
        send_sem=send_sem,
        recv_sem=recv_sem,
        device_id=(lax.rem(mine + hop, count),),
        device_id_type=pl.DeviceIdType.MESH,
    )
    sends = jnp.logical_and(lead, mine + hop < count)
    takes = jnp.logical_and(lead, mine - hop >= 0)
    odd, even = leaves.at[:size, :], leaves.at[size : 2 * size, :]
    solved = leaves.at[2 * size :, :]
    x_ref = even.at[ns : ns + tall, :]
    y_ref = odd.at[ns + tall :, :]
    later = odd[:ns, :]
    early = even[:ns, :]
    fill(through, exact(later, solved[:ns, :]), y_ref[ns:, :])
    later_spread(through, x_ref, later, odd.at[ns : ns + tall, :], s_out)
    pack(message, s_out[:ns, :], s_out[ns:, :])
    arrive()
    pl.when(sends)(copy.start)
    move_out[...] = exact(through[:ns, :], early)
    fill(through, y_ref[:ns, :], solved[ns:, :])
    both = medium(medium(through[...], solved[:ns, :]), early)
    bind = medium(early.T, both[:ns, :]) + even[ns + tall : ns + tall + ns, :]
    pull = both[ns:, :] + even[2 * ns + tall :, :]
    pack(bind_out, bind, pull)

    @pl.when(lead)
    def _():
        fill(y_out, bind, pull)

    @pl.when(side)
    def _():
        y_out[...] = jnp.zeros_like(y_out)
        x_out[...] = s_out[...]

    @pl.when(jnp.logical_and(lead, mine - hop < 0))
    def _():
        x_out[...] = jnp.zeros_like(x_out)

    @pl.when(takes)
    def _():
        copy.wait_recv()
        fill(x_out, *unpack(land))

    pl.when(sends)(copy.wait_send)


def exchange_kernel(
    hop, spread_hop, count, last,
    solved, x_ref, y_ref, s_ref, move_ref, bind_ref,
    x_out, y_out, s_out, move_out, bind_out,
    middle, through, spread_msg, bind_msg, move_land, pull_land, spread_land, bind_land,
    send_sems, recv_sems,
):
    ns = x_ref.shape[1]
    mine = lax.axis_index("tm")
    lead = lax.rem(mine, 2) == 0
    side = jnp.logical_not(lead)
    cases = [(lead, 1), (side, -1), (lead, spread_hop), (lead, -spread_hop)]
    if last:
        cases += [(side, hop), (side, -hop)]
    else:
        cases += [(True, hop), (True, -hop)]
    arrive = greet(mine, count, cases)

    def carry(source, land, send, recv, by):
        return pltpu.make_async_remote_copy(
            src_ref=source,
            dst_ref=land,
            send_sem=send_sems.at[send],
            recv_sem=recv_sems.at[recv],
            device_id=(lax.rem(mine + by + count, count),),
            device_id_type=pl.DeviceIdType.MESH,
        )

    def reaches(by):
        return jnp.logical_and(mine + by >= 0, mine + by < count)

    move_side = carry(move_ref, move_land, 0, 0, 1)
    pull_side = carry(bind_ref, pull_land, 1, 1, 1)
    spread_up = carry(spread_msg, spread_land, 2, 2, spread_hop)
    spread_side = carry(spread_msg, spread_land, 3, 2, 1)
    bind_down = carry(bind_msg, bind_land, 4, 3, -hop)
    move_sends = jnp.logical_and(lead, reaches(hop))
    spread_sends = jnp.logical_and(lead, reaches(spread_hop))
    bind_sends = jnp.logical_and(side, reaches(-hop))
    spread_takes = jnp.logical_or(side, reaches(-spread_hop))
    if last:
        move_takes = side
    else:
        move_up = carry(move_ref, move_land, 5, 0, hop)
        pull_up = carry(bind_ref, pull_land, 6, 1, hop)
        move_takes = jnp.logical_or(side, reaches(-hop))

    pl.when(lead)(arrive)
    if not last:

        @pl.when(move_sends)
        def _():
            move_up.start()
            pull_up.start()

    @pl.when(lead)
    def _():
        move_side.start()
        pull_side.start()
        fill(through, exact(move_ref[...], solved[:ns, :]), y_ref[ns:, :])

    def mix():
        fill(middle, y_ref[:ns, :], solved[ns:, :])
        middle[...] = medium(middle[...], solved[:ns, :])

    if last:
        pl.when(side)(mix)
    else:
        mix()

    @pl.when(lead)
    def _():
        later_spread(through, x_ref, move_ref[...], s_ref, s_out)
        pack(spread_msg, s_out[:ns, :], s_out[ns:, :])

    pl.when(spread_sends)(spread_up.start)
    pl.when(lead)(spread_side.start)

    @pl.when(move_takes)
    def _():
        move_side.wait_recv()

    @pl.when(jnp.logical_not(move_takes))
    def _():
        move_land[...] = jnp.zeros_like(move_land)
        pull_land[...] = jnp.zeros_like(pull_land)

    def rest():
        early = move_land[...]
        both = medium(middle[...], early)
        bind = medium(early.T, both[:ns, :])

        @pl.when(move_takes)
        def _():
            pull_side.wait_recv()

        bind_i, pull_i = unpack(pull_land)
        fill(y_out, bind + bind_i, both[ns:, :] + pull_i)
        pack(bind_msg, y_out[:ns, :], y_out[ns:, :])

    if last:
        pl.when(side)(rest)
    else:
        rest()
    pl.when(side)(arrive)
    pl.when(bind_sends)(bind_down.start)
    if not last:

        @pl.when(lead)
        def _():
            move_out[...] = exact(through[:ns, :], move_land[...])
            bind_out[...] = bind_msg[...]

    @pl.when(spread_takes)
    def _():
        spread_side.wait_recv()
        fill(x_out, *unpack(spread_land))

    @pl.when(jnp.logical_not(spread_takes))
    def _():
        x_out[...] = jnp.zeros_like(x_out)

    @pl.when(jnp.logical_and(side, reaches(hop)))
    def _():
        bind_down.wait_recv()
        fill(y_out, *unpack(bind_land))

    @pl.when(jnp.logical_and(side, jnp.logical_not(reaches(hop))))
    def _():
        y_out[...] = y_ref[...]

    if not last:

        @pl.when(move_sends)
        def _():
            move_up.wait_send()
            pull_up.wait_send()

    @pl.when(lead)
    def _():
        move_side.wait_send()
        pull_side.wait_send()

    pl.when(spread_sends)(spread_up.wait_send)
    pl.when(lead)(spread_side.wait_send)
    pl.when(bind_sends)(bind_down.wait_send)


def choose_kernel(place_ref, x_ref, y_ref, leaves, left, right):
    ns = x_ref.shape[1]
    tall = ns + 8
    core = lax.rem(place_ref[0], 2)
    odd, even = leaves.at[: 2 * tall + ns, :], leaves.at[2 * tall + ns : 4 * tall + 2 * ns, :]

    @pl.when(core == 0)
    def _():
        left[...] = x_ref[...]
        right[...] = even[ns + tall :, :]

    @pl.when(core != 0)
    def _():
        left[...] = odd[ns : ns + tall, :]
        right[...] = y_ref[...]


def finish_kernel(count, solved, x_ref, y_ref, leaves, s_out, y_out, middle, message, land, send_sem, recv_sem):
    ns = x_ref.shape[1]
    tall = ns + 8
    mine = lax.axis_index("tm")
    lead = lax.rem(mine, 2) == 0
    side = jnp.logical_not(lead)
    odd, even = leaves.at[: 2 * tall + ns, :], leaves.at[2 * tall + ns : 4 * tall + 2 * ns, :]
    arrive = greet(mine, count, [(lead, 1), (side, -1)])
    copy = pltpu.make_async_remote_copy(
        src_ref=message,
        dst_ref=land,
        send_sem=send_sem,
        recv_sem=recv_sem,
        device_id=(lax.rem(mine - 1 + count, count),),
        device_id_type=pl.DeviceIdType.MESH,
    )

    @pl.when(lead)
    def _():
        move = even[:ns, :]
        fill(middle, exact(move, solved[:ns, :]), even[2 * ns + tall :, :])
        later_spread(middle, x_ref, move, even.at[ns : ns + tall, :], s_out)

    @pl.when(side)
    def _():
        move = odd[:ns, :]
        fill(middle, y_ref[:ns, :], solved[ns:, :])
        both = medium(medium(middle[...], solved[:ns, :]), move)
        bind = medium(move.T, both[:ns, :]) + odd[ns + tall : 2 * ns + tall, :]
        pack(message, bind, both[ns:, :] + odd[2 * ns + tall :, :])
        s_out[...] = x_ref[...]
        y_out[...] = y_ref[...]

    arrive()

    @pl.when(side)
    def _():
        copy.start()
        copy.wait_send()

    @pl.when(lead)
    def _():
        copy.wait_recv()
        fill(y_out, *unpack(land))


def last_kernel(solved, own_ref, later_ref, mean_ref, cov_ref):
    ns = own_ref.shape[1]
    mixed = solved[:ns, :]
    whole = own_ref[:ns, :]
    cov_ref[...] = exact(mixed, whole)
    mean_ref[...] = exact(own_ref[ns:, :] + exact(later_ref[ns:, :], whole), mixed, NT)[:1, :]


KERNEL_VMEM = 16 * 2**20
ALL_VMEM = 67 * 10**6
VMEM = pl.BlockSpec(memory_space=pltpu.VMEM)
HBM = pl.BlockSpec(memory_space=pltpu.MemorySpace.HBM)
SMEM = pl.BlockSpec(memory_space=pltpu.SMEM)


def call(kernel, args, rows, scratch, work, name, far=(), room=KERNEL_VMEM, **params):
    width = args[-1].shape[-1]
    read = sum(a.size for a in args) * 4
    return pl.pallas_call(
        kernel,
        out_shape=tuple(jax.ShapeDtypeStruct((r, width), F32) for r in rows),
        in_specs=[
            HBM if i in far else SMEM if a.ndim == 1 else VMEM for i, a in enumerate(args)
        ],
        out_specs=tuple(VMEM for _ in rows),
        scratch_shapes=scratch,
        cost_estimate=pl.CostEstimate(flops=work, bytes_accessed=read, transcendentals=0),
        compiler_params=pltpu.CompilerParams(vmem_limit_bytes=room, **params),
        name=name,
    )(*args)


def shards(measurements, noise_levels, transition, sensing, process_noise, prior_mean, prior_covariance):
    ns = transition.shape[0]
    no = sensing.shape[0]
    count = lax.axis_size("tm")
    device = lax.axis_index("tm").astype(jnp.int32)
    place = device.reshape(1)
    half = ns // 2 + 8
    tall = ns + 8
    work = 2 * ns**3 * 60

    def rows(r, columns=ns):
        return pltpu.VMEM((r, columns), F32)

    pair = rows(3 * ns)
    mine = jnp.concatenate([measurements, noise_levels], axis=0)
    other = lax.ppermute(mine, "tm", [(i, i ^ 1) for i in range(count)])
    def resolved(x, y):
        return call(resolve_kernel, (x, y), (tall,), [pair], work, "resolve")[0]

    (leaves,) = call(
        start_kernel,
        (
            place,
            mine,
            other,
            transition,
            sensing,
            process_noise,
            prior_mean.reshape(1, ns),
            prior_covariance,
        ),
        (5 * tall + 2 * ns,),
        [
            rows(ns),
            rows(no),
            rows(ns),
            rows(ns),
            rows(8),
            rows(no),
            rows(no),
            rows(no, no),
            rows(3 * no, no),
            pair,
            pltpu.SemaphoreType.DMA((4,)),
        ],
        work,
        "start",
        far=(3, 4, 5, 7),
        room=ALL_VMEM,
    )
    x, y, s, moved, bound = call(
        functools.partial(pair_kernel, 2, count),
        (leaves,),
        (tall, tall, tall, ns, half),
        [rows(tall), rows(half), rows(half), pltpu.SemaphoreType.DMA, pltpu.SemaphoreType.DMA],
        work // 3,
        "pair",
        collective_id=1,
        has_side_effects=True,
    )
    hop = 2
    while hop < count:
        last = hop * 2 >= count
        small = (8, 8) if last else (ns, half)
        spread_hop = 2 if last else 2 * hop
        solved = resolved(x, y)
        x, y, s, moved, bound = call(
            functools.partial(exchange_kernel, hop, spread_hop, count, last),
            (solved, x, y, s, moved, bound),
            (tall, tall, tall) + small,
            [
                rows(tall),
                rows(tall),
                rows(half),
                rows(half),
                rows(ns),
                rows(half),
                rows(half),
                rows(half),
                pltpu.SemaphoreType.DMA((7,)),
                pltpu.SemaphoreType.DMA((4,)),
            ],
            work,
            f"exchange_{hop}",
            collective_id=hop.bit_length(),
            has_side_effects=True,
        )
        hop *= 2
    left, right = call(choose_kernel, (place, x, y, leaves), (tall, tall), [], work // 60, "choose")
    solved = resolved(left, right)
    own, later = call(
        functools.partial(finish_kernel, count),
        (solved, x, y, leaves),
        (tall, tall),
        [rows(tall), rows(half), rows(half), pltpu.SemaphoreType.DMA, pltpu.SemaphoreType.DMA],
        work,
        "finish",
        collective_id=0,
        has_side_effects=True,
    )
    mean, cov = call(last_kernel, (resolved(own, later), own, later), (1, ns), [], work // 20, "last")
    return (mean, cov[None])


def solution(mesh):
    return jax.shard_map(
        shards,
        mesh=mesh,
        in_specs=(P("tm", None), P("tm", None), P(), P(), P(), P(), P()),
        out_specs=(P("tm", None), P("tm", None, None)),
        check_vma=False,
    )
```

```python
import functools

import jax
import jax.numpy as jnp
from jax import lax
from jax.experimental import pallas as pl
from jax.experimental.pallas import tpu as pltpu
from jax.sharding import PartitionSpec as P

F32 = jnp.float32
BF16 = jnp.bfloat16
NN = (((1,), (0,)), ((), ()))
NT = (((1,), (1,)), ((), ()))


def exact(left, right, dims=NN):
    return lax.dot_general(
        left, right, dims, precision=lax.Precision.HIGHEST, preferred_element_type=F32
    )


def rough(left, right, dims=NN):
    return lax.dot_general(
        left.astype(BF16), right.astype(BF16), dims, preferred_element_type=F32
    )


def unit(size):
    rows = lax.broadcasted_iota(jnp.int32, (size, size), 0)
    columns = lax.broadcasted_iota(jnp.int32, (size, size), 1)
    return (rows == columns).astype(F32)


def medium(left, right, dims=NN):
    left_high, right_high = left.astype(BF16), right.astype(BF16)
    left_low = (left - left_high.astype(F32)).astype(BF16)
    right_low = (right - right_high.astype(F32)).astype(BF16)

    def times(a, b):
        return lax.dot_general(a, b, dims, preferred_element_type=F32)

    return times(left_high, right_high) + (
        times(left_high, right_low) + times(left_low, right_high)
    )


def inverse(product, bound, pair):
    size = product.shape[0]
    eye = unit(size)
    whole = eye + product
    small = bound < 128.0

    def gain_of(low):
        return 4.0 / ((1.0 + low) * (1.0 + low))

    def more(state):
        return jnp.logical_not(state[1])

    @pl.when(small)
    def _():
        low = 1.0 / bound
        scaled = whole * low
        step = gain_of(low) * ((1.0 + low) * eye - scaled)
        pair[:size, :] = step * low
        pair[size : 2 * size, :] = rough(scaled, step)

        def turn(state):
            low, _ = state
            ends = low >= 0.95
            low = jnp.where(ends, 1.0, low)
            step = gain_of(low) * ((1.0 + low) * eye - pair[size : 2 * size, :])
            pair[: 2 * size, :] = rough(pair[: 2 * size, :], step)
            return low * gain_of(low), ends

        lax.while_loop(more, turn, (low * gain_of(low), jnp.bool_(False)))

    @pl.when(jnp.logical_not(small))
    def _():
        low = 1.0 / bound
        pair[:size, :] = eye * low
        pair[size : 2 * size, :] = whole * low

        def turn(state):
            low, _ = state
            ends = low >= 0.999
            low = jnp.where(ends, 1.0, low)
            pair[2 * size :, :] = gain_of(low) * (
                (1.0 + low) * eye - pair[size : 2 * size, :]
            )

            def block(i, carry):
                at = pl.ds(pl.multiple_of(i * 32, 32), 32)
                pair[at, :] = exact(pair[at, :], pair[2 * size :, :])
                return carry

            lax.fori_loop(0, 2 * size // 32, block, 0)
            return low * gain_of(low), ends

        lax.while_loop(more, turn, (low, jnp.bool_(False)))

    def correct(i, carry):
        guess = pair[:size, :]
        pair[:size, :] = guess + rough(guess, eye - medium(whole, guess))
        return carry

    lax.fori_loop(0, 2, correct, 0)
    return pair[:size, :]


def spectral_bound(product, mirrored):
    return 1.0 + 1.02 * jnp.sqrt(jnp.maximum(jnp.sum(product * mirrored), 0.0))


def pack(out, value, vector):
    ns = value.shape[0]
    n = ns // 2
    rows = lax.broadcasted_iota(jnp.int32, (n, n), 0)
    columns = lax.broadcasted_iota(jnp.int32, (n, n), 1)
    low, high = value[:n, :n], value[n:, n:]
    out[:n, :n] = value[n:, :n]
    out[:n, n:] = jnp.where(rows >= columns, low, high)
    out[n : n + 8, :] = jnp.zeros((8, ns), F32)
    out[n : n + 1, :] = vector[:1, :]
    out[n + 1 : n + 2, :n] = jnp.sum(
        jnp.where(rows == columns, high, 0.0), axis=0, keepdims=True
    )


def unpack(ref):
    ns = ref.shape[1]
    n = ns // 2
    rows = lax.broadcasted_iota(jnp.int32, (n, n), 0)
    columns = lax.broadcasted_iota(jnp.int32, (n, n), 1)
    corner = ref[:n, :n]
    mixed = ref[:n, n:]
    turned = mixed.T
    diagonal = jnp.broadcast_to(ref[n + 1 : n + 2, :n], (n, n))
    low = jnp.where(rows >= columns, mixed, turned)
    high = jnp.where(rows < columns, mixed, jnp.where(rows == columns, diagonal, turned))
    value = jnp.concatenate(
        [
            jnp.concatenate([low, corner.T], axis=1),
            jnp.concatenate([corner, high], axis=1),
        ],
        axis=0,
    )
    return value, spread_rows(ref, n)


def spread_rows(ref, at):
    return jnp.broadcast_to(ref[at : at + 1, :], (8, ref.shape[1]))


def fill(ref, value, vector):
    ns = value.shape[1]
    ref[:ns, :] = value
    ref[ns:, :] = vector


def resolve(x_ref, y_ref, out, pair):
    ns = x_ref.shape[1]
    value = y_ref[:ns, :]
    both = medium(x_ref[...], value)
    product = both[:ns, :]
    bound = spectral_bound(product, rough(value, x_ref[:ns, :]))
    out[:ns, :] = inverse(product, bound, pair)
    out[ns:, :] = y_ref[ns:, :] - both[ns:, :]


def later_spread(through, x_ref, move, s_ref, out):
    ns = x_ref.shape[1]
    carried = medium(through[...], x_ref[:ns, :])
    offset = exact(x_ref[ns:, :] + carried[ns:, :], through[:ns, :], NT)
    fill(out, medium(carried[:ns, :], move, NT) + s_ref[:ns, :], offset + s_ref[ns:, :])


def start_kernel(
    place_ref, mine_ref, other_ref, f_hbm, h_hbm, q_hbm, m_ref, p_hbm,
    leaves,
    f_ref, h_ref, noise, p_ref, center, plain, sensed_plain, inner_plain, half_pair, pair, sems,
):
    chip, core = lax.div(place_ref[0], 2), lax.rem(place_ref[0], 2)
    lead = core == 0
    no, ns = h_ref.shape
    tall = ns + 8
    size = 2 * tall + ns
    copies = [
        pltpu.make_async_copy(source, target, sems.at[i])
        for i, (source, target) in enumerate(((h_hbm, h_ref), (f_hbm, f_ref), (q_hbm, noise)))
    ]
    for copy in copies:
        copy.start()
    center[...] = jnp.zeros_like(center)
    eye = unit(no)
    copies[0].wait()
    copies[1].wait()
    sensed_plain[...] = exact(h_ref[...], f_ref[...])
    copies[2].wait()

    def leaf(i, carry):
        first = jnp.logical_and(i == 1, chip == 0)
        own = (i == 1) == lead
        at = pl.multiple_of(i * size, 8)

        @pl.when(first)
        def _():
            copy = pltpu.make_async_copy(p_hbm, p_ref, sems.at[3])
            copy.start()
            copy.wait()
            noise[...] += exact(exact(f_ref[...], p_ref[...]), f_ref[...], NT)
            center[...] = exact(jnp.broadcast_to(m_ref[...], center.shape), f_ref[...], NT)

        @pl.when(jnp.logical_or(i == 0, first))
        def _():
            plain[...] = exact(h_ref[...], noise[...])
            inner_plain[...] = exact(plain[...], h_ref[...], NT)

        weight = lax.rsqrt(jnp.where(own, mine_ref[1:2, :], other_ref[1:2, :]))
        y = jnp.where(own, mine_ref[:1, :], other_ref[:1, :]) * weight
        y = jnp.broadcast_to(y, (8, no))
        weights = jnp.sum(eye * weight, axis=1, keepdims=True)
        gain = plain[...] * weights
        sensed = sensed_plain[...] * weights
        inner = inner_plain[...] * weights * weight
        active = jnp.where(first, 0.0, 1.0)
        mixed = inverse(inner, spectral_bound(inner, inner), half_pair)
        gained = medium(mixed, gain)
        joined = exact(mixed, sensed)
        gain_t = gain.T
        error = y - exact(center[...], h_ref[...], NT) * weight
        leaves[pl.ds(at, ns), :] = active * (f_ref[...] - exact(gain_t, joined))
        leaves[pl.ds(at + ns, ns), :] = noise[...] - medium(gain_t, gained)
        leaves[pl.ds(at + 2 * ns, 8), :] = center[...] + exact(error, gained)
        leaves[pl.ds(at + ns + tall, ns), :] = active * medium(sensed.T, joined)
        leaves[pl.ds(at + 2 * ns + tall, 8), :] = active * exact(y, joined)
        return carry

    lax.fori_loop(0, 2, leaf, 0)
    resolve(
        leaves.at[size + ns : size + ns + tall, :],
        leaves.at[ns + tall : size, :],
        leaves.at[2 * size :, :],
        pair,
    )


def resolve_kernel(x_ref, y_ref, out, pair):
    resolve(x_ref, y_ref, out, pair)


def greet(mine, count, cases):
    barrier = pltpu.get_barrier_semaphore()
    expected = jnp.int32(0)
    for wanted, hop in cases:
        inside = jnp.logical_and(mine + hop >= 0, mine + hop < count)
        inside = jnp.logical_and(inside, wanted)
        expected = expected + inside.astype(jnp.int32)

        @pl.when(inside)
        def _(hop=hop):
            pl.semaphore_signal(
                barrier, inc=1, device_id=(mine + hop,), device_id_type=pl.DeviceIdType.MESH
            )


    def arrive():
        @pl.when(expected > 0)
        def _():
            pl.semaphore_wait(barrier, expected)

    return arrive


def pair_kernel(
    hop, count,
    leaves, x_out, y_out, s_out, move_out, bind_out,
    through, message, land, send_sem, recv_sem,
):
    ns = leaves.shape[1]
    tall = ns + 8
    size = 2 * tall + ns
    mine = lax.axis_index("tm")
    lead = lax.rem(mine, 2) == 0
    side = jnp.logical_not(lead)
    arrive = greet(mine, count, [(lead, hop), (lead, -hop)])
    copy = pltpu.make_async_remote_copy(
        src_ref=message,
        dst_ref=land,
        send_sem=send_sem,
        recv_sem=recv_sem,
        device_id=(lax.rem(mine + hop, count),),
        device_id_type=pl.DeviceIdType.MESH,
    )
    sends = jnp.logical_and(lead, mine + hop < count)
    takes = jnp.logical_and(lead, mine - hop >= 0)
    odd, even = leaves.at[:size, :], leaves.at[size : 2 * size, :]
    solved = leaves.at[2 * size :, :]
    x_ref = even.at[ns : ns + tall, :]
    y_ref = odd.at[ns + tall :, :]
    later = odd[:ns, :]
    early = even[:ns, :]
    fill(through, exact(later, solved[:ns, :]), y_ref[ns:, :])
    later_spread(through, x_ref, later, odd.at[ns : ns + tall, :], s_out)
    pack(message, s_out[:ns, :], s_out[ns:, :])
    arrive()
    pl.when(sends)(copy.start)
    move_out[...] = exact(through[:ns, :], early)
    fill(through, y_ref[:ns, :], solved[ns:, :])
    both = medium(medium(through[...], solved[:ns, :]), early)
    bind = medium(early.T, both[:ns, :]) + even[ns + tall : ns + tall + ns, :]
    pull = both[ns:, :] + even[2 * ns + tall :, :]
    pack(bind_out, bind, pull)

    @pl.when(lead)
    def _():
        fill(y_out, bind, pull)

    @pl.when(side)
    def _():
        y_out[...] = jnp.zeros_like(y_out)
        x_out[...] = s_out[...]

    @pl.when(jnp.logical_and(lead, mine - hop < 0))
    def _():
        x_out[...] = jnp.zeros_like(x_out)

    @pl.when(takes)
    def _():
        copy.wait_recv()
        fill(x_out, *unpack(land))

    pl.when(sends)(copy.wait_send)


def exchange_kernel(
    hop, spread_hop, count, last,
    solved, x_ref, y_ref, s_ref, move_ref, bind_ref,
    x_out, y_out, s_out, move_out, bind_out,
    middle, through, spread_msg, bind_msg, move_land, pull_land, spread_land, bind_land,
    send_sems, recv_sems,
):
    ns = x_ref.shape[1]
    mine = lax.axis_index("tm")
    lead = lax.rem(mine, 2) == 0
    side = jnp.logical_not(lead)
    cases = [(lead, 1), (side, -1), (lead, spread_hop), (lead, -spread_hop)]
    if last:
        cases += [(side, hop), (side, -hop)]
    else:
        cases += [(True, hop), (True, -hop)]
    arrive = greet(mine, count, cases)

    def carry(source, land, send, recv, by):
        return pltpu.make_async_remote_copy(
            src_ref=source,
            dst_ref=land,
            send_sem=send_sems.at[send],
            recv_sem=recv_sems.at[recv],
            device_id=(lax.rem(mine + by + count, count),),
            device_id_type=pl.DeviceIdType.MESH,
        )

    def reaches(by):
        return jnp.logical_and(mine + by >= 0, mine + by < count)

    move_side = carry(move_ref, move_land, 0, 0, 1)
    pull_side = carry(bind_ref, pull_land, 1, 1, 1)
    spread_up = carry(spread_msg, spread_land, 2, 2, spread_hop)
    spread_side = carry(spread_msg, spread_land, 3, 2, 1)
    bind_down = carry(bind_msg, bind_land, 4, 3, -hop)
    move_sends = jnp.logical_and(jnp.logical_and(lead, reaches(hop)), mine >= hop)
    spread_sends = jnp.logical_and(lead, reaches(spread_hop))
    bind_sends = jnp.logical_and(side, reaches(-hop))
    spread_takes = jnp.logical_or(side, reaches(-spread_hop))
    if last:
        move_takes = side
    else:
        move_up = carry(move_ref, move_land, 5, 0, hop)
        pull_up = carry(bind_ref, pull_land, 6, 1, hop)
        move_takes = jnp.logical_or(side, mine >= 2 * hop)

    pl.when(lead)(arrive)
    if not last:

        @pl.when(move_sends)
        def _():
            move_up.start()
            pull_up.start()

    @pl.when(lead)
    def _():
        move_side.start()
        pull_side.start()
        fill(through, exact(move_ref[...], solved[:ns, :]), y_ref[ns:, :])

    def mix():
        fill(middle, y_ref[:ns, :], solved[ns:, :])
        middle[...] = medium(middle[...], solved[:ns, :])

    if last:
        pl.when(side)(mix)
    else:
        mix()

    @pl.when(lead)
    def _():
        later_spread(through, x_ref, move_ref[...], s_ref, s_out)
        pack(spread_msg, s_out[:ns, :], s_out[ns:, :])

    pl.when(spread_sends)(spread_up.start)
    pl.when(lead)(spread_side.start)

    @pl.when(move_takes)
    def _():
        move_side.wait_recv()

    @pl.when(jnp.logical_not(move_takes))
    def _():
        move_land[...] = jnp.zeros_like(move_land)
        pull_land[...] = jnp.zeros_like(pull_land)

    def rest():
        early = move_land[...]
        both = medium(middle[...], early)
        bind = medium(early.T, both[:ns, :])

        @pl.when(move_takes)
        def _():
            pull_side.wait_recv()

        bind_i, pull_i = unpack(pull_land)
        fill(y_out, bind + bind_i, both[ns:, :] + pull_i)
        pack(bind_msg, y_out[:ns, :], y_out[ns:, :])

    if last:
        pl.when(side)(rest)
    else:
        rest()
    pl.when(side)(arrive)
    pl.when(bind_sends)(bind_down.start)
    if not last:

        @pl.when(lead)
        def _():
            move_out[...] = exact(through[:ns, :], move_land[...])
            bind_out[...] = bind_msg[...]

    @pl.when(spread_takes)
    def _():
        spread_side.wait_recv()
        fill(x_out, *unpack(spread_land))

    @pl.when(jnp.logical_not(spread_takes))
    def _():
        x_out[...] = jnp.zeros_like(x_out)

    @pl.when(jnp.logical_and(side, reaches(hop)))
    def _():
        bind_down.wait_recv()
        fill(y_out, *unpack(bind_land))

    @pl.when(jnp.logical_and(side, jnp.logical_not(reaches(hop))))
    def _():
        y_out[...] = y_ref[...]

    if not last:

        @pl.when(move_sends)
        def _():
            move_up.wait_send()
            pull_up.wait_send()

    @pl.when(lead)
    def _():
        move_side.wait_send()
        pull_side.wait_send()

    pl.when(spread_sends)(spread_up.wait_send)
    pl.when(lead)(spread_side.wait_send)
    pl.when(bind_sends)(bind_down.wait_send)


def choose_kernel(place_ref, x_ref, y_ref, leaves, left, right):
    ns = x_ref.shape[1]
    tall = ns + 8
    core = lax.rem(place_ref[0], 2)
    odd, even = leaves.at[: 2 * tall + ns, :], leaves.at[2 * tall + ns : 4 * tall + 2 * ns, :]

    @pl.when(core == 0)
    def _():
        left[...] = x_ref[...]
        right[...] = even[ns + tall :, :]

    @pl.when(core != 0)
    def _():
        left[...] = odd[ns : ns + tall, :]
        right[...] = y_ref[...]


def finish_kernel(count, solved, x_ref, y_ref, leaves, s_out, y_out, middle, message, land, send_sem, recv_sem):
    ns = x_ref.shape[1]
    tall = ns + 8
    mine = lax.axis_index("tm")
    lead = lax.rem(mine, 2) == 0
    side = jnp.logical_not(lead)
    odd, even = leaves.at[: 2 * tall + ns, :], leaves.at[2 * tall + ns : 4 * tall + 2 * ns, :]
    arrive = greet(mine, count, [(lead, 1), (side, -1)])
    copy = pltpu.make_async_remote_copy(
        src_ref=message,
        dst_ref=land,
        send_sem=send_sem,
        recv_sem=recv_sem,
        device_id=(lax.rem(mine - 1 + count, count),),
        device_id_type=pl.DeviceIdType.MESH,
    )

    @pl.when(lead)
    def _():
        move = even[:ns, :]
        fill(middle, exact(move, solved[:ns, :]), even[2 * ns + tall :, :])
        later_spread(middle, x_ref, move, even.at[ns : ns + tall, :], s_out)

    @pl.when(side)
    def _():
        move = odd[:ns, :]
        fill(middle, y_ref[:ns, :], solved[ns:, :])
        both = medium(medium(middle[...], solved[:ns, :]), move)
        bind = medium(move.T, both[:ns, :]) + odd[ns + tall : 2 * ns + tall, :]
        pack(message, bind, both[ns:, :] + odd[2 * ns + tall :, :])
        s_out[...] = x_ref[...]
        y_out[...] = y_ref[...]

    arrive()

    @pl.when(side)
    def _():
        copy.start()
        copy.wait_send()

    @pl.when(lead)
    def _():
        copy.wait_recv()
        fill(y_out, *unpack(land))


def last_kernel(solved, own_ref, later_ref, mean_ref, cov_ref):
    ns = own_ref.shape[1]
    mixed = solved[:ns, :]
    whole = own_ref[:ns, :]
    cov_ref[...] = exact(mixed, whole)
    mean_ref[...] = exact(own_ref[ns:, :] + exact(later_ref[ns:, :], whole), mixed, NT)[:1, :]


KERNEL_VMEM = 16 * 2**20
ALL_VMEM = 67 * 10**6
VMEM = pl.BlockSpec(memory_space=pltpu.VMEM)
HBM = pl.BlockSpec(memory_space=pltpu.MemorySpace.HBM)
SMEM = pl.BlockSpec(memory_space=pltpu.SMEM)


def call(kernel, args, rows, scratch, work, name, far=(), room=KERNEL_VMEM, **params):
    width = args[-1].shape[-1]
    read = sum(a.size for a in args) * 4
    return pl.pallas_call(
        kernel,
        out_shape=tuple(jax.ShapeDtypeStruct((r, width), F32) for r in rows),
        in_specs=[
            HBM if i in far else SMEM if a.ndim == 1 else VMEM for i, a in enumerate(args)
        ],
        out_specs=tuple(VMEM for _ in rows),
        scratch_shapes=scratch,
        cost_estimate=pl.CostEstimate(flops=work, bytes_accessed=read, transcendentals=0),
        compiler_params=pltpu.CompilerParams(vmem_limit_bytes=room, **params),
        name=name,
    )(*args)


def shards(measurements, noise_levels, transition, sensing, process_noise, prior_mean, prior_covariance):
    ns = transition.shape[0]
    no = sensing.shape[0]
    count = lax.axis_size("tm")
    device = lax.axis_index("tm").astype(jnp.int32)
    place = device.reshape(1)
    half = ns // 2 + 8
    tall = ns + 8
    work = 2 * ns**3 * 60

    def rows(r, columns=ns):
        return pltpu.VMEM((r, columns), F32)

    pair = rows(3 * ns)
    mine = jnp.concatenate([measurements, noise_levels], axis=0)
    other = lax.ppermute(mine, "tm", [(i, i ^ 1) for i in range(count)])
    def resolved(x, y):
        return call(resolve_kernel, (x, y), (tall,), [pair], work, "resolve")[0]

    (leaves,) = call(
        start_kernel,
        (
            place,
            mine,
            other,
            transition,
            sensing,
            process_noise,
            prior_mean.reshape(1, ns),
            prior_covariance,
        ),
        (5 * tall + 2 * ns,),
        [
            rows(ns),
            rows(no),
            rows(ns),
            rows(ns),
            rows(8),
            rows(no),
            rows(no),
            rows(no, no),
            rows(3 * no, no),
            pair,
            pltpu.SemaphoreType.DMA((4,)),
        ],
        work,
        "start",
        far=(3, 4, 5, 7),
        room=ALL_VMEM,
    )
    x, y, s, moved, bound = call(
        functools.partial(pair_kernel, 2, count),
        (leaves,),
        (tall, tall, tall, ns, half),
        [rows(tall), rows(half), rows(half), pltpu.SemaphoreType.DMA, pltpu.SemaphoreType.DMA],
        work // 3,
        "pair",
        collective_id=1,
        has_side_effects=True,
    )
    hop = 2
    while hop < count:
        last = hop * 2 >= count
        small = (8, 8) if last else (ns, half)
        spread_hop = 2 if last else 2 * hop
        solved = resolved(x, y)
        x, y, s, moved, bound = call(
            functools.partial(exchange_kernel, hop, spread_hop, count, last),
            (solved, x, y, s, moved, bound),
            (tall, tall, tall) + small,
            [
                rows(tall),
                rows(tall),
                rows(half),
                rows(half),
                rows(ns),
                rows(half),
                rows(half),
                rows(half),
                pltpu.SemaphoreType.DMA((7,)),
                pltpu.SemaphoreType.DMA((4,)),
            ],
            work,
            f"exchange_{hop}",
            collective_id=hop.bit_length(),
            has_side_effects=True,
        )
        hop *= 2
    left, right = call(choose_kernel, (place, x, y, leaves), (tall, tall), [], work // 60, "choose")
    solved = resolved(left, right)
    own, later = call(
        functools.partial(finish_kernel, count),
        (solved, x, y, leaves),
        (tall, tall),
        [rows(tall), rows(half), rows(half), pltpu.SemaphoreType.DMA, pltpu.SemaphoreType.DMA],
        work,
        "finish",
        collective_id=0,
        has_side_effects=True,
    )
    mean, cov = call(last_kernel, (resolved(own, later), own, later), (1, ns), [], work // 20, "last")
    return (mean, cov[None])


def solution(mesh):
    return jax.shard_map(
        shards,
        mesh=mesh,
        in_specs=(P("tm", None), P("tm", None), P(), P(), P(), P(), P()),
        out_specs=(P("tm", None), P("tm", None, None)),
        check_vma=False,
    )
```

```python
import functools

import jax
import jax.numpy as jnp
from jax import lax
from jax.experimental import pallas as pl
from jax.experimental.pallas import tpu as pltpu
from jax.sharding import PartitionSpec as P

F32 = jnp.float32
BF16 = jnp.bfloat16
NN = (((1,), (0,)), ((), ()))
NT = (((1,), (1,)), ((), ()))


def exact(left, right, dims=NN):
    return lax.dot_general(
        left, right, dims, precision=lax.Precision.HIGHEST, preferred_element_type=F32
    )


def rough(left, right, dims=NN):
    return lax.dot_general(
        left.astype(BF16), right.astype(BF16), dims, preferred_element_type=F32
    )


def unit(size):
    rows = lax.broadcasted_iota(jnp.int32, (size, size), 0)
    columns = lax.broadcasted_iota(jnp.int32, (size, size), 1)
    return (rows == columns).astype(F32)


def medium(left, right, dims=NN):
    left_high, right_high = left.astype(BF16), right.astype(BF16)
    left_low = (left - left_high.astype(F32)).astype(BF16)
    right_low = (right - right_high.astype(F32)).astype(BF16)

    def times(a, b):
        return lax.dot_general(a, b, dims, preferred_element_type=F32)

    return times(left_high, right_high) + (
        times(left_high, right_low) + times(left_low, right_high)
    )


def inverse(product, bound, pair):
    size = product.shape[0]
    eye = unit(size)
    whole = eye + product
    small = bound < 128.0

    def gain_of(low):
        return 4.0 / ((1.0 + low) * (1.0 + low))

    def more(state):
        return jnp.logical_not(state[1])

    @pl.when(small)
    def _():
        low = 1.0 / bound
        scaled = whole * low
        step = gain_of(low) * ((1.0 + low) * eye - scaled)
        pair[:size, :] = step * low
        pair[size : 2 * size, :] = rough(scaled, step)

        def turn(state):
            low, _ = state
            ends = low >= 0.95
            low = jnp.where(ends, 1.0, low)
            step = gain_of(low) * ((1.0 + low) * eye - pair[size : 2 * size, :])
            pair[: 2 * size, :] = rough(pair[: 2 * size, :], step)
            return low * gain_of(low), ends

        lax.while_loop(more, turn, (low * gain_of(low), jnp.bool_(False)))

    @pl.when(jnp.logical_not(small))
    def _():
        low = 1.0 / bound
        pair[:size, :] = eye * low
        pair[size : 2 * size, :] = whole * low

        def turn(state):
            low, _ = state
            ends = low >= 0.999
            low = jnp.where(ends, 1.0, low)
            pair[2 * size :, :] = gain_of(low) * (
                (1.0 + low) * eye - pair[size : 2 * size, :]
            )

            def block(i, carry):
                at = pl.ds(pl.multiple_of(i * 32, 32), 32)
                pair[at, :] = exact(pair[at, :], pair[2 * size :, :])
                return carry

            lax.fori_loop(0, 2 * size // 32, block, 0)
            return low * gain_of(low), ends

        lax.while_loop(more, turn, (low, jnp.bool_(False)))

    def correct(i, carry):
        guess = pair[:size, :]
        pair[:size, :] = guess + rough(guess, eye - medium(whole, guess))
        return carry

    lax.fori_loop(0, 2, correct, 0)
    return pair[:size, :]


def spectral_bound(product, mirrored):
    return 1.0 + 1.02 * jnp.sqrt(jnp.maximum(jnp.sum(product * mirrored), 0.0))


def pack(out, value, vector):
    ns = value.shape[0]
    n = ns // 2
    rows = lax.broadcasted_iota(jnp.int32, (n, n), 0)
    columns = lax.broadcasted_iota(jnp.int32, (n, n), 1)
    low, high = value[:n, :n], value[n:, n:]
    out[:n, :n] = value[n:, :n]
    out[:n, n:] = jnp.where(rows >= columns, low, high)
    out[n : n + 8, :] = jnp.zeros((8, ns), F32)
    out[n : n + 1, :] = vector[:1, :]
    out[n + 1 : n + 2, :n] = jnp.sum(
        jnp.where(rows == columns, high, 0.0), axis=0, keepdims=True
    )


def unpack(ref):
    ns = ref.shape[1]
    n = ns // 2
    rows = lax.broadcasted_iota(jnp.int32, (n, n), 0)
    columns = lax.broadcasted_iota(jnp.int32, (n, n), 1)
    corner = ref[:n, :n]
    mixed = ref[:n, n:]
    turned = mixed.T
    diagonal = jnp.broadcast_to(ref[n + 1 : n + 2, :n], (n, n))
    low = jnp.where(rows >= columns, mixed, turned)
    high = jnp.where(rows < columns, mixed, jnp.where(rows == columns, diagonal, turned))
    value = jnp.concatenate(
        [
            jnp.concatenate([low, corner.T], axis=1),
            jnp.concatenate([corner, high], axis=1),
        ],
        axis=0,
    )
    return value, spread_rows(ref, n)


def spread_rows(ref, at):
    return jnp.broadcast_to(ref[at : at + 1, :], (8, ref.shape[1]))


def fill(ref, value, vector):
    ns = value.shape[1]
    ref[:ns, :] = value
    ref[ns:, :] = vector


def resolve(x_ref, y_ref, out, pair):
    ns = x_ref.shape[1]
    value = y_ref[:ns, :]
    both = medium(x_ref[...], value)
    product = both[:ns, :]
    bound = spectral_bound(product, rough(value, x_ref[:ns, :]))
    out[:ns, :] = inverse(product, bound, pair)
    out[ns:, :] = y_ref[ns:, :] - both[ns:, :]


def later_spread(through, x_ref, move, s_ref, out):
    ns = x_ref.shape[1]
    carried = medium(through[...], x_ref[:ns, :])
    offset = exact(x_ref[ns:, :] + carried[ns:, :], through[:ns, :], NT)
    fill(out, medium(carried[:ns, :], move, NT) + s_ref[:ns, :], offset + s_ref[ns:, :])


def start_kernel(
    place_ref, mine_ref, other_ref, f_hbm, h_hbm, q_hbm, m_ref, p_hbm,
    leaves,
    f_ref, h_ref, noise, p_ref, center, plain, sensed_plain, inner_plain, half_pair, pair, sems,
):
    chip, core = lax.div(place_ref[0], 2), lax.rem(place_ref[0], 2)
    lead = core == 0
    no, ns = h_ref.shape
    tall = ns + 8
    size = 2 * tall + ns
    copies = [
        pltpu.make_async_copy(source, target, sems.at[i])
        for i, (source, target) in enumerate(((h_hbm, h_ref), (f_hbm, f_ref), (q_hbm, noise)))
    ]
    for copy in copies:
        copy.start()
    prior_copy = pltpu.make_async_copy(p_hbm, p_ref, sems.at[3])
    pl.when(chip == 0)(prior_copy.start)
    center[...] = jnp.zeros_like(center)
    eye = unit(no)
    copies[0].wait()
    copies[1].wait()
    sensed_plain[...] = exact(h_ref[...], f_ref[...])
    copies[2].wait()

    def leaf(i, carry):
        first = jnp.logical_and(i == 1, chip == 0)
        own = (i == 1) == lead
        at = pl.multiple_of(i * size, 8)

        @pl.when(first)
        def _():
            prior_copy.wait()
            noise[...] += exact(exact(f_ref[...], p_ref[...]), f_ref[...], NT)
            center[...] = exact(jnp.broadcast_to(m_ref[...], center.shape), f_ref[...], NT)

        @pl.when(jnp.logical_or(i == 0, first))
        def _():
            plain[...] = exact(h_ref[...], noise[...])
            inner_plain[...] = exact(plain[...], h_ref[...], NT)

        weight = lax.rsqrt(jnp.where(own, mine_ref[1:2, :], other_ref[1:2, :]))
        y = jnp.where(own, mine_ref[:1, :], other_ref[:1, :]) * weight
        y = jnp.broadcast_to(y, (8, no))
        weights = jnp.sum(eye * weight, axis=1, keepdims=True)
        gain = plain[...] * weights
        sensed = sensed_plain[...] * weights
        inner = inner_plain[...] * weights * weight
        active = jnp.where(first, 0.0, 1.0)
        mixed = inverse(inner, spectral_bound(inner, inner), half_pair)
        gained = medium(mixed, gain)
        joined = exact(mixed, sensed)
        gain_t = gain.T
        error = y - exact(center[...], h_ref[...], NT) * weight
        leaves[pl.ds(at, ns), :] = active * (f_ref[...] - exact(gain_t, joined))
        leaves[pl.ds(at + ns, ns), :] = noise[...] - medium(gain_t, gained)
        leaves[pl.ds(at + 2 * ns, 8), :] = center[...] + exact(error, gained)
        leaves[pl.ds(at + ns + tall, ns), :] = active * medium(sensed.T, joined)
        leaves[pl.ds(at + 2 * ns + tall, 8), :] = active * exact(y, joined)
        return carry

    lax.fori_loop(0, 2, leaf, 0)
    resolve(
        leaves.at[size + ns : size + ns + tall, :],
        leaves.at[ns + tall : size, :],
        leaves.at[2 * size :, :],
        pair,
    )


def resolve_kernel(x_ref, y_ref, out, pair):
    resolve(x_ref, y_ref, out, pair)


def greet(mine, count, cases):
    barrier = pltpu.get_barrier_semaphore()
    expected = jnp.int32(0)
    for wanted, hop in cases:
        inside = jnp.logical_and(mine + hop >= 0, mine + hop < count)
        inside = jnp.logical_and(inside, wanted)
        expected = expected + inside.astype(jnp.int32)

        @pl.when(inside)
        def _(hop=hop):
            pl.semaphore_signal(
                barrier, inc=1, device_id=(mine + hop,), device_id_type=pl.DeviceIdType.MESH
            )


    def arrive():
        @pl.when(expected > 0)
        def _():
            pl.semaphore_wait(barrier, expected)

    return arrive


def pair_kernel(
    hop, count,
    leaves, x_out, y_out, s_out, move_out, bind_out,
    through, message, land, send_sem, recv_sem,
):
    ns = leaves.shape[1]
    tall = ns + 8
    size = 2 * tall + ns
    mine = lax.axis_index("tm")
    lead = lax.rem(mine, 2) == 0
    side = jnp.logical_not(lead)
    arrive = greet(mine, count, [(lead, hop), (lead, -hop)])
    copy = pltpu.make_async_remote_copy(
        src_ref=message,
        dst_ref=land,
        send_sem=send_sem,
        recv_sem=recv_sem,
        device_id=(lax.rem(mine + hop, count),),
        device_id_type=pl.DeviceIdType.MESH,
    )
    sends = jnp.logical_and(lead, mine + hop < count)
    takes = jnp.logical_and(lead, mine - hop >= 0)
    odd, even = leaves.at[:size, :], leaves.at[size : 2 * size, :]
    solved = leaves.at[2 * size :, :]
    x_ref = even.at[ns : ns + tall, :]
    y_ref = odd.at[ns + tall :, :]
    later = odd[:ns, :]
    early = even[:ns, :]
    fill(through, exact(later, solved[:ns, :]), y_ref[ns:, :])
    later_spread(through, x_ref, later, odd.at[ns : ns + tall, :], s_out)
    pack(message, s_out[:ns, :], s_out[ns:, :])
    arrive()
    pl.when(sends)(copy.start)
    move_out[...] = exact(through[:ns, :], early)
    fill(through, y_ref[:ns, :], solved[ns:, :])
    both = medium(medium(through[...], solved[:ns, :]), early)
    bind = medium(early.T, both[:ns, :]) + even[ns + tall : ns + tall + ns, :]
    pull = both[ns:, :] + even[2 * ns + tall :, :]
    pack(bind_out, bind, pull)

    @pl.when(lead)
    def _():
        fill(y_out, bind, pull)

    @pl.when(side)
    def _():
        y_out[...] = jnp.zeros_like(y_out)
        x_out[...] = s_out[...]

    @pl.when(jnp.logical_and(lead, mine - hop < 0))
    def _():
        x_out[...] = jnp.zeros_like(x_out)

    @pl.when(takes)
    def _():
        copy.wait_recv()
        fill(x_out, *unpack(land))

    pl.when(sends)(copy.wait_send)


def exchange_kernel(
    hop, spread_hop, count, last,
    solved, x_ref, y_ref, s_ref, move_ref, bind_ref,
    x_out, y_out, s_out, move_out, bind_out,
    middle, through, spread_msg, bind_msg, move_land, pull_land, spread_land, bind_land,
    send_sems, recv_sems,
):
    ns = x_ref.shape[1]
    mine = lax.axis_index("tm")
    lead = lax.rem(mine, 2) == 0
    side = jnp.logical_not(lead)
    cases = [(lead, 1), (side, -1), (lead, spread_hop), (lead, -spread_hop)]
    if last:
        cases += [(side, hop), (side, -hop)]
    else:
        cases += [(True, hop), (True, -hop)]
    arrive = greet(mine, count, cases)

    def carry(source, land, send, recv, by):
        return pltpu.make_async_remote_copy(
            src_ref=source,
            dst_ref=land,
            send_sem=send_sems.at[send],
            recv_sem=recv_sems.at[recv],
            device_id=(lax.rem(mine + by + count, count),),
            device_id_type=pl.DeviceIdType.MESH,
        )

    def reaches(by):
        return jnp.logical_and(mine + by >= 0, mine + by < count)

    move_side = carry(move_ref, move_land, 0, 0, 1)
    pull_side = carry(bind_ref, pull_land, 1, 1, 1)
    spread_up = carry(spread_msg, spread_land, 2, 2, spread_hop)
    spread_side = carry(spread_msg, spread_land, 3, 2, 1)
    bind_down = carry(bind_msg, bind_land, 4, 3, -hop)
    move_sends = jnp.logical_and(jnp.logical_and(lead, reaches(hop)), mine >= hop)
    spread_sends = jnp.logical_and(lead, reaches(spread_hop))
    bind_sends = jnp.logical_and(side, reaches(-hop))
    spread_takes = jnp.logical_or(side, reaches(-spread_hop))
    if last:
        move_takes = side
    else:
        move_up = carry(move_ref, move_land, 5, 0, hop)
        pull_up = carry(bind_ref, pull_land, 6, 1, hop)
        move_takes = jnp.logical_or(side, mine >= 2 * hop)

    pl.when(lead)(arrive)
    if not last:

        @pl.when(move_sends)
        def _():
            move_up.start()
            pull_up.start()

    @pl.when(lead)
    def _():
        move_side.start()
        pull_side.start()
        fill(through, exact(move_ref[...], solved[:ns, :]), y_ref[ns:, :])

    def mix():
        fill(middle, y_ref[:ns, :], solved[ns:, :])
        middle[...] = medium(middle[...], solved[:ns, :])

    if last:
        pl.when(side)(mix)
    else:
        mix()

    @pl.when(lead)
    def _():
        later_spread(through, x_ref, move_ref[...], s_ref, s_out)
        pack(spread_msg, s_out[:ns, :], s_out[ns:, :])

    pl.when(spread_sends)(spread_up.start)
    pl.when(lead)(spread_side.start)

    @pl.when(move_takes)
    def _():
        move_side.wait_recv()

    @pl.when(jnp.logical_not(move_takes))
    def _():
        move_land[...] = jnp.zeros_like(move_land)
        pull_land[...] = jnp.zeros_like(pull_land)

    def rest():
        early = move_land[...]
        both = medium(middle[...], early)
        bind = medium(early.T, both[:ns, :])

        @pl.when(move_takes)
        def _():
            pull_side.wait_recv()

        bind_i, pull_i = unpack(pull_land)
        fill(y_out, bind + bind_i, both[ns:, :] + pull_i)
        pack(bind_msg, y_out[:ns, :], y_out[ns:, :])

    if last:
        pl.when(side)(rest)
    else:
        rest()
    pl.when(side)(arrive)
    pl.when(bind_sends)(bind_down.start)
    if not last:

        @pl.when(lead)
        def _():
            move_out[...] = exact(through[:ns, :], move_land[...])
            bind_out[...] = bind_msg[...]

    @pl.when(spread_takes)
    def _():
        spread_side.wait_recv()
        fill(x_out, *unpack(spread_land))

    @pl.when(jnp.logical_not(spread_takes))
    def _():
        x_out[...] = jnp.zeros_like(x_out)

    @pl.when(jnp.logical_and(side, reaches(hop)))
    def _():
        bind_down.wait_recv()
        fill(y_out, *unpack(bind_land))

    @pl.when(jnp.logical_and(side, jnp.logical_not(reaches(hop))))
    def _():
        y_out[...] = y_ref[...]

    if not last:

        @pl.when(move_sends)
        def _():
            move_up.wait_send()
            pull_up.wait_send()

    @pl.when(lead)
    def _():
        move_side.wait_send()
        pull_side.wait_send()

    pl.when(spread_sends)(spread_up.wait_send)
    pl.when(lead)(spread_side.wait_send)
    pl.when(bind_sends)(bind_down.wait_send)


def choose_kernel(place_ref, x_ref, y_ref, leaves, left, right):
    ns = x_ref.shape[1]
    tall = ns + 8
    core = lax.rem(place_ref[0], 2)
    odd, even = leaves.at[: 2 * tall + ns, :], leaves.at[2 * tall + ns : 4 * tall + 2 * ns, :]

    @pl.when(core == 0)
    def _():
        left[...] = x_ref[...]
        right[...] = even[ns + tall :, :]

    @pl.when(core != 0)
    def _():
        left[...] = odd[ns : ns + tall, :]
        right[...] = y_ref[...]


def finish_kernel(count, solved, x_ref, y_ref, leaves, s_out, y_out, middle, message, land, send_sem, recv_sem):
    ns = x_ref.shape[1]
    tall = ns + 8
    mine = lax.axis_index("tm")
    lead = lax.rem(mine, 2) == 0
    side = jnp.logical_not(lead)
    odd, even = leaves.at[: 2 * tall + ns, :], leaves.at[2 * tall + ns : 4 * tall + 2 * ns, :]
    arrive = greet(mine, count, [(lead, 1), (side, -1)])
    copy = pltpu.make_async_remote_copy(
        src_ref=message,
        dst_ref=land,
        send_sem=send_sem,
        recv_sem=recv_sem,
        device_id=(lax.rem(mine - 1 + count, count),),
        device_id_type=pl.DeviceIdType.MESH,
    )

    @pl.when(lead)
    def _():
        move = even[:ns, :]
        fill(middle, exact(move, solved[:ns, :]), even[2 * ns + tall :, :])
        later_spread(middle, x_ref, move, even.at[ns : ns + tall, :], s_out)

    @pl.when(side)
    def _():
        move = odd[:ns, :]
        fill(middle, y_ref[:ns, :], solved[ns:, :])
        both = medium(medium(middle[...], solved[:ns, :]), move)
        bind = medium(move.T, both[:ns, :]) + odd[ns + tall : 2 * ns + tall, :]
        pack(message, bind, both[ns:, :] + odd[2 * ns + tall :, :])
        s_out[...] = x_ref[...]
        y_out[...] = y_ref[...]

    arrive()

    @pl.when(side)
    def _():
        copy.start()
        copy.wait_send()

    @pl.when(lead)
    def _():
        copy.wait_recv()
        fill(y_out, *unpack(land))


def last_kernel(solved, own_ref, later_ref, mean_ref, cov_ref):
    ns = own_ref.shape[1]
    mixed = solved[:ns, :]
    whole = own_ref[:ns, :]
    cov_ref[...] = exact(mixed, whole)
    mean_ref[...] = exact(own_ref[ns:, :] + exact(later_ref[ns:, :], whole), mixed, NT)[:1, :]


KERNEL_VMEM = 16 * 2**20
ALL_VMEM = 67 * 10**6
VMEM = pl.BlockSpec(memory_space=pltpu.VMEM)
HBM = pl.BlockSpec(memory_space=pltpu.MemorySpace.HBM)
SMEM = pl.BlockSpec(memory_space=pltpu.SMEM)


def call(kernel, args, rows, scratch, work, name, far=(), room=KERNEL_VMEM, **params):
    width = args[-1].shape[-1]
    read = sum(a.size for a in args) * 4
    return pl.pallas_call(
        kernel,
        out_shape=tuple(jax.ShapeDtypeStruct((r, width), F32) for r in rows),
        in_specs=[
            HBM if i in far else SMEM if a.ndim == 1 else VMEM for i, a in enumerate(args)
        ],
        out_specs=tuple(VMEM for _ in rows),
        scratch_shapes=scratch,
        cost_estimate=pl.CostEstimate(flops=work, bytes_accessed=read, transcendentals=0),
        compiler_params=pltpu.CompilerParams(vmem_limit_bytes=room, **params),
        name=name,
    )(*args)


def shards(measurements, noise_levels, transition, sensing, process_noise, prior_mean, prior_covariance):
    ns = transition.shape[0]
    no = sensing.shape[0]
    count = lax.axis_size("tm")
    device = lax.axis_index("tm").astype(jnp.int32)
    place = device.reshape(1)
    half = ns // 2 + 8
    tall = ns + 8
    work = 2 * ns**3 * 60

    def rows(r, columns=ns):
        return pltpu.VMEM((r, columns), F32)

    pair = rows(3 * ns)
    mine = jnp.concatenate([measurements, noise_levels], axis=0)
    other = lax.ppermute(mine, "tm", [(i, i ^ 1) for i in range(count)])
    def resolved(x, y):
        return call(resolve_kernel, (x, y), (tall,), [pair], work, "resolve")[0]

    (leaves,) = call(
        start_kernel,
        (
            place,
            mine,
            other,
            transition,
            sensing,
            process_noise,
            prior_mean.reshape(1, ns),
            prior_covariance,
        ),
        (5 * tall + 2 * ns,),
        [
            rows(ns),
            rows(no),
            rows(ns),
            rows(ns),
            rows(8),
            rows(no),
            rows(no),
            rows(no, no),
            rows(3 * no, no),
            pair,
            pltpu.SemaphoreType.DMA((4,)),
        ],
        work,
        "start",
        far=(3, 4, 5, 7),
        room=ALL_VMEM,
    )
    x, y, s, moved, bound = call(
        functools.partial(pair_kernel, 2, count),
        (leaves,),
        (tall, tall, tall, ns, half),
        [rows(tall), rows(half), rows(half), pltpu.SemaphoreType.DMA, pltpu.SemaphoreType.DMA],
        work // 3,
        "pair",
        collective_id=1,
        has_side_effects=True,
    )
    hop = 2
    while hop < count:
        last = hop * 2 >= count
        small = (8, 8) if last else (ns, half)
        spread_hop = 2 if last else 2 * hop
        solved = resolved(x, y)
        x, y, s, moved, bound = call(
            functools.partial(exchange_kernel, hop, spread_hop, count, last),
            (solved, x, y, s, moved, bound),
            (tall, tall, tall) + small,
            [
                rows(tall),
                rows(tall),
                rows(half),
                rows(half),
                rows(ns),
                rows(half),
                rows(half),
                rows(half),
                pltpu.SemaphoreType.DMA((7,)),
                pltpu.SemaphoreType.DMA((4,)),
            ],
            work,
            f"exchange_{hop}",
            collective_id=hop.bit_length(),
            has_side_effects=True,
        )
        hop *= 2
    left, right = call(choose_kernel, (place, x, y, leaves), (tall, tall), [], work // 60, "choose")
    solved = resolved(left, right)
    own, later = call(
        functools.partial(finish_kernel, count),
        (solved, x, y, leaves),
        (tall, tall),
        [rows(tall), rows(half), rows(half), pltpu.SemaphoreType.DMA, pltpu.SemaphoreType.DMA],
        work,
        "finish",
        collective_id=0,
        has_side_effects=True,
    )
    mean, cov = call(last_kernel, (resolved(own, later), own, later), (1, ns), [], work // 20, "last")
    return (mean, cov[None])


def solution(mesh):
    return jax.shard_map(
        shards,
        mesh=mesh,
        in_specs=(P("tm", None), P("tm", None), P(), P(), P(), P(), P()),
        out_specs=(P("tm", None), P("tm", None, None)),
        check_vma=False,
    )
```
